32 devices in a mesh: dp: 8 (over y, x, core), seq: 4 (over z).
Axes of the slice: x: 2, y: 2, z: 4, core: 2. Of those that a mesh axis runs over, the one named last changes fastest.
Arguments:
- tokens: bfloat16 [8, 1024, 1024], P('dp', 'seq'), may hold values from -6 to 6
- encoded: bfloat16 [8, 512, 1024], P('dp', 'seq'), may hold values from -6 to 6
- cotangent: bfloat16 [8, 1024, 1024], P('dp', 'seq'), may hold values from -6 to 6
- doc_ids: int32 [8, 1024], P('dp'), may hold values from 0 to 2, as said below
- block_ids: int32 [8, 1024], P('dp'), may hold values from 0 to 7, never falling along the last dimension, each value on 1 to 256 neighbouring positions
- query_weight: float32 [1024, 1024], P(('dp', 'seq')), may hold values from -0.1875 to 0.1875
- key_weight: float32 [1024, 1024], P(('dp', 'seq')), may hold values from -0.1875 to 0.1875
- value_weight: float32 [1024, 1024], P(('dp', 'seq')), may hold values from -0.1875 to 0.1875
- out_weight: float32 [1024, 1024], P(('dp', 'seq')), may hold values from -0.75 to 0.75
- query_bias: float32 [1024], P(('dp', 'seq')), may hold values from -3 to 3
- value_bias: float32 [1024], P(('dp', 'seq')), may hold values from -3 to 3
- out_bias: float32 [1024], P(('dp', 'seq')), may hold values from -3 to 3
- first_gain: float32 [1024], P(('dp', 'seq')), may hold values from 0.1 to 1.9
- first_shift: float32 [1024], P(('dp', 'seq')), may hold values from -3 to 3
- probe_weight: float32 [1024, 1024], P(('dp', 'seq')), may hold values from -0.1875 to 0.1875
- lookup_weight: float32 [1024, 1024], P(('dp', 'seq')), may hold values from -0.1875 to 0.1875
- content_weight: float32 [1024, 1024], P(('dp', 'seq')), may hold values from -0.1875 to 0.1875
- merge_weight: float32 [1024, 1024], P(('dp', 'seq')), may hold values from -0.75 to 0.75
- probe_bias: float32 [1024], P(('dp', 'seq')), may hold values from -3 to 3
- content_bias: float32 [1024], P(('dp', 'seq')), may hold values from -3 to 3
- merge_bias: float32 [1024], P(('dp', 'seq')), may hold values from -3 to 3
- second_gain: float32 [1024], P(('dp', 'seq')), may hold values from 0.1 to 1.9
- second_shift: float32 [1024], P(('dp', 'seq')), may hold values from -3 to 3
- expand_weight: float32 [1024, 4096], P(('dp', 'seq')), may hold values from -0.1875 to 0.1875
- expand_bias: float32 [4096], P(('dp', 'seq')), may hold values from -3 to 3
- reduce_weight: float32 [4096, 1024], P(('dp', 'seq')), may hold values from -0.09375 to 0.09375
- reduce_bias: float32 [1024], P(('dp', 'seq')), may hold values from -3 to 3
- third_gain: float32 [1024], P(('dp', 'seq')), may hold values from 0.1 to 1.9
- third_shift: float32 [1024], P(('dp', 'seq')), may hold values from -3 to 3
Outputs:
- output: bfloat16 [8, 1024, 1024], P('dp', 'seq')
- tokens_grad: float32 [8, 1024, 1024], P('dp', 'seq')
- encoded_grad: float32 [8, 512, 1024], P('dp', 'seq')
- query_weight_grad: float32 [1024, 1024], P(('dp', 'seq'))
- key_weight_grad: float32 [1024, 1024], P(('dp', 'seq'))
- value_weight_grad: float32 [1024, 1024], P(('dp', 'seq'))
- out_weight_grad: float32 [1024, 1024], P(('dp', 'seq'))
- query_bias_grad: float32 [1024], P(('dp', 'seq'))
- value_bias_grad: float32 [1024], P(('dp', 'seq'))
- out_bias_grad: float32 [1024], P(('dp', 'seq'))
- first_gain_grad: float32 [1024], P(('dp', 'seq'))
- first_shift_grad: float32 [1024], P(('dp', 'seq'))
- probe_weight_grad: float32 [1024, 1024], P(('dp', 'seq'))
- lookup_weight_grad: float32 [1024, 1024], P(('dp', 'seq'))
- content_weight_grad: float32 [1024, 1024], P(('dp', 'seq'))
- merge_weight_grad: float32 [1024, 1024], P(('dp', 'seq'))
- probe_bias_grad: float32 [1024], P(('dp', 'seq'))
- content_bias_grad: float32 [1024], P(('dp', 'seq'))
- merge_bias_grad: float32 [1024], P(('dp', 'seq'))
- second_gain_grad: float32 [1024], P(('dp', 'seq'))
- second_shift_grad: float32 [1024], P(('dp', 'seq'))
- expand_weight_grad: float32 [1024, 4096], P(('dp', 'seq'))
- expand_bias_grad: float32 [4096], P(('dp', 'seq'))
- reduce_weight_grad: float32 [4096, 1024], P(('dp', 'seq'))
- reduce_bias_grad: float32 [1024], P(('dp', 'seq'))
- third_gain_grad: float32 [1024], P(('dp', 'seq'))
- third_shift_grad: float32 [1024], P(('dp', 'seq'))
The draws below stay inside these ranges and needn't reach their ends.
Inputs may be any that keep to these rules, and one draw needn't show every extreme that they name: `doc_ids`: along a row the ids never fall; id 1 begins within the first 256 positions and id 2 within the last 256 positions. `block_ids`: along a row the ids never fall and each block holds 1 to 256 tokens.
All inputs are finite; a program needn't handle non-finite values.
Results may differ from the reference program's by a relative error of at most 0.035.
Values may be sent and summed in bfloat16 or wider, within the bound.
A program may use at most 256 MiB of HBM per device.

```python
import math
import jax
import jax.numpy as jnp
import numpy as np
from jax import lax

D = 1024
H = 16
DH = 64
FF = 4096
BLOCK = 256
TOK_SEQ = 256
SEQ_LEN = 1024
ENC_LEN = 512
BATCH = 8
NBLK = 8


def draw_doc_ids(key, part):
    first_key = jax.random.fold_in(key, 11)
    second_key = jax.random.fold_in(key, 12)
    first_cut = jax.random.randint(first_key, (BATCH, 1), 1, TOK_SEQ)
    second_cut = jax.random.randint(second_key, (BATCH, 1), SEQ_LEN - TOK_SEQ + 1, SEQ_LEN)
    places = jnp.arange(SEQ_LEN, dtype=jnp.int32)[None, :]
    return (places >= first_cut).astype(jnp.int32) + (places >= second_cut).astype(jnp.int32)


def levels(rng, extent, cuts, least, top_value):
    level = 1.0
    for position, shards_of in cuts:
        draws = jax.random.uniform(jax.random.fold_in(jax.random.fold_in(rng, 6), position), (shards_of,), jnp.float32, least / len(cuts), top_value / len(cuts))
        level = level * jnp.repeat(jnp.exp(draws), extent[position] // shards_of).reshape((-1,) + (1,) * (len(extent) - 1 - position))
    return level


def length_profile(amount, total, bound, lean):
    loads = [(1 << 20) // math.isqrt(grade ** lean) + 1 for grade in range(2, amount + 1)]
    rest, holding = total - bound - (amount - 1), [1] * (amount - 1)
    while rest > 0:
        candidates = [i for i in range(amount - 1) if holding[i] < bound]
        whole, remaining = sum([loads[i] for i in candidates]), rest
        for i in candidates:
            extra = min(bound - holding[i], max(1, remaining * loads[i] // whole), rest)
            holding[i] = holding[i] + extra
            rest = rest - extra
    return np.array([bound] + holding)


def uneven(key, amount, total, reach, slope):
    if amount == 2:
        one = jax.random.randint(key, (), max(1, total - reach), min(reach, total - 1) + 1)
        return jnp.stack([one, total - one])
    sizes = jnp.asarray(length_profile(amount, total, reach, slope), jnp.int32)
    couples = (amount - 1) // 2
    giver, sink = sizes[1:1 + 2 * couples:2], sizes[2:2 + 2 * couples:2]
    room = jnp.minimum(giver - 1, reach - sink)
    moved = jax.random.randint(jax.random.fold_in(key, 1), (couples,), 0, 1 << 20) % (room + 1)
    sizes = sizes.at[1:1 + 2 * couples:2].set(giver - moved).at[2:2 + 2 * couples:2].set(sink + moved)
    return sizes[jax.random.permutation(jax.random.fold_in(key, 2), amount)]


def normal_values(stream_key, shape, spread, bound, split=(), held_as=jnp.bfloat16):
    entries = spread * jax.random.normal(stream_key, shape, jnp.float32)
    if split:
        entries = entries * levels(stream_key, shape, split, -0.22, 0.18)
    return jnp.clip(entries, -bound, bound).astype(held_as)


def setup_inputs(seed: int = 0) -> dict:
    streams_of = jax.random.split(jax.random.key(seed), 30)
    tokens = normal_values(streams_of[0], (BATCH, SEQ_LEN, D), 1.0, 6.0, ((0, 8), (1, 4)))
    encoded = normal_values(streams_of[1], (BATCH, ENC_LEN, D), 1.0, 6.0, ((0, 8), (1, 4)))
    cotangent = normal_values(streams_of[2], (BATCH, SEQ_LEN, D), 1.0, 6.0, ((0, 8), (1, 4)))
    doc_ids = draw_doc_ids(jax.random.fold_in(streams_of[29], 71), 0)
    block_ids = jax.vmap(lambda own: jnp.searchsorted(jnp.cumsum(uneven(own, NBLK, SEQ_LEN, BLOCK, 0)), jnp.arange(SEQ_LEN), side="right"))(jax.random.split(streams_of[4], BATCH)).reshape((BATCH, SEQ_LEN)).astype(jnp.int32)
    query_weight = normal_values(streams_of[5], (D, D), D ** -0.5, 0.1875, ((0, 32),), jnp.float32)
    key_weight = normal_values(streams_of[6], (D, D), D ** -0.5, 0.1875, ((0, 32),), jnp.float32)
    value_weight = normal_values(streams_of[7], (D, D), D ** -0.5, 0.1875, ((0, 32),), jnp.float32)
    out_weight = normal_values(streams_of[8], (D, D), (D // 16) ** -0.5, 0.75, ((0, 32),), jnp.float32)
    query_bias = normal_values(streams_of[9], (D,), 0.5, 3.0, ((0, 32),), jnp.float32)
    value_bias = normal_values(streams_of[10], (D,), 0.5, 3.0, ((0, 32),), jnp.float32)
    out_bias = normal_values(streams_of[11], (D,), 0.5, 3.0, ((0, 32),), jnp.float32)
    first_gain = jnp.clip(1.0 + 0.18 * jax.random.normal(streams_of[12], (D,), jnp.float32), 0.1, 1.9)
    first_shift = normal_values(streams_of[13], (D,), 0.5, 3.0, ((0, 32),), jnp.float32)
    probe_weight = normal_values(streams_of[14], (D, D), D ** -0.5, 0.1875, ((0, 32),), jnp.float32)
    lookup_weight = normal_values(streams_of[15], (D, D), D ** -0.5, 0.1875, ((0, 32),), jnp.float32)
    content_weight = normal_values(streams_of[16], (D, D), D ** -0.5, 0.1875, ((0, 32),), jnp.float32)
    merge_weight = normal_values(streams_of[17], (D, D), (D // 16) ** -0.5, 0.75, ((0, 32),), jnp.float32)
    probe_bias = normal_values(streams_of[18], (D,), 0.5, 3.0, ((0, 32),), jnp.float32)
    content_bias = normal_values(streams_of[19], (D,), 0.5, 3.0, ((0, 32),), jnp.float32)
    merge_bias = normal_values(streams_of[20], (D,), 0.5, 3.0, ((0, 32),), jnp.float32)
    second_gain = jnp.clip(1.0 + 0.18 * jax.random.normal(streams_of[21], (D,), jnp.float32), 0.1, 1.9)
    second_shift = normal_values(streams_of[22], (D,), 0.5, 3.0, ((0, 32),), jnp.float32)
    expand_weight = normal_values(streams_of[23], (D, FF), D ** -0.5, 0.1875, ((0, 32),), jnp.float32)
    expand_bias = normal_values(streams_of[24], (FF,), 0.5, 3.0, ((0, 32),), jnp.float32)
    reduce_weight = normal_values(streams_of[25], (FF, D), FF ** -0.5, 0.09375, ((0, 32),), jnp.float32)
    reduce_bias = normal_values(streams_of[26], (D,), 0.5, 3.0, ((0, 32),), jnp.float32)
    third_gain = jnp.clip(1.0 + 0.18 * jax.random.normal(streams_of[27], (D,), jnp.float32), 0.1, 1.9)
    third_shift = normal_values(streams_of[28], (D,), 0.5, 3.0, ((0, 32),), jnp.float32)
    return {"tokens": tokens, "encoded": encoded, "cotangent": cotangent, "doc_ids": doc_ids, "block_ids": block_ids, "query_weight": query_weight, "key_weight": key_weight, "value_weight": value_weight, "out_weight": out_weight, "query_bias": query_bias, "value_bias": value_bias, "out_bias": out_bias, "first_gain": first_gain, "first_shift": first_shift, "probe_weight": probe_weight, "lookup_weight": lookup_weight, "content_weight": content_weight, "merge_weight": merge_weight, "probe_bias": probe_bias, "content_bias": content_bias, "merge_bias": merge_bias, "second_gain": second_gain, "second_shift": second_shift, "expand_weight": expand_weight, "expand_bias": expand_bias, "reduce_weight": reduce_weight, "reduce_bias": reduce_bias, "third_gain": third_gain, "third_shift": third_shift}


@jax.custom_vjp
def low(v):
    return lax.optimization_barrier(v.astype(jnp.bfloat16)).astype(jnp.float32)

@jax.custom_vjp
def low_back(v):
    return v

def low_keep(v):
    return (low(v), None)

def low_pass(kept, grad):
    return (grad,)

def back_keep(v):
    return (v, None)

def back_low(kept, grad):
    return (low(grad),)
low.defvjp(low_keep, low_pass)
low_back.defvjp(back_keep, back_low)
EPS = 1e-05
NEG = -1000000000.0
HIGH = lax.Precision.HIGHEST

def both_round(value):
    return low(low_back(value))

def matmul(left_arg, right_arg):
    return jnp.dot(left_arg, right_arg, precision=HIGH)

def norm_layer(hidden, gain, shift):
    row_mean = lax.optimization_barrier(jnp.mean(hidden, axis=-1, keepdims=True))
    centered = hidden - row_mean
    variance = lax.optimization_barrier(jnp.mean(centered * centered, axis=-1, keepdims=True))
    return centered * lax.rsqrt(variance + EPS) * gain + shift

def attend(queries, keys, values, query_doc, query_block, key_doc, key_block, masked):
    row_count = queries.shape[0]
    step_rows = math.gcd(row_count, 512)
    key_heads = keys.reshape(keys.shape[0], H, DH)
    value_heads = values.reshape(values.shape[0], H, DH)

    def one_block(items):
        query_part, doc_part, block_part = items
        scores = jnp.einsum('qhd,khd->hqk', query_part.reshape(step_rows, H, DH), key_heads, precision=HIGH)
        scores = low_back(scores)
        if masked:
            allow = (doc_part[:, None] == key_doc[None, :]) & (key_block[None, :] <= block_part[:, None])
            scores = jnp.where(allow[None], scores, NEG)
        probs = low(jax.nn.softmax(scores, axis=-1))
        return jnp.einsum('hqk,khd->qhd', probs, value_heads, precision=HIGH).reshape(step_rows, D)
    pieces = lax.map(jax.checkpoint(one_block), (queries.reshape(-1, step_rows, D), query_doc.reshape(-1, step_rows), query_block.reshape(-1, step_rows)))
    return pieces.reshape(row_count, D)

def layer(weights, token_rows, enc_rows, doc_row, block_row):
    query_weight, key_weight, value_weight, out_weight, query_bias, value_bias, out_bias, first_gain, first_shift, probe_weight, lookup_weight, content_weight, merge_weight, probe_bias, content_bias, merge_bias, second_gain, second_shift, expand_weight, expand_bias, reduce_weight, reduce_bias, third_gain, third_shift = weights
    scale = DH ** (-0.5)
    queries = both_round((matmul(token_rows, query_weight) + query_bias) * scale)
    keys = both_round(matmul(token_rows, key_weight))
    values = both_round(matmul(token_rows, value_weight) + value_bias)
    attended = both_round(attend(queries, keys, values, doc_row, block_row, doc_row, block_row, True))
    first_sum = token_rows + low_back(matmul(attended, out_weight)) + out_bias
    stream_one = low(norm_layer(first_sum, first_gain, first_shift))
    probe = both_round((matmul(stream_one, probe_weight) + probe_bias) * scale)
    enc_keys = both_round(matmul(enc_rows, lookup_weight))
    enc_values = both_round(matmul(enc_rows, content_weight) + content_bias)
    cross_attended = both_round(attend(probe, enc_keys, enc_values, doc_row, block_row, doc_row, block_row, False))
    second_sum = stream_one + low_back(matmul(cross_attended, merge_weight)) + merge_bias
    stream_two = low(norm_layer(second_sum, second_gain, second_shift))
    expanded = low_back(matmul(stream_two, expand_weight)) + expand_bias
    activated = low(jax.nn.gelu(expanded, approximate=False))
    third_sum = stream_two + low_back(matmul(activated, reduce_weight)) + reduce_bias
    return norm_layer(third_sum, third_gain, third_shift)

def reference(tokens, encoded, cotangent, doc_ids, block_ids, query_weight, key_weight, value_weight, out_weight, query_bias, value_bias, out_bias, first_gain, first_shift, probe_weight, lookup_weight, content_weight, merge_weight, probe_bias, content_bias, merge_bias, second_gain, second_shift, expand_weight, expand_bias, reduce_weight, reduce_bias, third_gain, third_shift):
    params = (query_weight, key_weight, value_weight, out_weight, query_bias, value_bias, out_bias, first_gain, first_shift, probe_weight, lookup_weight, content_weight, merge_weight, probe_bias, content_bias, merge_bias, second_gain, second_shift, expand_weight, expand_bias, reduce_weight, reduce_bias, third_gain, third_shift)

    def forward(weights, token_all, enc_all):
        lowered = tuple((low(weight) if weight.ndim == 2 else weight for weight in weights))
        checked = jax.checkpoint(layer)

        def step(carry, items):
            token_rows, enc_rows, doc_row, block_row = items
            return (carry, checked(lowered, token_rows, enc_rows, doc_row, block_row))
        _, result = lax.scan(step, jnp.zeros((), jnp.float32), (token_all, enc_all, doc_ids, block_ids))
        return result
    result, pullback = jax.vjp(forward, params, tokens.astype(jnp.float32), encoded.astype(jnp.float32))
    grads, token_grad, enc_grad = pullback(cotangent.astype(jnp.float32))
    return (result.astype(jnp.bfloat16), token_grad, enc_grad, grads[0], grads[1], grads[2], grads[3], grads[4], grads[5], grads[6], grads[7], grads[8], grads[9], grads[10], grads[11], grads[12], grads[13], grads[14], grads[15], grads[16], grads[17], grads[18], grads[19], grads[20], grads[21], grads[22], grads[23])
```

```python
import functools
import math

import jax
import jax.numpy as jnp
from jax import lax
from jax.experimental import pallas as pl
from jax.experimental.pallas import tpu as pltpu
from jax.sharding import PartitionSpec as P

H = 16
DH = 64

EPS = 1e-05
NEG = -1000000000.0
INV_ROOT_TWO = 0.7071067811865476
DENSITY_CONST = 0.3989422804014327
MESH = pl.DeviceIdType.MESH
BF = jnp.bfloat16
F32 = jnp.float32


def matmul(left_arg, right_arg):
    return jnp.dot(left_arg, right_arg, preferred_element_type=F32)


def left_outer(left_arg, right_arg):
    return lax.dot_general(
        left_arg, right_arg, (((0,), (0,)), ((), ())), preferred_element_type=F32
    )


def right_trans(left_arg, right_arg):
    return lax.dot_general(
        left_arg, right_arg, (((1,), (1,)), ((), ())), preferred_element_type=F32
    )


def layer_stats(hidden):
    row_mean = jnp.mean(hidden, axis=-1, keepdims=True)
    centered = hidden - row_mean
    inv_std = lax.rsqrt(jnp.mean(centered * centered, axis=-1, keepdims=True) + EPS)
    return (centered * inv_std, inv_std)


def layer_back(grad_norm, normed, inv_std):
    first_mean = jnp.mean(grad_norm, axis=-1, keepdims=True)
    second_mean = jnp.mean(grad_norm * normed, axis=-1, keepdims=True)
    return inv_std * (grad_norm - first_mean - normed * second_mean)


class Cube:
    def __init__(self, mesh):
        self.n_dp = mesh.shape["dp"]
        self.n_seq = mesh.shape["seq"]
        self.dp_bits = self.n_dp.bit_length() - 1
        self.seq_bits = self.n_seq.bit_length() - 1
        assert self.n_dp == 1 << self.dp_bits and self.n_seq == 1 << self.seq_bits
        self.n_dev = self.n_dp * self.n_seq

    def lead(self, full):
        return ((2,) * self.dp_bits if full else ()) + (self.n_seq,)


def bit_of(index, bit):
    return (index // (1 << bit)) % 2


def flipped(index, bit):
    return index + (1 << bit) * (1 - 2 * bit_of(index, bit))


def block_shape(rows, cols):
    if rows % 16 == 0:
        return (rows, cols)
    return (16, rows * cols // 16)


def meet(cube):
    dp, seq = lax.axis_index("dp"), lax.axis_index("seq")
    barrier = pltpu.get_barrier_semaphore()
    for bit in range(cube.dp_bits):
        pl.semaphore_signal(
            barrier, inc=1, device_id=(flipped(dp, bit), seq), device_id_type=MESH
        )
    for bit in range(cube.seq_bits):
        pl.semaphore_signal(
            barrier, inc=1, device_id=(dp, flipped(seq, bit)), device_id_type=MESH
        )
    pl.semaphore_wait(barrier, cube.dp_bits + cube.seq_bits)


def dim_order(cube, variant):
    bits = list(range(1, cube.dp_bits))
    return bits if variant == 0 else bits[::-1]


def gather_kernel(cube, kinds, *refs):
    count = len(kinds)
    ins, outs = refs[:count], refs[count : 2 * count]
    send_sem, recv_sem, local_sem = refs[2 * count :]
    dp, seq = lax.axis_index("dp"), lax.axis_index("seq")
    sends = []

    def region(full, open_bits, fixed, seq_part):
        if not full:
            return (seq_part,)
        places = []
        for bit in reversed(range(cube.dp_bits)):
            if bit in open_bits:
                places.append(slice(None))
            else:
                places.append(fixed.get(bit, bit_of(dp, bit)))
        return tuple(places) + (seq_part,)

    def push(array, slot, place, device):
        copy = pltpu.make_async_remote_copy(
            src_ref=outs[array].at[place],
            dst_ref=outs[array].at[place],
            send_sem=send_sem.at[array, slot],
            recv_sem=recv_sem.at[array, slot],
            device_id=device,
            device_id_type=MESH,
        )
        copy.start()
        sends.append(copy)
        return copy

    own = []
    for array, (full, _) in enumerate(kinds):
        copy = pltpu.make_async_copy(
            ins[array], outs[array].at[region(full, (), {}, seq)], local_sem.at[array]
        )
        copy.start()
        own.append(copy)
    meet(cube)
    latest = own
    for bit in range(cube.seq_bits):
        span = 1 << bit
        started = []
        for array, (full, _) in enumerate(kinds):
            latest[array].wait() if bit == 0 else latest[array].wait_recv()
            place = region(full, (), {}, pl.ds(seq - seq % span, span))
            started.append(push(array, bit, place, (dp, flipped(seq, bit))))
        latest = started
    every = pl.ds(0, cube.n_seq)
    cores = []
    slot = cube.seq_bits
    for stage in range(cube.dp_bits):
        started = []
        for array, (full, variant) in enumerate(kinds):
            if latest[array] is None:
                started.append(None)
                continue
            latest[array].wait_recv()
            if not full:
                started.append(None)
                continue
            order = dim_order(cube, variant)
            if stage < len(order):
                place = region(full, order[:stage], {}, every)
                device = (flipped(dp, order[stage]), seq)
                started.append(push(array, slot + 2 * stage, place, device))
            else:
                started.append(None)
            if stage == 0:
                fresh = region(full, (), {}, every)
            else:
                last = order[stage - 1]
                fresh = region(full, order[: stage - 1], {last: 1 - bit_of(dp, last)}, every)
            cores.append(push(array, slot + 2 * stage + 1, fresh, (flipped(dp, 0), seq)))
        latest = started
    for copy in cores:
        copy.wait_recv()
    for copy in sends:
        copy.wait_send()


def gather_all(cube, arrays, kinds, collective_id):
    outs = [
        jax.ShapeDtypeStruct(cube.lead(full) + array.shape, array.dtype)
        for array, (full, _) in zip(arrays, kinds)
    ]
    slots = cube.seq_bits + 2 * cube.dp_bits
    return pl.pallas_call(
        functools.partial(gather_kernel, cube, kinds),
        out_shape=outs,
        in_specs=[pl.BlockSpec(memory_space=pl.ANY)] * len(arrays),
        out_specs=[pl.BlockSpec(memory_space=pl.ANY)] * len(arrays),
        scratch_shapes=[
            pltpu.SemaphoreType.DMA((len(arrays), slots)),
            pltpu.SemaphoreType.DMA((len(arrays), slots)),
            pltpu.SemaphoreType.DMA((len(arrays),)),
        ],
        compiler_params=pltpu.CompilerParams(
            collective_id=collective_id, has_side_effects=True
        ),
        name="gather_weights",
    )(*arrays)


def add_blocks(total, part, places, rows, cols):
    count, pick = places
    step = rows
    while step * cols > 32768 and step % 32 == 0:
        step //= 2
    chunks = rows // step

    def body(index, carry):
        to, of = pick(index // chunks)
        part_rows = pl.ds(pl.multiple_of((index % chunks) * step, step), step)
        left = total[to + (part_rows,)].astype(F32)
        right = part[of + (part_rows,)].astype(F32)
        total[to + (part_rows,)] = (left + right).astype(total.dtype)
        return carry

    lax.fori_loop(0, count * chunks, body, 0)


def scatter_kernel(cube, kinds, *refs):
    count = len(kinds)
    ins, outs = refs[:count], refs[count : 2 * count]
    refs = refs[2 * count :]
    owns, parts = [], []
    for full, _ in kinds:
        stages = (cube.dp_bits if full else 0) + cube.seq_bits
        owns.append(refs[0])
        parts.append(refs[1 : 1 + stages])
        refs = refs[1 + stages :]
    send_sem, recv_sem, local_sem = refs
    dp, seq = lax.axis_index("dp"), lax.axis_index("seq")
    sends = []

    def push(array, stage, source, device):
        copy = pltpu.make_async_remote_copy(
            src_ref=source,
            dst_ref=parts[array][stage],
            send_sem=send_sem.at[array, stage],
            recv_sem=recv_sem.at[array, stage],
            device_id=device,
            device_id_type=MESH,
        )
        copy.start()
        sends.append(copy)
        return copy

    def dims(fixed, kept):
        return tuple(
            fixed[bit] if bit in fixed else kept for bit in reversed(range(1, cube.dp_bits))
        )

    top = cube.seq_bits - 1
    half = cube.n_seq // 2
    local, latest = [], []
    for array, (full, _) in enumerate(kinds):
        if full:
            lead = (slice(None),) * (cube.dp_bits - 1)
            kept = ins[array].at[lead + (bit_of(dp, 0),)]
        else:
            kept = ins[array].at[pl.ds(half * bit_of(seq, top), half)]
        copy = pltpu.make_async_copy(kept, owns[array], local_sem.at[array])
        copy.start()
        local.append(copy)
    meet(cube)
    for array, (full, _) in enumerate(kinds):
        if full:
            lead = (slice(None),) * (cube.dp_bits - 1)
            source = ins[array].at[lead + (1 - bit_of(dp, 0),)]
            device = (flipped(dp, 0), seq)
        else:
            source = ins[array].at[pl.ds(half * (1 - bit_of(seq, top)), half)]
            device = (dp, flipped(seq, top))
        latest.append(push(array, 0, source, device))

    longest = cube.dp_bits + cube.seq_bits
    for stage in range(longest):
        for array, (full, variant) in enumerate(kinds):
            stages = (cube.dp_bits if full else 0) + cube.seq_bits
            if stage >= stages:
                continue
            rows, cols = outs[array].shape
            order = dim_order(cube, variant) if full else []
            own, part = owns[array], parts[array][stage]
            if stage == 0:
                local[array].wait()
            latest[array].wait_recv()
            after = max(stage - (cube.dp_bits - 1), 0) if full else stage + 1
            closed = order[: min(stage, len(order))]
            fixed = {bit: bit_of(dp, bit) for bit in closed}
            open_bits = [
                bit for bit in reversed(range(1, cube.dp_bits)) if full and bit not in closed
            ]
            span = cube.n_seq >> after
            base = seq - seq % span
            if not full:
                base = base - half * bit_of(seq, top)
            if stage == stages - 1:
                where = (dims(fixed, None) if full else ()) + (base,)
                outs[array][...] = own[where].astype(F32) + part[0].astype(F32)
                continue

            def pick(index, full=full, fixed=fixed, open_bits=open_bits, span=span, base=base):
                place = index % span
                rest = index // span
                values = {}
                for bit in reversed(open_bits):
                    values[bit] = rest % 2
                    rest = rest // 2
                of = tuple(values[bit] for bit in open_bits) + (place,)
                to = (dims({**fixed, **values}, None) if full else ()) + (base + place,)
                return to, of

            amount = span * (1 << len(open_bits))
            add_blocks(own, part, (amount, pick), rows, cols)
            if full and stage < len(order):
                bit = order[stage]
                lead = dims({**fixed, bit: 1 - bit_of(dp, bit)}, slice(None))
                source = own.at[lead + (pl.ds(0, cube.n_seq),)]
                device = (flipped(dp, bit), seq)
            else:
                bit = cube.seq_bits - 1 - after
                other = base + (1 - bit_of(seq, bit)) * (span // 2)
                lead = dims(fixed, None) if full else ()
                source = own.at[lead + (pl.ds(other, span // 2),)]
                device = (dp, flipped(seq, bit))
            latest[array] = push(array, stage + 1, source, device)
    for copy in sends:
        copy.wait_send()


def scatter_all(cube, arrays, kinds, collective_id):
    outs, scratch = [], []
    for array, (full, _) in zip(arrays, kinds):
        block = array.shape[-2:]
        outs.append(jax.ShapeDtypeStruct(block, F32))
        if full:
            shape = (2,) * (cube.dp_bits - 1) + (cube.n_seq,)
            scratch.append(pltpu.VMEM(shape + block, array.dtype))
            for stage in range(cube.dp_bits):
                lead = (2,) * (cube.dp_bits - 1 - stage) + (cube.n_seq,)
                scratch.append(pltpu.VMEM(lead + block, array.dtype))
        else:
            scratch.append(pltpu.VMEM((cube.n_seq // 2,) + block, array.dtype))
        for stage in range(cube.seq_bits):
            scratch.append(pltpu.VMEM((cube.n_seq >> (stage + 1),) + block, array.dtype))
    slots = cube.seq_bits + cube.dp_bits
    scratch += [
        pltpu.SemaphoreType.DMA((len(arrays), slots)),
        pltpu.SemaphoreType.DMA((len(arrays), slots)),
        pltpu.SemaphoreType.DMA((len(arrays),)),
    ]
    return pl.pallas_call(
        functools.partial(scatter_kernel, cube, kinds),
        out_shape=outs,
        in_specs=[pl.BlockSpec(memory_space=pl.ANY)] * len(arrays),
        out_specs=[pl.BlockSpec(memory_space=pltpu.VMEM)] * len(arrays),
        scratch_shapes=scratch,
        compiler_params=pltpu.CompilerParams(
            collective_id=collective_id,
            has_side_effects=True,
            vmem_limit_bytes=56 * 1024 * 1024,
        ),
        name="scatter_grads",
    )(*arrays)


def head_slice(array, group_index, group_size):
    part = lax.dynamic_slice_in_dim(array, group_index * group_size * DH, group_size * DH, 2)
    return part.reshape(array.shape[0], array.shape[1], group_size, DH)


def regroup(stacked):
    group_count, seq_count, row_count, group_span = stacked.shape
    return jnp.moveaxis(stacked, 0, 2).reshape(seq_count, row_count, group_count * group_span)


def masked_scores(query_part, key_part, allow):
    scores = jnp.einsum("sqhd,skhd->shqk", query_part, key_part, preferred_element_type=F32)
    if allow is not None:
        scores = jnp.where(allow[:, None], scores, NEG)
    return scores


def attn_forward(queries, keys, values, allow):
    group_size = math.gcd(H, 4)

    def one_group(group_index):
        query_part = head_slice(queries, group_index, group_size)
        key_part = head_slice(keys, group_index, group_size)
        value_part = head_slice(values, group_index, group_size)
        scores = masked_scores(query_part, key_part, allow)
        row_max = jnp.max(scores, axis=-1, keepdims=True)
        expon = jnp.exp(scores - row_max)
        row_total = jnp.sum(expon, axis=-1, keepdims=True)
        probab = (expon / row_total).astype(BF)
        attended = jnp.einsum("shqk,skhd->sqhd", probab, value_part, preferred_element_type=F32)
        attended = attended.reshape(queries.shape[0], queries.shape[1], group_size * DH)
        return (attended, (row_max + jnp.log(row_total))[..., 0])

    stacked, log_sums = lax.map(one_group, jnp.arange(H // group_size, dtype=jnp.int32))
    return (regroup(stacked), log_sums)


def attn_backward(queries, keys, values, allow, log_sums, grad_attended):
    group_size = math.gcd(H, 4)

    def one_group(items):
        group_index, log_part = items
        query_part = head_slice(queries, group_index, group_size)
        key_part = head_slice(keys, group_index, group_size)
        value_part = head_slice(values, group_index, group_size)
        grad_part = head_slice(grad_attended, group_index, group_size)
        scores = masked_scores(query_part, key_part, allow)
        probab = jnp.exp(scores - log_part[..., None])
        grad_probs = jnp.einsum("sqhd,skhd->shqk", grad_part, value_part, preferred_element_type=F32)
        row_delta = jnp.sum(probab * grad_probs, axis=-1, keepdims=True)
        grad_scores = (probab * (grad_probs - row_delta)).astype(BF)
        grad_query = jnp.einsum("shqk,skhd->sqhd", grad_scores, key_part, preferred_element_type=F32)
        grad_key = jnp.einsum("shqk,sqhd->skhd", grad_scores, query_part, preferred_element_type=F32)
        grad_value = jnp.einsum(
            "shqk,sqhd->skhd", probab.astype(BF), grad_part, preferred_element_type=F32
        )
        seq_count = queries.shape[0]
        return (
            grad_query.reshape(seq_count, queries.shape[1], group_size * DH),
            grad_key.reshape(seq_count, keys.shape[1], group_size * DH),
            grad_value.reshape(seq_count, keys.shape[1], group_size * DH),
        )

    group_ids = jnp.arange(H // group_size, dtype=jnp.int32)
    grad_queries, grad_keys, grad_values = lax.map(one_group, (group_ids, log_sums))
    return (regroup(grad_queries), regroup(grad_keys), regroup(grad_values))


WIDE = 13


def local(
    cube,
    tokens,
    encoded,
    cotangent,
    doc_ids,
    block_ids,
    query_weight,
    key_weight,
    value_weight,
    out_weight,
    query_bias,
    value_bias,
    out_bias,
    first_gain,
    first_shift,
    probe_weight,
    lookup_weight,
    content_weight,
    merge_weight,
    probe_bias,
    content_bias,
    merge_bias,
    second_gain,
    second_shift,
    expand_weight,
    expand_bias,
    reduce_weight,
    reduce_bias,
    third_gain,
    third_shift,
):
    seq_count, local_rows, feat_width = tokens.shape
    assert seq_count == 1
    enc_local = encoded.shape[1]
    scale = DH ** (-0.5)
    flat = tokens.reshape(local_rows, feat_width)
    enc_flat = encoded.reshape(enc_local, feat_width)

    weights = [
        query_weight, key_weight, value_weight, out_weight, probe_weight,
        lookup_weight, content_weight, merge_weight, expand_weight, reduce_weight,
    ]
    vectors = [
        query_bias, value_bias, out_bias, first_gain, first_shift, probe_bias, content_bias,
        merge_bias, second_gain, second_shift, reduce_bias, third_gain, third_shift,
    ]
    part = vectors[0].shape[0]
    long_part = expand_bias.shape[0]
    held = WIDE * part + long_part
    padded = -(-held // 1024) * 1024
    vec_block = (8, padded // 8)
    packed = jnp.concatenate(vectors + [expand_bias, jnp.zeros((padded - held,), F32)])
    blocks = [w.astype(BF).reshape(block_shape(*w.shape)) for w in weights]
    kinds = [(False, 0), (False, 0)] + [(True, i % 2) for i in range(len(blocks))] + [(True, 0)]
    gathered = gather_all(
        cube, [flat, enc_flat] + blocks + [packed.reshape(vec_block)], kinds, 0
    )
    n_dev = cube.n_dev
    tok_all = gathered[0].reshape(cube.n_seq * local_rows, feat_width)
    enc_all = gathered[1].reshape(cube.n_seq * enc_local, feat_width)
    (
        query_mat, key_mat, value_mat, out_mat, probe_mat,
        lookup_mat, content_mat, merge_mat, expand_mat, reduce_mat,
    ) = [
        g.reshape(w.shape[0] * n_dev, w.shape[1]) for g, w in zip(gathered[2:12], weights)
    ]
    vec_all = gathered[12].reshape(n_dev, padded)
    wide_all = (
        vec_all[:, : WIDE * part].reshape(n_dev, WIDE, part).transpose(1, 0, 2).reshape(WIDE, -1)
    )
    (
        query_vec, value_vec, out_vec, gain_first, shift_first, probe_vec, content_vec,
        merge_vec, gain_second, shift_second, reduce_vec, gain_third, shift_third,
    ) = [wide_all[i] for i in range(WIDE)]
    expand_vec = vec_all[:, WIDE * part : held].reshape(-1)

    offset = lax.axis_index("seq") * local_rows
    query_doc = lax.dynamic_slice_in_dim(doc_ids, offset, local_rows, 1)
    query_block = lax.dynamic_slice_in_dim(block_ids, offset, local_rows, 1)
    allow = (query_doc[:, :, None] == doc_ids[:, None, :]) & (
        block_ids[:, None, :] <= query_block[:, :, None]
    )
    token_float = flat.astype(F32)
    queries = ((matmul(flat, query_mat) + query_vec) * scale).astype(BF)
    all_keys = matmul(tok_all, key_mat).astype(BF)
    all_values = (matmul(tok_all, value_mat) + value_vec).astype(BF)
    self_out, self_logs = attn_forward(queries[None], all_keys[None], all_values[None], allow)
    self_outb = self_out[0].astype(BF)
    first_sum = token_float + matmul(self_outb, out_mat) + out_vec
    normed_one, inv_one = layer_stats(first_sum)
    stream_one = (normed_one * gain_first + shift_first).astype(BF)
    probe = ((matmul(stream_one, probe_mat) + probe_vec) * scale).astype(BF)
    enc_keys = matmul(enc_all, lookup_mat).astype(BF)
    enc_values = (matmul(enc_all, content_mat) + content_vec).astype(BF)
    cross_out, cross_logs = attn_forward(probe[None], enc_keys[None], enc_values[None], None)
    cross_outb = cross_out[0].astype(BF)
    second_sum = stream_one.astype(F32) + matmul(cross_outb, merge_mat) + merge_vec
    normed_two, inv_two = layer_stats(second_sum)
    stream_two = (normed_two * gain_second + shift_second).astype(BF)
    expanded = matmul(stream_two, expand_mat) + expand_vec
    activated = jax.nn.gelu(expanded, approximate=False).astype(BF)
    third_sum = stream_two.astype(F32) + matmul(activated, reduce_mat) + reduce_vec
    normed_three, inv_three = layer_stats(third_sum)
    output = (normed_three * gain_third + shift_third).astype(BF)

    grad_output = cotangent.reshape(local_rows, feat_width).astype(F32)
    g_shift_third = jnp.sum(grad_output, axis=0)
    g_gain_third = jnp.sum(grad_output * normed_three, axis=0)
    grad_three = layer_back(grad_output * gain_third, normed_three, inv_three)
    reduce_rows = grad_three.astype(BF)
    g_reduce_vec = jnp.sum(grad_three, axis=0)
    g_reduce_mat = left_outer(activated, reduce_rows)
    grad_act = right_trans(reduce_rows, reduce_mat)
    slope = 0.5 * (
        1.0 + jax.scipy.special.erf(expanded * INV_ROOT_TWO)
    ) + expanded * DENSITY_CONST * jnp.exp(-0.5 * expanded * expanded)
    grad_expanded = grad_act * slope
    g_expand_vec = jnp.sum(grad_expanded, axis=0)
    expand_rows = grad_expanded.astype(BF)
    g_expand_mat = left_outer(stream_two, expand_rows)

    def spread(grad, weight):
        return grad.astype(BF).reshape(cube.lead(True) + block_shape(*weight.shape))

    expand_sum, reduce_sum = scatter_all(
        cube,
        [spread(g_reduce_mat, reduce_weight), spread(g_expand_mat, expand_weight)],
        [(True, 0), (True, 1)],
        1,
    )[::-1]

    grad_two = grad_three + right_trans(expand_rows, expand_mat)
    g_shift_second = jnp.sum(grad_two, axis=0)
    g_gain_second = jnp.sum(grad_two * normed_two, axis=0)
    grad_second = layer_back(grad_two * gain_second, normed_two, inv_two)
    merge_rows = grad_second.astype(BF)
    g_merge_vec = jnp.sum(grad_second, axis=0)
    g_merge_mat = left_outer(cross_outb, merge_rows)
    grad_cross = right_trans(merge_rows, merge_mat).astype(BF)
    grad_probe, grad_enc_keys, grad_enc_values = attn_backward(
        probe[None], enc_keys[None], enc_values[None], None, cross_logs, grad_cross[None]
    )
    probe_rows = (grad_probe[0].astype(BF).astype(F32) * scale).astype(BF)
    g_probe_vec = jnp.sum(probe_rows.astype(F32), axis=0)
    g_probe_mat = left_outer(stream_one, probe_rows)
    enc_key_rows = grad_enc_keys[0].astype(BF)
    enc_value_rows = grad_enc_values[0].astype(BF)
    g_lookup_mat = left_outer(enc_all, enc_key_rows)
    g_content_mat = left_outer(enc_all, enc_value_rows)
    g_content_vec = jnp.sum(grad_enc_values[0], axis=0)
    enc_part = right_trans(enc_key_rows, lookup_mat) + right_trans(enc_value_rows, content_mat)
    grad_one = grad_second + right_trans(probe_rows, probe_mat)
    g_shift_first = jnp.sum(grad_one, axis=0)
    g_gain_first = jnp.sum(grad_one * normed_one, axis=0)
    grad_first = layer_back(grad_one * gain_first, normed_one, inv_one)
    out_rows = grad_first.astype(BF)
    g_out_vec = jnp.sum(grad_first, axis=0)
    g_out_mat = left_outer(self_outb, out_rows)
    grad_self = right_trans(out_rows, out_mat).astype(BF)
    grad_query, grad_keys, grad_values = attn_backward(
        queries[None], all_keys[None], all_values[None], allow, self_logs, grad_self[None]
    )
    query_rows = (grad_query[0].astype(BF).astype(F32) * scale).astype(BF)
    key_rows = grad_keys[0].astype(BF)
    value_rows = grad_values[0].astype(BF)
    g_query_vec = jnp.sum(query_rows.astype(F32), axis=0)
    g_value_vec = jnp.sum(grad_values[0], axis=0)
    g_query_mat = left_outer(flat, query_rows)
    g_key_mat = left_outer(tok_all, key_rows)
    g_value_mat = left_outer(tok_all, value_rows)
    tok_part = right_trans(key_rows, key_mat) + right_trans(value_rows, value_mat)
    tok_own = grad_first + right_trans(query_rows, query_mat)

    wide_grads = jnp.stack(
        [
            g_query_vec, g_value_vec, g_out_vec, g_gain_first, g_shift_first, g_probe_vec, g_content_vec,
            g_merge_vec, g_gain_second, g_shift_second, g_reduce_vec, g_gain_third, g_shift_third,
        ]
    )
    vec_grads = jnp.concatenate(
        [
            wide_grads.reshape(WIDE, n_dev, part).transpose(1, 0, 2).reshape(n_dev, WIDE * part),
            g_expand_vec.reshape(n_dev, long_part),
            jnp.zeros((n_dev, padded - held), F32),
        ],
        axis=1,
    ).reshape(cube.lead(True) + vec_block)
    mats = [
        g_merge_mat, g_probe_mat, g_lookup_mat, g_content_mat, g_out_mat,
        g_query_mat, g_key_mat, g_value_mat,
    ]
    shards = [
        merge_weight, probe_weight, lookup_weight, content_weight, out_weight,
        query_weight, key_weight, value_weight,
    ]
    sums = scatter_all(
        cube,
        [
            enc_part.astype(BF).reshape(cube.n_seq, enc_local, feat_width),
            tok_part.astype(BF).reshape(cube.n_seq, local_rows, feat_width),
        ]
        + [spread(g, w) for g, w in zip(mats, shards)]
        + [vec_grads],
        [(False, 0), (False, 0)] + [(True, i % 2) for i in range(len(mats))] + [(True, 0)],
        2,
    )
    encoded_grad = sums[0]
    tokens_grad = tok_own + sums[1]
    (
        merge_sum, probe_sum, lookup_sum, content_sum, out_sum, query_sum, key_sum, value_sum,
    ) = [s.reshape(w.shape) for s, w in zip(sums[2:10], shards)]
    expand_sum = expand_sum.reshape(expand_weight.shape)
    reduce_sum = reduce_sum.reshape(reduce_weight.shape)
    vec_sum = sums[10].reshape(padded)
    (
        query_vs, value_vs, out_vs, gain1_vs, shift1_vs, probe_vs, content_vs,
        merge_vs, gain2_vs, shift2_vs, reduce_vs, gain3_vs, shift3_vs,
    ) = [vec_sum[i * part : (i + 1) * part] for i in range(WIDE)]
    expand_vs = vec_sum[WIDE * part : held]
    return (
        output[None],
        tokens_grad[None],
        encoded_grad[None],
        query_sum,
        key_sum,
        value_sum,
        out_sum,
        query_vs,
        value_vs,
        out_vs,
        gain1_vs,
        shift1_vs,
        probe_sum,
        lookup_sum,
        content_sum,
        merge_sum,
        probe_vs,
        content_vs,
        merge_vs,
        gain2_vs,
        shift2_vs,
        expand_sum,
        expand_vs,
        reduce_sum,
        reduce_vs,
        gain3_vs,
        shift3_vs,
    )


def solution(mesh):
    rows = P("dp", "seq", None)
    ids = P("dp", None)
    mat = P(("dp", "seq"), None)
    vec = P(("dp", "seq"))
    return jax.shard_map(
        functools.partial(local, Cube(mesh)),
        mesh=mesh,
        in_specs=(
            (rows, rows, rows, ids, ids)
            + (mat, mat, mat, mat, vec, vec, vec, vec, vec)
            + (mat, mat, mat, mat, vec, vec, vec, vec, vec)
            + (mat, vec, mat, vec, vec, vec)
        ),
        out_specs=(
            (rows, rows, rows)
            + (mat, mat, mat, mat, vec, vec, vec, vec, vec)
            + (mat, mat, mat, mat, vec, vec, vec, vec, vec)
            + (mat, vec, mat, vec, vec, vec)
        ),
        check_vma=False,
    )
```

```python
import functools
import itertools
import math

import jax
import jax.numpy as jnp
from jax import lax
from jax.experimental import pallas as pl
from jax.experimental.pallas import tpu as pltpu
from jax.sharding import PartitionSpec as P

H = 16
DH = 64

EPS = 1e-05
NEG = -1000000000.0
INV_ROOT_TWO = 0.7071067811865476
DENSITY_CONST = 0.3989422804014327
MESH = pl.DeviceIdType.MESH
PIECE = 16384
BF = jnp.bfloat16
F32 = jnp.float32


def matmul(left_arg, right_arg):
    return jnp.dot(left_arg, right_arg, preferred_element_type=F32)


def left_outer(left_arg, right_arg):
    return lax.dot_general(
        left_arg, right_arg, (((0,), (0,)), ((), ())), preferred_element_type=F32
    )


def right_trans(left_arg, right_arg):
    return lax.dot_general(
        left_arg, right_arg, (((1,), (1,)), ((), ())), preferred_element_type=F32
    )


def layer_stats(hidden):
    row_mean = jnp.mean(hidden, axis=-1, keepdims=True)
    centered = hidden - row_mean
    inv_std = lax.rsqrt(jnp.mean(centered * centered, axis=-1, keepdims=True) + EPS)
    return (centered * inv_std, inv_std)


def layer_back(grad_norm, normed, inv_std):
    first_mean = jnp.mean(grad_norm, axis=-1, keepdims=True)
    second_mean = jnp.mean(grad_norm * normed, axis=-1, keepdims=True)
    return inv_std * (grad_norm - first_mean - normed * second_mean)


class Cube:
    def __init__(self, mesh):
        self.n_dp = mesh.shape["dp"]
        self.n_seq = mesh.shape["seq"]
        self.dp_bits = self.n_dp.bit_length() - 1
        assert self.n_dp == 1 << self.dp_bits
        self.n_dev = self.n_dp * self.n_seq

    def lead(self, full):
        return ((2,) * self.dp_bits if full else ()) + (self.n_seq,)


class Place:
    def __init__(self, cube):
        self.dp, self.seq = lax.axis_index("dp"), lax.axis_index("seq")
        self.bits, self.flips = [], []
        rest = self.dp
        for bit in range(cube.dp_bits):
            half = rest // 2
            self.bits.append(rest - 2 * half)
            self.flips.append(self.dp + (1 << bit) * (1 - 2 * self.bits[-1]))
            rest = half


def block_shape(rows, cols):
    if rows % 16 == 0:
        return (rows, cols)
    return (16, rows * cols // 16)


def dim_order(cube, variant):
    bits = list(range(1, cube.dp_bits))
    return bits if variant == 0 else bits[::-1]


def meet(cube, here):
    dp, seq = here.dp, here.seq
    barrier = pltpu.get_barrier_semaphore()

    def greet(device):
        pl.semaphore_signal(barrier, inc=1, device_id=device, device_id_type=MESH)

    for bit in range(cube.dp_bits):
        greet((here.flips[bit], seq))
    greet((dp, lax.rem(seq + 1, cube.n_seq)))
    greet((dp, lax.rem(seq + cube.n_seq - 1, cube.n_seq)))
    pl.semaphore_wait(barrier, cube.dp_bits + 2)


def in_slots(pieces, lag):
    depth = max(len(stages) for stages in pieces)
    for slot in range(len(pieces) + lag * (depth - 1)):
        for k in reversed(range(depth)):
            p = slot - lag * k
            if 0 <= p < len(pieces) and k < len(pieces[p]):
                pieces[p][k]()


def remote(source, target, send_sem, recv_sem, device):
    return pltpu.make_async_remote_copy(
        src_ref=source,
        dst_ref=target,
        send_sem=send_sem,
        recv_sem=recv_sem,
        device_id=device,
        device_id_type=MESH,
    )


def gather_stages(cube, here, full, variant, source, target, send_sem, recv_sem, local_sem):
    dp, seq = here.dp, here.seq
    n = cube.n_seq
    order = dim_order(cube, variant)
    every = pl.ds(0, n)
    waits = []

    def region(open_bits, fixed, seq_part):
        if not full:
            return (seq_part,)
        places = []
        for bit in reversed(range(cube.dp_bits)):
            if bit in open_bits:
                places.append(slice(None))
            else:
                places.append(fixed.get(bit, here.bits[bit]))
        return tuple(places) + (seq_part,)

    def move(place, slot, device):
        at = target.at[place]
        return remote(at, at, send_sem.at[slot], recv_sem.at[slot], device)

    own = pltpu.make_async_copy(source, target.at[region((), {}, seq)], local_sem)

    def line(step, way):
        slot = 2 * step + (1 if way > 0 else 0)
        block = seq - way * step
        inside = (seq + way >= 0) & (seq + way < n)
        sends = inside & (block >= 0) & (block < n)
        copy = lambda: move(region((), {}, block), slot, (dp, seq + way))
        came = seq - way * (step + 1)
        gets = (came >= 0) & (came < n)
        arrival = lambda: move(region((), {}, came), slot, (dp, seq - way))
        return sends, copy, gets, arrival

    def line_start(step):
        for way in (1, -1):
            sends, copy, _, _ = line(step, way)
            pl.when(sends)(lambda: copy().start())
            waits.append((sends, copy))

    def line_wait(step):
        for way in (1, -1):
            _, _, gets, arrival = line(step, way)
            pl.when(gets)(lambda: arrival().wait_recv())

    base = 2 * (n - 1)
    cores, arrivals = [], []

    def dims_start(stage):
        if stage < len(order):
            copy = move(
                region(order[:stage], {}, every), base + 2 * stage, (here.flips[order[stage]], seq)
            )
            copy.start()
            waits.append((None, copy))
            arrivals.append(copy)
        if stage == 0:
            fresh = region((), {}, every)
        else:
            last = order[stage - 1]
            fresh = region(order[: stage - 1], {last: 1 - here.bits[last]}, every)
        copy = move(fresh, base + 2 * stage + 1, (here.flips[0], seq))
        copy.start()
        waits.append((None, copy))
        cores.append(copy)

    def first():
        own.wait()
        line_start(0)

    stages = [first]
    for step in range(n - 1):

        def after_line(step=step):
            line_wait(step)
            if step < n - 2:
                line_start(step + 1)
            elif full:
                dims_start(0)

        stages.append(after_line)
    if full:
        for stage in range(len(order)):

            def after_dims(stage=stage):
                arrivals[stage].wait_recv()
                dims_start(stage + 1)

            stages.append(after_dims)

        def last():
            for copy in cores:
                copy.wait_recv()

        stages.append(last)

    def finish():
        for sends, copy in waits:
            if sends is None:
                copy.wait_send()
            else:
                pl.when(sends)(lambda: copy().wait_send())

    return own, stages, finish


def gather_slots(cube):
    return 2 * (cube.n_seq - 1) + 2 * cube.dp_bits


def gather_kernel(cube, pieces, *refs):
    count = 1 + max(piece[0] for piece in pieces)
    ins, outs = refs[:count], refs[count : 2 * count]
    send_sem, recv_sem, local_sem = refs[2 * count :]
    here = Place(cube)
    plans = []
    for index, (array, full, variant, col, cols) in enumerate(pieces):
        lead = cube.dp_bits * full + 1
        cut = (slice(None), pl.ds(col, cols))
        plans.append(
            gather_stages(
                cube,
                here,
                full,
                variant,
                ins[array].at[cut],
                outs[array].at[(slice(None),) * lead + cut],
                send_sem.at[index],
                recv_sem.at[index],
                local_sem.at[index],
            )
        )
    for own, _, _ in plans:
        own.start()
    meet(cube, here)
    in_slots([stages for _, stages, _ in plans], 3)
    for _, _, finish in plans:
        finish()


def cut_columns(kinds, arrays):
    whole, along = [], []
    for index, (full, array) in enumerate(zip(kinds, arrays)):
        cols = array.shape[-1]
        count = max(1, math.prod(array.shape[-2:]) // (PIECE if full else PIECE))
        while cols % (128 * count):
            count //= 2
        width = cols // count
        for i in range(count):
            if full:
                whole.append((index, True, len(whole) % 2, width * i, width))
            else:
                along.append((index, False, 0, width * i, width))
    placed = [((i + 0.5) / len(whole), 0, piece) for i, piece in enumerate(whole)]
    placed += [((i + 0.5) / len(along), 1, piece) for i, piece in enumerate(along)]
    return tuple(piece for _, _, piece in sorted(placed, key=lambda item: item[:2]))


def gather_all(cube, arrays, kinds, collective_id):
    pieces = cut_columns(kinds, arrays)
    outs = [
        jax.ShapeDtypeStruct(cube.lead(full) + array.shape, array.dtype)
        for array, full in zip(arrays, kinds)
    ]
    slots = gather_slots(cube)
    return pl.pallas_call(
        functools.partial(gather_kernel, cube, pieces),
        out_shape=outs,
        in_specs=[pl.BlockSpec(memory_space=pl.ANY)] * len(arrays),
        out_specs=[pl.BlockSpec(memory_space=pl.ANY)] * len(arrays),
        scratch_shapes=[
            pltpu.SemaphoreType.DMA((len(pieces), slots)),
            pltpu.SemaphoreType.DMA((len(pieces), slots)),
            pltpu.SemaphoreType.DMA((len(pieces),)),
        ],
        compiler_params=pltpu.CompilerParams(
            collective_id=collective_id, has_side_effects=True
        ),
        name="gather_weights",
    )(*arrays)


def add_block(total, part):
    total[...] = (total[...].astype(F32) + part[...].astype(F32)).astype(total.dtype)


def add_rows(pairs, count, rows, cols):
    step = rows
    while step * cols > 32768 and step % 32 == 0:
        step //= 2

    def body(index, carry):
        for total, part in pairs:
            for row in range(0, rows, step):
                at = (index, pl.ds(row, step))
                add_block(total.at[at], part.at[at])
        return carry

    lax.fori_loop(0, count, body, 0)


def scatter_stages(
    cube, here, full, variant, source, out, own, parts, send_sem, recv_sem, local_sem
):
    dp, seq = here.dp, here.seq
    n = cube.n_seq
    order = dim_order(cube, variant) if full else []
    rows, cols = out.shape
    line_part = parts[-1]
    waits = []
    arrivals = []

    def dims(fixed, kept):
        return tuple(
            fixed[bit] if bit in fixed else kept for bit in reversed(range(1, cube.dp_bits))
        )

    mine = {bit: here.bits[bit] for bit in range(1, cube.dp_bits)}
    settled = dims(mine, None) if full else ()
    lead = (slice(None),) * (cube.dp_bits - 1)
    kept = source.at[lead + (here.bits[0],)] if full else source
    local = pltpu.make_async_copy(kept, own, local_sem)

    def push(stage, what, device):
        copy = remote(what, parts[stage], send_sem.at[stage], recv_sem.at[stage], device)
        copy.start()
        waits.append((None, copy))
        arrivals.append(copy)

    base = cube.dp_bits if full else 0

    def line(step, way):
        target = seq + way * (n - 1 - step)
        passes = (target >= 0) & (target < n)
        further = passes & ((seq > 0) if way > 0 else (seq < n - 1))
        slot = n if way < 0 and step == n - 2 else target
        block = own.at[settled + (target,)]
        index = base + 2 * step + (1 if way > 0 else 0)

        def copy():
            return remote(
                block, line_part.at[slot], send_sem.at[index], recv_sem.at[index], (dp, seq + way)
            )

        def arrival():
            at = line_part.at[target]
            return remote(at, at, send_sem.at[index - 2], recv_sem.at[index - 2], (dp, seq - way))

        return target, passes, further, copy, arrival

    def line_step(step):
        for way in (1, -1):
            target, passes, further, copy, arrival = line(step, way)
            if step > 0:

                @pl.when(further)
                def _():
                    arrival().wait_recv()
                    to, of = own.at[settled + (pl.ds(target, 1),)], line_part.at[pl.ds(target, 1)]
                    add_rows([(to, of)], 1, rows, cols)

            pl.when(passes)(lambda: copy().start())
            waits.append((passes, copy))

    def start():
        local.start()
        if full:
            push(0, source.at[lead + (1 - here.bits[0],)], (here.flips[0], seq))

    def after_dims(stage):
        if stage == 0:
            local.wait()
        arrivals[stage].wait_recv()
        closed = order[:stage]
        fixed = {bit: mine[bit] for bit in closed}
        open_bits = [bit for bit in reversed(range(1, cube.dp_bits)) if bit not in closed]

        pairs = []
        for values in itertools.product((0, 1), repeat=len(open_bits)):
            to = dims({**fixed, **dict(zip(open_bits, values))}, None)
            pairs.append((own.at[to], parts[stage].at[values]))
        add_rows(pairs, n, rows, cols)
        if stage < len(order):
            bit = order[stage]
            at = dims({**fixed, bit: 1 - mine[bit]}, slice(None)) + (pl.ds(0, n),)
            push(stage + 1, own.at[at], (here.flips[bit], seq))
        else:
            line_step(0)

    def last():
        where = settled + (seq,)

        def sem(way):
            return recv_sem.at[base + 2 * (n - 2) + (1 if way > 0 else 0)]

        @pl.when(seq > 0)
        def _():
            at = line_part.at[seq]
            remote(at, at, send_sem.at[base], sem(1), (dp, seq - 1)).wait_recv()

        @pl.when(seq < n - 1)
        def _():
            at = line_part.at[n]
            remote(at, at, send_sem.at[base], sem(-1), (dp, seq + 1)).wait_recv()

        @pl.when(seq == 0)
        def _():
            out[...] = own[where].astype(F32) + line_part[n].astype(F32)

        @pl.when(seq == n - 1)
        def _():
            out[...] = own[where].astype(F32) + line_part[n - 1].astype(F32)

        @pl.when((seq > 0) & (seq < n - 1))
        def _():
            both = line_part[seq].astype(F32) + line_part[n].astype(F32)
            out[...] = own[where].astype(F32) + both

    stages = [start]
    if full:
        stages += [functools.partial(after_dims, stage) for stage in range(cube.dp_bits)]
    else:

        def begin():
            local.wait()
            line_step(0)

        stages.append(begin)
    stages += [functools.partial(line_step, step) for step in range(1, n - 1)]
    stages.append(last)

    def finish():
        for passes, copy in waits:
            if passes is None:
                copy.wait_send()
            else:
                pl.when(passes)(lambda: copy().wait_send())

    return stages, finish


def scatter_kernel(cube, pieces, *refs):
    count = 1 + max(piece[0] for piece in pieces)
    ins, outs = refs[:count], refs[count : 2 * count]
    refs = refs[2 * count :]
    send_sem, recv_sem, local_sem = refs[-3:]
    here = Place(cube)
    plans = []
    for index, (array, full, variant, col, cols) in enumerate(pieces):
        held = 2 + (cube.dp_bits if full else 0)
        cut = (slice(None), pl.ds(col, cols))
        plans.append(
            scatter_stages(
                cube,
                here,
                full,
                variant,
                ins[array].at[(slice(None),) * (cube.dp_bits * full + 1) + cut],
                outs[array].at[cut],
                refs[0],
                refs[1:held],
                send_sem.at[index],
                recv_sem.at[index],
                local_sem.at[index],
            )
        )
        refs = refs[held:]
    meet(cube, here)
    in_slots([stages for stages, _ in plans], 2)
    for _, finish in plans:
        finish()


def scatter_all(cube, arrays, kinds, collective_id):
    pieces = cut_columns(kinds, arrays)
    outs = [jax.ShapeDtypeStruct(array.shape[-2:], F32) for array in arrays]
    scratch = []
    for array, full, _, _, cols in pieces:
        block = (arrays[array].shape[-2], cols)
        dtype = arrays[array].dtype
        if full:
            for stage in range(-1, cube.dp_bits):
                lead = (2,) * (cube.dp_bits - 1 - max(stage, 0)) + (cube.n_seq,)
                scratch.append(pltpu.VMEM(lead + block, dtype))
        else:
            scratch.append(pltpu.VMEM((cube.n_seq,) + block, dtype))
        scratch.append(pltpu.VMEM((cube.n_seq + 1,) + block, dtype))
    slots = 2 * cube.n_seq + cube.dp_bits
    scratch += [
        pltpu.SemaphoreType.DMA((len(pieces), slots)),
        pltpu.SemaphoreType.DMA((len(pieces), slots)),
        pltpu.SemaphoreType.DMA((len(pieces),)),
    ]
    return pl.pallas_call(
        functools.partial(scatter_kernel, cube, pieces),
        out_shape=outs,
        in_specs=[pl.BlockSpec(memory_space=pl.ANY)] * len(arrays),
        out_specs=[pl.BlockSpec(memory_space=pltpu.VMEM)] * len(arrays),
        scratch_shapes=scratch,
        compiler_params=pltpu.CompilerParams(
            collective_id=collective_id,
            has_side_effects=True,
            vmem_limit_bytes=60 * 1024 * 1024,
        ),
        name="scatter_grads",
    )(*arrays)


def head_slice(array, group_index, group_size):
    part = lax.dynamic_slice_in_dim(array, group_index * group_size * DH, group_size * DH, 2)
    return part.reshape(array.shape[0], array.shape[1], group_size, DH)


def regroup(stacked):
    group_count, seq_count, row_count, group_span = stacked.shape
    return jnp.moveaxis(stacked, 0, 2).reshape(seq_count, row_count, group_count * group_span)


def masked_scores(query_part, key_part, allow):
    scores = jnp.einsum("sqhd,skhd->shqk", query_part, key_part, preferred_element_type=F32)
    if allow is not None:
        scores = jnp.where(allow[:, None], scores, NEG)
    return scores


def attn_forward(queries, keys, values, allow):
    group_size = math.gcd(H, 4)

    def one_group(group_index):
        query_part = head_slice(queries, group_index, group_size)
        key_part = head_slice(keys, group_index, group_size)
        value_part = head_slice(values, group_index, group_size)
        scores = masked_scores(query_part, key_part, allow)
        row_max = jnp.max(scores, axis=-1, keepdims=True)
        expon = jnp.exp(scores - row_max)
        row_total = jnp.sum(expon, axis=-1, keepdims=True)
        probab = (expon / row_total).astype(BF)
        attended = jnp.einsum("shqk,skhd->sqhd", probab, value_part, preferred_element_type=F32)
        attended = attended.reshape(queries.shape[0], queries.shape[1], group_size * DH)
        return (attended, (row_max + jnp.log(row_total))[..., 0])

    stacked, log_sums = lax.map(one_group, jnp.arange(H // group_size, dtype=jnp.int32))
    return (regroup(stacked), log_sums)


def attn_backward(queries, keys, values, allow, log_sums, grad_attended):
    group_size = math.gcd(H, 4)

    def one_group(items):
        group_index, log_part = items
        query_part = head_slice(queries, group_index, group_size)
        key_part = head_slice(keys, group_index, group_size)
        value_part = head_slice(values, group_index, group_size)
        grad_part = head_slice(grad_attended, group_index, group_size)
        scores = masked_scores(query_part, key_part, allow)
        probab = jnp.exp(scores - log_part[..., None])
        grad_probs = jnp.einsum("sqhd,skhd->shqk", grad_part, value_part, preferred_element_type=F32)
        row_delta = jnp.sum(probab * grad_probs, axis=-1, keepdims=True)
        grad_scores = (probab * (grad_probs - row_delta)).astype(BF)
        grad_query = jnp.einsum("shqk,skhd->sqhd", grad_scores, key_part, preferred_element_type=F32)
        grad_key = jnp.einsum("shqk,sqhd->skhd", grad_scores, query_part, preferred_element_type=F32)
        grad_value = jnp.einsum(
            "shqk,sqhd->skhd", probab.astype(BF), grad_part, preferred_element_type=F32
        )
        seq_count = queries.shape[0]
        return (
            grad_query.reshape(seq_count, queries.shape[1], group_size * DH),
            grad_key.reshape(seq_count, keys.shape[1], group_size * DH),
            grad_value.reshape(seq_count, keys.shape[1], group_size * DH),
        )

    group_ids = jnp.arange(H // group_size, dtype=jnp.int32)
    grad_queries, grad_keys, grad_values = lax.map(one_group, (group_ids, log_sums))
    return (regroup(grad_queries), regroup(grad_keys), regroup(grad_values))


WIDE = 13


def local(
    cube,
    tokens,
    encoded,
    cotangent,
    doc_ids,
    block_ids,
    query_weight,
    key_weight,
    value_weight,
    out_weight,
    query_bias,
    value_bias,
    out_bias,
    first_gain,
    first_shift,
    probe_weight,
    lookup_weight,
    content_weight,
    merge_weight,
    probe_bias,
    content_bias,
    merge_bias,
    second_gain,
    second_shift,
    expand_weight,
    expand_bias,
    reduce_weight,
    reduce_bias,
    third_gain,
    third_shift,
):
    seq_count, local_rows, feat_width = tokens.shape
    assert seq_count == 1
    enc_local = encoded.shape[1]
    scale = DH ** (-0.5)
    flat = tokens.reshape(local_rows, feat_width)
    enc_flat = encoded.reshape(enc_local, feat_width)

    weights = [
        query_weight, key_weight, value_weight, out_weight, probe_weight,
        lookup_weight, content_weight, merge_weight, expand_weight, reduce_weight,
    ]
    vectors = [
        query_bias, value_bias, out_bias, first_gain, first_shift, probe_bias, content_bias,
        merge_bias, second_gain, second_shift, reduce_bias, third_gain, third_shift,
    ]
    part = vectors[0].shape[0]
    long_part = expand_bias.shape[0]
    held = WIDE * part + long_part
    padded = -(-held // 1024) * 1024
    vec_block = (8, padded // 8)
    packed = jnp.concatenate(vectors + [expand_bias, jnp.zeros((padded - held,), F32)])
    blocks = [w.astype(BF).reshape(block_shape(*w.shape)) for w in weights]
    kinds = [False, False] + [True] * (len(blocks) + 1)
    gathered = gather_all(
        cube, [flat, enc_flat] + blocks + [packed.reshape(vec_block)], kinds, 0
    )
    n_dev = cube.n_dev
    tok_all = gathered[0].reshape(cube.n_seq * local_rows, feat_width)
    enc_all = gathered[1].reshape(cube.n_seq * enc_local, feat_width)
    (
        query_mat, key_mat, value_mat, out_mat, probe_mat,
        lookup_mat, content_mat, merge_mat, expand_mat, reduce_mat,
    ) = [
        g.reshape(w.shape[0] * n_dev, w.shape[1]) for g, w in zip(gathered[2:12], weights)
    ]
    vec_all = gathered[12].reshape(n_dev, padded)
    wide_all = (
        vec_all[:, : WIDE * part].reshape(n_dev, WIDE, part).transpose(1, 0, 2).reshape(WIDE, -1)
    )
    (
        query_vec, value_vec, out_vec, gain_first, shift_first, probe_vec, content_vec,
        merge_vec, gain_second, shift_second, reduce_vec, gain_third, shift_third,
    ) = [wide_all[i] for i in range(WIDE)]
    expand_vec = vec_all[:, WIDE * part : held].reshape(-1)

    offset = lax.axis_index("seq") * local_rows
    query_doc = lax.dynamic_slice_in_dim(doc_ids, offset, local_rows, 1)
    query_block = lax.dynamic_slice_in_dim(block_ids, offset, local_rows, 1)
    allow = (query_doc[:, :, None] == doc_ids[:, None, :]) & (
        block_ids[:, None, :] <= query_block[:, :, None]
    )
    token_float = flat.astype(F32)
    queries = ((matmul(flat, query_mat) + query_vec) * scale).astype(BF)
    all_keys = matmul(tok_all, key_mat).astype(BF)
    all_values = (matmul(tok_all, value_mat) + value_vec).astype(BF)
    self_out, self_logs = attn_forward(queries[None], all_keys[None], all_values[None], allow)
    self_outb = self_out[0].astype(BF)
    first_sum = token_float + matmul(self_outb, out_mat) + out_vec
    normed_one, inv_one = layer_stats(first_sum)
    stream_one = (normed_one * gain_first + shift_first).astype(BF)
    probe = ((matmul(stream_one, probe_mat) + probe_vec) * scale).astype(BF)
    enc_keys = matmul(enc_all, lookup_mat).astype(BF)
    enc_values = (matmul(enc_all, content_mat) + content_vec).astype(BF)
    cross_out, cross_logs = attn_forward(probe[None], enc_keys[None], enc_values[None], None)
    cross_outb = cross_out[0].astype(BF)
    second_sum = stream_one.astype(F32) + matmul(cross_outb, merge_mat) + merge_vec
    normed_two, inv_two = layer_stats(second_sum)
    stream_two = (normed_two * gain_second + shift_second).astype(BF)
    expanded = matmul(stream_two, expand_mat) + expand_vec
    activated = jax.nn.gelu(expanded, approximate=False).astype(BF)
    third_sum = stream_two.astype(F32) + matmul(activated, reduce_mat) + reduce_vec
    normed_three, inv_three = layer_stats(third_sum)
    output = (normed_three * gain_third + shift_third).astype(BF)

    grad_output = cotangent.reshape(local_rows, feat_width).astype(F32)
    g_shift_third = jnp.sum(grad_output, axis=0)
    g_gain_third = jnp.sum(grad_output * normed_three, axis=0)
    grad_three = layer_back(grad_output * gain_third, normed_three, inv_three)
    reduce_rows = grad_three.astype(BF)
    g_reduce_vec = jnp.sum(grad_three, axis=0)
    g_reduce_mat = left_outer(activated, reduce_rows)
    grad_act = right_trans(reduce_rows, reduce_mat)
    slope = 0.5 * (
        1.0 + jax.scipy.special.erf(expanded * INV_ROOT_TWO)
    ) + expanded * DENSITY_CONST * jnp.exp(-0.5 * expanded * expanded)
    grad_expanded = grad_act * slope
    g_expand_vec = jnp.sum(grad_expanded, axis=0)
    expand_rows = grad_expanded.astype(BF)
    g_expand_mat = left_outer(stream_two, expand_rows)

    def spread(grad, weight):
        return grad.astype(BF).reshape(cube.lead(True) + block_shape(*weight.shape))

    expand_sum, reduce_sum = scatter_all(
        cube,
        [spread(g_reduce_mat, reduce_weight), spread(g_expand_mat, expand_weight)],
        [True, True],
        1,
    )[::-1]

    grad_two = grad_three + right_trans(expand_rows, expand_mat)
    g_shift_second = jnp.sum(grad_two, axis=0)
    g_gain_second = jnp.sum(grad_two * normed_two, axis=0)
    grad_second = layer_back(grad_two * gain_second, normed_two, inv_two)
    merge_rows = grad_second.astype(BF)
    g_merge_vec = jnp.sum(grad_second, axis=0)
    g_merge_mat = left_outer(cross_outb, merge_rows)
    grad_cross = right_trans(merge_rows, merge_mat).astype(BF)
    grad_probe, grad_enc_keys, grad_enc_values = attn_backward(
        probe[None], enc_keys[None], enc_values[None], None, cross_logs, grad_cross[None]
    )
    probe_rows = (grad_probe[0].astype(BF).astype(F32) * scale).astype(BF)
    g_probe_vec = jnp.sum(probe_rows.astype(F32), axis=0)
    g_probe_mat = left_outer(stream_one, probe_rows)
    enc_key_rows = grad_enc_keys[0].astype(BF)
    enc_value_rows = grad_enc_values[0].astype(BF)
    g_lookup_mat = left_outer(enc_all, enc_key_rows)
    g_content_mat = left_outer(enc_all, enc_value_rows)
    g_content_vec = jnp.sum(grad_enc_values[0], axis=0)
    enc_part = right_trans(enc_key_rows, lookup_mat) + right_trans(enc_value_rows, content_mat)
    grad_one = grad_second + right_trans(probe_rows, probe_mat)
    g_shift_first = jnp.sum(grad_one, axis=0)
    g_gain_first = jnp.sum(grad_one * normed_one, axis=0)
    grad_first = layer_back(grad_one * gain_first, normed_one, inv_one)
    out_rows = grad_first.astype(BF)
    g_out_vec = jnp.sum(grad_first, axis=0)
    g_out_mat = left_outer(self_outb, out_rows)
    grad_self = right_trans(out_rows, out_mat).astype(BF)
    grad_query, grad_keys, grad_values = attn_backward(
        queries[None], all_keys[None], all_values[None], allow, self_logs, grad_self[None]
    )
    query_rows = (grad_query[0].astype(BF).astype(F32) * scale).astype(BF)
    key_rows = grad_keys[0].astype(BF)
    value_rows = grad_values[0].astype(BF)
    g_query_vec = jnp.sum(query_rows.astype(F32), axis=0)
    g_value_vec = jnp.sum(grad_values[0], axis=0)
    g_query_mat = left_outer(flat, query_rows)
    g_key_mat = left_outer(tok_all, key_rows)
    g_value_mat = left_outer(tok_all, value_rows)
    tok_part = right_trans(key_rows, key_mat) + right_trans(value_rows, value_mat)
    tok_own = grad_first + right_trans(query_rows, query_mat)

    wide_grads = jnp.stack(
        [
            g_query_vec, g_value_vec, g_out_vec, g_gain_first, g_shift_first, g_probe_vec, g_content_vec,
            g_merge_vec, g_gain_second, g_shift_second, g_reduce_vec, g_gain_third, g_shift_third,
        ]
    )
    vec_grads = jnp.concatenate(
        [
            wide_grads.reshape(WIDE, n_dev, part).transpose(1, 0, 2).reshape(n_dev, WIDE * part),
            g_expand_vec.reshape(n_dev, long_part),
            jnp.zeros((n_dev, padded - held), F32),
        ],
        axis=1,
    ).reshape(cube.lead(True) + vec_block)
    mats = [
        g_merge_mat, g_probe_mat, g_lookup_mat, g_content_mat, g_out_mat,
        g_query_mat, g_key_mat, g_value_mat,
    ]
    shards = [
        merge_weight, probe_weight, lookup_weight, content_weight, out_weight,
        query_weight, key_weight, value_weight,
    ]
    sums = scatter_all(
        cube,
        [
            enc_part.astype(BF).reshape(cube.n_seq, enc_local, feat_width),
            tok_part.astype(BF).reshape(cube.n_seq, local_rows, feat_width),
        ]
        + [spread(g, w) for g, w in zip(mats, shards)]
        + [vec_grads],
        [False, False] + [True] * (len(mats) + 1),
        2,
    )
    encoded_grad = sums[0]
    tokens_grad = tok_own + sums[1]
    (
        merge_sum, probe_sum, lookup_sum, content_sum, out_sum, query_sum, key_sum, value_sum,
    ) = [s.reshape(w.shape) for s, w in zip(sums[2:10], shards)]
    expand_sum = expand_sum.reshape(expand_weight.shape)
    reduce_sum = reduce_sum.reshape(reduce_weight.shape)
    vec_sum = sums[10].reshape(padded)
    (
        query_vs, value_vs, out_vs, gain1_vs, shift1_vs, probe_vs, content_vs,
        merge_vs, gain2_vs, shift2_vs, reduce_vs, gain3_vs, shift3_vs,
    ) = [vec_sum[i * part : (i + 1) * part] for i in range(WIDE)]
    expand_vs = vec_sum[WIDE * part : held]
    return (
        output[None],
        tokens_grad[None],
        encoded_grad[None],
        query_sum,
        key_sum,
        value_sum,
        out_sum,
        query_vs,
        value_vs,
        out_vs,
        gain1_vs,
        shift1_vs,
        probe_sum,
        lookup_sum,
        content_sum,
        merge_sum,
        probe_vs,
        content_vs,
        merge_vs,
        gain2_vs,
        shift2_vs,
        expand_sum,
        expand_vs,
        reduce_sum,
        reduce_vs,
        gain3_vs,
        shift3_vs,
    )


def solution(mesh):
    rows = P("dp", "seq", None)
    ids = P("dp", None)
    mat = P(("dp", "seq"), None)
    vec = P(("dp", "seq"))
    return jax.shard_map(
        functools.partial(local, Cube(mesh)),
        mesh=mesh,
        in_specs=(
            (rows, rows, rows, ids, ids)
            + (mat, mat, mat, mat, vec, vec, vec, vec, vec)
            + (mat, mat, mat, mat, vec, vec, vec, vec, vec)
            + (mat, vec, mat, vec, vec, vec)
        ),
        out_specs=(
            (rows, rows, rows)
            + (mat, mat, mat, mat, vec, vec, vec, vec, vec)
            + (mat, mat, mat, mat, vec, vec, vec, vec, vec)
            + (mat, vec, mat, vec, vec, vec)
        ),
        check_vma=False,
    )
```

```python
import functools
import itertools
import math

import jax
import jax.numpy as jnp
from jax import lax
from jax.experimental import pallas as pl
from jax.experimental.pallas import tpu as pltpu
from jax.sharding import PartitionSpec as P

H = 16
DH = 64

EPS = 1e-05
NEG = -1000000000.0
INV_ROOT_TWO = 0.7071067811865476
DENSITY_CONST = 0.3989422804014327
MESH = pl.DeviceIdType.MESH
PIECE = 16384
BF = jnp.bfloat16
F32 = jnp.float32


def matmul(left_arg, right_arg):
    return jnp.dot(left_arg, right_arg, preferred_element_type=F32)


def left_outer(left_arg, right_arg):
    return lax.dot_general(
        left_arg, right_arg, (((0,), (0,)), ((), ())), preferred_element_type=F32
    )


def right_trans(left_arg, right_arg):
    return lax.dot_general(
        left_arg, right_arg, (((1,), (1,)), ((), ())), preferred_element_type=F32
    )


def layer_stats(hidden):
    row_mean = jnp.mean(hidden, axis=-1, keepdims=True)
    centered = hidden - row_mean
    inv_std = lax.rsqrt(jnp.mean(centered * centered, axis=-1, keepdims=True) + EPS)
    return (centered * inv_std, inv_std)


def layer_back(grad_norm, normed, inv_std):
    first_mean = jnp.mean(grad_norm, axis=-1, keepdims=True)
    second_mean = jnp.mean(grad_norm * normed, axis=-1, keepdims=True)
    return inv_std * (grad_norm - first_mean - normed * second_mean)


class Cube:
    def __init__(self, mesh):
        self.n_dp = mesh.shape["dp"]
        self.n_seq = mesh.shape["seq"]
        self.dp_bits = self.n_dp.bit_length() - 1
        assert self.n_dp == 1 << self.dp_bits
        self.n_dev = self.n_dp * self.n_seq

    def lead(self, full):
        return ((2,) * self.dp_bits if full else ()) + (self.n_seq,)


class Place:
    def __init__(self, cube):
        self.dp, self.seq = lax.axis_index("dp"), lax.axis_index("seq")
        self.bits, self.flips = [], []
        rest = self.dp
        for bit in range(cube.dp_bits):
            half = rest // 2
            self.bits.append(rest - 2 * half)
            self.flips.append(self.dp + (1 << bit) * (1 - 2 * self.bits[-1]))
            rest = half


def block_shape(rows, cols):
    if rows % 16 == 0:
        return (rows, cols)
    return (16, rows * cols // 16)


def dim_order(cube, variant):
    bits = list(range(1, cube.dp_bits))
    return bits if variant == 0 else bits[::-1]


def meet(cube, here):
    dp, seq = here.dp, here.seq
    barrier = pltpu.get_barrier_semaphore()

    def greet(device):
        pl.semaphore_signal(barrier, inc=1, device_id=device, device_id_type=MESH)

    for bit in range(cube.dp_bits):
        greet((here.flips[bit], seq))
    greet((dp, lax.rem(seq + 1, cube.n_seq)))
    greet((dp, lax.rem(seq + cube.n_seq - 1, cube.n_seq)))
    pl.semaphore_wait(barrier, cube.dp_bits + 2)


def in_slots(pieces, lag):
    depth = max(len(stages) for stages in pieces)
    for slot in range(len(pieces) + lag * (depth - 1)):
        for k in reversed(range(depth)):
            p = slot - lag * k
            if 0 <= p < len(pieces) and k < len(pieces[p]):
                pieces[p][k]()


def remote(source, target, send_sem, recv_sem, device):
    return pltpu.make_async_remote_copy(
        src_ref=source,
        dst_ref=target,
        send_sem=send_sem,
        recv_sem=recv_sem,
        device_id=device,
        device_id_type=MESH,
    )


def gather_stages(cube, here, full, variant, source, target, send_sem, recv_sem, local_sem):
    dp, seq = here.dp, here.seq
    n = cube.n_seq
    order = dim_order(cube, variant)
    every = pl.ds(0, n)
    waits = []

    def region(open_bits, fixed, seq_part):
        if not full:
            return (seq_part,)
        places = []
        for bit in reversed(range(cube.dp_bits)):
            if bit in open_bits:
                places.append(slice(None))
            else:
                places.append(fixed.get(bit, here.bits[bit]))
        return tuple(places) + (seq_part,)

    def move(place, slot, device):
        at = target.at[place]
        return remote(at, at, send_sem.at[slot], recv_sem.at[slot], device)

    own = pltpu.make_async_copy(source, target.at[region((), {}, seq)], local_sem)

    def line(step, way):
        slot = 2 * step + (1 if way > 0 else 0)
        block = seq - way * step
        inside = (seq + way >= 0) & (seq + way < n)
        sends = inside & (block >= 0) & (block < n)
        copy = lambda: move(region((), {}, block), slot, (dp, seq + way))
        came = seq - way * (step + 1)
        gets = (came >= 0) & (came < n)
        arrival = lambda: move(region((), {}, came), slot, (dp, seq - way))
        return sends, copy, gets, arrival

    def line_start(step):
        for way in (1, -1):
            sends, copy, _, _ = line(step, way)
            pl.when(sends)(lambda: copy().start())
            waits.append((sends, copy))

    def line_wait(step):
        for way in (1, -1):
            _, _, gets, arrival = line(step, way)
            pl.when(gets)(lambda: arrival().wait_recv())

    base = 2 * (n - 1)
    cores, arrivals = [], []

    def dims_start(stage):
        if stage < len(order):
            copy = move(
                region(order[:stage], {}, every), base + 2 * stage, (here.flips[order[stage]], seq)
            )
            copy.start()
            waits.append((None, copy))
            arrivals.append(copy)
        if stage == 0:
            fresh = region((), {}, every)
        else:
            last = order[stage - 1]
            fresh = region(order[: stage - 1], {last: 1 - here.bits[last]}, every)
        copy = move(fresh, base + 2 * stage + 1, (here.flips[0], seq))
        copy.start()
        waits.append((None, copy))
        cores.append(copy)

    def first():
        own.wait()
        line_start(0)

    stages = [first]
    for step in range(n - 1):

        def after_line(step=step):
            line_wait(step)
            if step < n - 2:
                line_start(step + 1)
            elif full:
                dims_start(0)

        stages.append(after_line)
    if full:
        for stage in range(len(order)):

            def after_dims(stage=stage):
                arrivals[stage].wait_recv()
                dims_start(stage + 1)

            stages.append(after_dims)

        def last():
            for copy in cores:
                copy.wait_recv()

        stages.append(last)

    def finish():
        for sends, copy in waits:
            if sends is None:
                copy.wait_send()
            else:
                pl.when(sends)(lambda: copy().wait_send())

    return own, stages, finish


def gather_slots(cube):
    return 2 * (cube.n_seq - 1) + 2 * cube.dp_bits


def gather_kernel(cube, pieces, *refs):
    count = 1 + max(piece[0] for piece in pieces)
    ins, outs = refs[:count], refs[count : 2 * count]
    send_sem, recv_sem, local_sem = refs[2 * count :]
    here = Place(cube)
    plans = []
    for index, (array, full, variant, col, cols) in enumerate(pieces):
        lead = cube.dp_bits * full + 1
        cut = (slice(None), pl.ds(col, cols))
        plans.append(
            gather_stages(
                cube,
                here,
                full,
                variant,
                ins[array].at[cut],
                outs[array].at[(slice(None),) * lead + cut],
                send_sem.at[index],
                recv_sem.at[index],
                local_sem.at[index],
            )
        )
    for own, _, _ in plans:
        own.start()
    meet(cube, here)
    in_slots([stages for _, stages, _ in plans], 3)
    for _, _, finish in plans:
        finish()


def cut_columns(kinds, arrays):
    whole, along = [], []
    for index, (full, array) in enumerate(zip(kinds, arrays)):
        cols = array.shape[-1]
        count = max(1, math.prod(array.shape[-2:]) // (PIECE if full else PIECE))
        while cols % (128 * count):
            count //= 2
        width = cols // count
        for i in range(count):
            if full:
                whole.append((index, True, len(whole) % 2, width * i, width))
            else:
                along.append((index, False, 0, width * i, width))
    placed = [((i + 0.5) / len(whole), 0, piece) for i, piece in enumerate(whole)]
    placed += [((i + 0.5) / len(along), 1, piece) for i, piece in enumerate(along)]
    return tuple(piece for _, _, piece in sorted(placed, key=lambda item: item[:2]))


def gather_all(cube, arrays, kinds, collective_id):
    pieces = cut_columns(kinds, arrays)
    outs = [
        jax.ShapeDtypeStruct(cube.lead(full) + array.shape, array.dtype)
        for array, full in zip(arrays, kinds)
    ]
    slots = gather_slots(cube)
    return pl.pallas_call(
        functools.partial(gather_kernel, cube, pieces),
        out_shape=outs,
        in_specs=[pl.BlockSpec(memory_space=pl.ANY)] * len(arrays),
        out_specs=[pl.BlockSpec(memory_space=pl.ANY)] * len(arrays),
        scratch_shapes=[
            pltpu.SemaphoreType.DMA((len(pieces), slots)),
            pltpu.SemaphoreType.DMA((len(pieces), slots)),
            pltpu.SemaphoreType.DMA((len(pieces),)),
        ],
        compiler_params=pltpu.CompilerParams(
            collective_id=collective_id, has_side_effects=True
        ),
        name="gather_weights",
    )(*arrays)


def add_block(total, part):
    total[...] = (total[...].astype(F32) + part[...].astype(F32)).astype(total.dtype)


def add_rows(pairs, count, rows, cols):
    step = rows
    while step * cols > 32768 and step % 32 == 0:
        step //= 2

    def body(index, carry):
        for total, part in pairs:
            for row in range(0, rows, step):
                at = (index, pl.ds(row, step))
                add_block(total.at[at], part.at[at])
        return carry

    lax.fori_loop(0, count, body, 0)


def scatter_stages(
    cube, here, full, variant, source, out, own, parts, send_sem, recv_sem, local_sem
):
    dp, seq = here.dp, here.seq
    n = cube.n_seq
    order = dim_order(cube, variant) if full else []
    rows, cols = out.shape
    line_part = parts[-1]
    waits = []
    arrivals = []

    def dims(fixed, kept):
        return tuple(
            fixed[bit] if bit in fixed else kept for bit in reversed(range(1, cube.dp_bits))
        )

    mine = {bit: here.bits[bit] for bit in range(1, cube.dp_bits)}
    settled = dims(mine, None) if full else ()
    lead = (slice(None),) * (cube.dp_bits - 1)
    kept = source.at[lead + (here.bits[0],)] if full else source
    local = pltpu.make_async_copy(kept, own, local_sem)

    def push(stage, what, device):
        copy = remote(what, parts[stage], send_sem.at[stage], recv_sem.at[stage], device)
        copy.start()
        waits.append((None, copy))
        arrivals.append(copy)

    base = cube.dp_bits if full else 0

    def line(step, way):
        target = seq + way * (n - 1 - step)
        passes = (target >= 0) & (target < n)
        further = passes & ((seq > 0) if way > 0 else (seq < n - 1))
        slot = n if way < 0 and step == n - 2 else target
        block = own.at[settled + (target,)]
        index = base + 2 * step + (1 if way > 0 else 0)

        def copy():
            return remote(
                block, line_part.at[slot], send_sem.at[index], recv_sem.at[index], (dp, seq + way)
            )

        def arrival():
            at = line_part.at[target]
            return remote(at, at, send_sem.at[index - 2], recv_sem.at[index - 2], (dp, seq - way))

        return target, passes, further, copy, arrival

    def line_step(step):
        for way in (1, -1):
            target, passes, further, copy, arrival = line(step, way)
            if step > 0:

                @pl.when(further)
                def _():
                    arrival().wait_recv()
                    to, of = own.at[settled + (pl.ds(target, 1),)], line_part.at[pl.ds(target, 1)]
                    add_rows([(to, of)], 1, rows, cols)

            pl.when(passes)(lambda: copy().start())
            waits.append((passes, copy))

    def start():
        local.start()
        if full:
            push(0, source.at[lead + (1 - here.bits[0],)], (here.flips[0], seq))

    def after_dims(stage):
        if stage == 0:
            local.wait()
        arrivals[stage].wait_recv()
        closed = order[:stage]
        fixed = {bit: mine[bit] for bit in closed}
        open_bits = [bit for bit in reversed(range(1, cube.dp_bits)) if bit not in closed]

        pairs = []
        for values in itertools.product((0, 1), repeat=len(open_bits)):
            to = dims({**fixed, **dict(zip(open_bits, values))}, None)
            pairs.append((own.at[to], parts[stage].at[values]))
        add_rows(pairs, n, rows, cols)
        if stage < len(order):
            bit = order[stage]
            at = dims({**fixed, bit: 1 - mine[bit]}, slice(None)) + (pl.ds(0, n),)
            push(stage + 1, own.at[at], (here.flips[bit], seq))
        else:
            line_step(0)

    def last():
        where = settled + (seq,)

        def sem(way):
            return recv_sem.at[base + 2 * (n - 2) + (1 if way > 0 else 0)]

        @pl.when(seq > 0)
        def _():
            at = line_part.at[seq]
            remote(at, at, send_sem.at[base], sem(1), (dp, seq - 1)).wait_recv()

        @pl.when(seq < n - 1)
        def _():
            at = line_part.at[n]
            remote(at, at, send_sem.at[base], sem(-1), (dp, seq + 1)).wait_recv()

        @pl.when(seq == 0)
        def _():
            out[...] = own[where].astype(F32) + line_part[n].astype(F32)

        @pl.when(seq == n - 1)
        def _():
            out[...] = own[where].astype(F32) + line_part[n - 1].astype(F32)

        @pl.when((seq > 0) & (seq < n - 1))
        def _():
            both = line_part[seq].astype(F32) + line_part[n].astype(F32)
            out[...] = own[where].astype(F32) + both

    stages = [start]
    if full:
        stages += [functools.partial(after_dims, stage) for stage in range(cube.dp_bits)]
    else:

        def begin():
            local.wait()
            line_step(0)

        stages.append(begin)
    stages += [functools.partial(line_step, step) for step in range(1, n - 1)]
    stages.append(last)

    def finish():
        for passes, copy in waits:
            if passes is None:
                copy.wait_send()
            else:
                pl.when(passes)(lambda: copy().wait_send())

    return stages, finish


def scatter_kernel(cube, pieces, *refs):
    count = 1 + max(piece[0] for piece in pieces)
    ins, outs = refs[:count], refs[count : 2 * count]
    refs = refs[2 * count :]
    send_sem, recv_sem, local_sem = refs[-3:]
    here = Place(cube)
    plans = []
    for index, (array, full, variant, col, cols) in enumerate(pieces):
        held = 2 + (cube.dp_bits if full else 0)
        cut = (slice(None), pl.ds(col, cols))
        plans.append(
            scatter_stages(
                cube,
                here,
                full,
                variant,
                ins[array].at[(slice(None),) * (cube.dp_bits * full + 1) + cut],
                outs[array].at[cut],
                refs[0],
                refs[1:held],
                send_sem.at[index],
                recv_sem.at[index],
                local_sem.at[index],
            )
        )
        refs = refs[held:]
    meet(cube, here)
    in_slots([stages for stages, _ in plans], 4)
    for _, finish in plans:
        finish()


def scatter_all(cube, arrays, kinds, collective_id):
    pieces = cut_columns(kinds, arrays)
    outs = [jax.ShapeDtypeStruct(array.shape[-2:], F32) for array in arrays]
    scratch = []
    for array, full, _, _, cols in pieces:
        block = (arrays[array].shape[-2], cols)
        dtype = arrays[array].dtype
        if full:
            for stage in range(-1, cube.dp_bits):
                lead = (2,) * (cube.dp_bits - 1 - max(stage, 0)) + (cube.n_seq,)
                scratch.append(pltpu.VMEM(lead + block, dtype))
        else:
            scratch.append(pltpu.VMEM((cube.n_seq,) + block, dtype))
        scratch.append(pltpu.VMEM((cube.n_seq + 1,) + block, dtype))
    slots = 2 * cube.n_seq + cube.dp_bits
    scratch += [
        pltpu.SemaphoreType.DMA((len(pieces), slots)),
        pltpu.SemaphoreType.DMA((len(pieces), slots)),
        pltpu.SemaphoreType.DMA((len(pieces),)),
    ]
    return pl.pallas_call(
        functools.partial(scatter_kernel, cube, pieces),
        out_shape=outs,
        in_specs=[pl.BlockSpec(memory_space=pl.ANY)] * len(arrays),
        out_specs=[pl.BlockSpec(memory_space=pltpu.VMEM)] * len(arrays),
        scratch_shapes=scratch,
        compiler_params=pltpu.CompilerParams(
            collective_id=collective_id,
            has_side_effects=True,
            vmem_limit_bytes=60 * 1024 * 1024,
        ),
        name="scatter_grads",
    )(*arrays)


def write_bias(bias, key_ids, query_ids):
    same = key_ids[:, 0:1] == query_ids[0:1, :]
    early = key_ids[:, 1:2] <= query_ids[1:2, :]
    bias[...] = jnp.where(same & early, 0.0, NEG)


def one_head(array, head):
    lane = lax.broadcasted_iota(jnp.int32, array.shape, 1)
    keep = (lane < DH) if head == 0 else (lane >= DH)
    return jnp.where(keep, array, jnp.zeros_like(array))


def attend_kernel(masked, *refs):
    if masked:
        key_ids, query_ids, query_ref, key_ref, value_ref, out_ref, log_ref, bias = refs
        pl.when(pl.program_id(0) == 0)(lambda: write_bias(bias, key_ids[...], query_ids[...]))
    else:
        query_ref, key_ref, value_ref, out_ref, log_ref = refs
    query, key = query_ref[...], key_ref[...]
    value_t = value_ref[...].T
    outs, logs = [], []
    for head in range(2):
        scores = right_trans(key, one_head(query, head))
        if masked:
            scores = scores + bias[...]
        top = jnp.max(scores, axis=0, keepdims=True)
        expon = jnp.exp(scores - top)
        total = jnp.sum(expon, axis=0, keepdims=True)
        got = matmul(value_t[head * DH : (head + 1) * DH], expon.astype(BF))
        outs.append(got * (1.0 / total))
        logs.append(top + jnp.log(total))
    out_ref[...] = jnp.concatenate(outs, axis=0).T.astype(BF)
    log_ref[0] = jnp.concatenate(logs, axis=0)


def attend_back_kernel(masked, *refs):
    if masked:
        key_ids, query_ids, query_ref, key_ref, value_ref, grad_ref, log_ref = refs[:7]
        dq_ref, dk_ref, dv_ref, bias = refs[7:]
        pl.when(pl.program_id(0) == 0)(lambda: write_bias(bias, key_ids[...], query_ids[...]))
    else:
        query_ref, key_ref, value_ref, grad_ref, log_ref, dq_ref, dk_ref, dv_ref = refs
    query, key, value, grad = query_ref[...], key_ref[...], value_ref[...], grad_ref[...]
    key_t = key.T
    dq, dk, dv = [], None, None
    for head in range(2):
        query_head, grad_head = one_head(query, head), one_head(grad, head)
        scores = right_trans(key, query_head)
        if masked:
            scores = scores + bias[...]
        probs = jnp.exp(scores - log_ref[0, head : head + 1, :])
        grad_probs = right_trans(value, grad_head)
        delta = jnp.sum(probs * grad_probs, axis=0, keepdims=True)
        grad_scores = (probs * (grad_probs - delta)).astype(BF)
        dq.append(matmul(key_t[head * DH : (head + 1) * DH], grad_scores))
        dk_head = matmul(grad_scores, query_head)
        dv_head = matmul(probs.astype(BF), grad_head)
        dk = dk_head if dk is None else dk + dk_head
        dv = dv_head if dv is None else dv + dv_head
    scale = DH ** (-0.5)
    dq_ref[...] = (jnp.concatenate(dq, axis=0).T.astype(BF).astype(F32) * scale).astype(BF)
    dk_ref[...] = dk.astype(BF)
    dv_ref[...] = dv.astype(BF)


def attend_call(back, ids, arrays):
    rows, width = arrays[0].shape
    keys = arrays[1].shape[0]
    pair = 2 * DH
    steps = width // pair
    masked = ids is not None
    by_query = pl.BlockSpec((rows, pair), lambda i: (0, i))
    by_key = pl.BlockSpec((keys, pair), lambda i: (0, i))
    logs = pl.BlockSpec((1, 2, rows), lambda i: (i, 0, 0))
    in_specs = [by_query, by_key, by_key]
    if masked:
        in_specs = [
            pl.BlockSpec((keys, 2), lambda i: (0, 0)),
            pl.BlockSpec((2, rows), lambda i: (0, 0)),
        ] + in_specs
        arrays = list(ids) + list(arrays)
    log_shape = jax.ShapeDtypeStruct((steps, 2, rows), F32)
    query_shape = jax.ShapeDtypeStruct((rows, width), BF)
    key_shape = jax.ShapeDtypeStruct((keys, width), BF)
    if back:
        in_specs += [by_query, logs]
        out_specs, out_shape = [by_query, by_key, by_key], [query_shape, key_shape, key_shape]
    else:
        out_specs, out_shape = [by_query, logs], [query_shape, log_shape]
    products = 7 if back else 2
    return pl.pallas_call(
        functools.partial(attend_back_kernel if back else attend_kernel, masked),
        grid=(steps,),
        in_specs=in_specs,
        out_specs=out_specs,
        out_shape=out_shape,
        scratch_shapes=[pltpu.VMEM((keys, rows), F32)] if masked else [],
        cost_estimate=pl.CostEstimate(
            flops=2 * products * rows * keys * width,
            bytes_accessed=2 * width * (rows + keys) * products,
            transcendentals=rows * keys * width // DH,
        ),
        compiler_params=pltpu.CompilerParams(vmem_limit_bytes=48 * 1024 * 1024),
        name="attend_back" if back else "attend",
    )(*arrays)


WIDE = 13


def local(
    cube,
    tokens,
    encoded,
    cotangent,
    doc_ids,
    block_ids,
    query_weight,
    key_weight,
    value_weight,
    out_weight,
    query_bias,
    value_bias,
    out_bias,
    first_gain,
    first_shift,
    probe_weight,
    lookup_weight,
    content_weight,
    merge_weight,
    probe_bias,
    content_bias,
    merge_bias,
    second_gain,
    second_shift,
    expand_weight,
    expand_bias,
    reduce_weight,
    reduce_bias,
    third_gain,
    third_shift,
):
    seq_count, local_rows, feat_width = tokens.shape
    assert seq_count == 1
    enc_local = encoded.shape[1]
    scale = DH ** (-0.5)
    flat = tokens.reshape(local_rows, feat_width)
    enc_flat = encoded.reshape(enc_local, feat_width)

    weights = [
        query_weight, key_weight, value_weight, out_weight, probe_weight,
        lookup_weight, content_weight, merge_weight, expand_weight, reduce_weight,
    ]
    vectors = [
        query_bias, value_bias, out_bias, first_gain, first_shift, probe_bias, content_bias,
        merge_bias, second_gain, second_shift, reduce_bias, third_gain, third_shift,
    ]
    part = vectors[0].shape[0]
    long_part = expand_bias.shape[0]
    held = WIDE * part + long_part
    padded = -(-held // 1024) * 1024
    vec_block = (8, padded // 8)
    packed = jnp.concatenate(vectors + [expand_bias, jnp.zeros((padded - held,), F32)])
    blocks = [w.astype(BF).reshape(block_shape(*w.shape)) for w in weights]
    kinds = [False, False] + [True] * (len(blocks) + 1)
    gathered = gather_all(
        cube, [flat, enc_flat] + blocks + [packed.reshape(vec_block)], kinds, 0
    )
    n_dev = cube.n_dev
    tok_all = gathered[0].reshape(cube.n_seq * local_rows, feat_width)
    enc_all = gathered[1].reshape(cube.n_seq * enc_local, feat_width)
    (
        query_mat, key_mat, value_mat, out_mat, probe_mat,
        lookup_mat, content_mat, merge_mat, expand_mat, reduce_mat,
    ) = [
        g.reshape(w.shape[0] * n_dev, w.shape[1]) for g, w in zip(gathered[2:12], weights)
    ]
    vec_all = gathered[12].reshape(n_dev, padded)
    wide_all = (
        vec_all[:, : WIDE * part].reshape(n_dev, WIDE, part).transpose(1, 0, 2).reshape(WIDE, -1)
    )
    (
        query_vec, value_vec, out_vec, gain_first, shift_first, probe_vec, content_vec,
        merge_vec, gain_second, shift_second, reduce_vec, gain_third, shift_third,
    ) = [wide_all[i] for i in range(WIDE)]
    expand_vec = vec_all[:, WIDE * part : held].reshape(-1)

    offset = lax.axis_index("seq") * local_rows
    query_doc = lax.dynamic_slice_in_dim(doc_ids, offset, local_rows, 1)
    query_block = lax.dynamic_slice_in_dim(block_ids, offset, local_rows, 1)
    ids = (
        jnp.concatenate([doc_ids, block_ids], axis=0).T,
        jnp.concatenate([query_doc, query_block], axis=0),
    )
    token_float = flat.astype(F32)
    queries = ((matmul(flat, query_mat) + query_vec) * scale).astype(BF)
    all_keys = matmul(tok_all, key_mat).astype(BF)
    all_values = (matmul(tok_all, value_mat) + value_vec).astype(BF)
    self_outb, self_logs = attend_call(False, ids, [queries, all_keys, all_values])
    first_sum = token_float + matmul(self_outb, out_mat) + out_vec
    normed_one, inv_one = layer_stats(first_sum)
    stream_one = (normed_one * gain_first + shift_first).astype(BF)
    probe = ((matmul(stream_one, probe_mat) + probe_vec) * scale).astype(BF)
    enc_keys = matmul(enc_all, lookup_mat).astype(BF)
    enc_values = (matmul(enc_all, content_mat) + content_vec).astype(BF)
    cross_outb, cross_logs = attend_call(False, None, [probe, enc_keys, enc_values])
    second_sum = stream_one.astype(F32) + matmul(cross_outb, merge_mat) + merge_vec
    normed_two, inv_two = layer_stats(second_sum)
    stream_two = (normed_two * gain_second + shift_second).astype(BF)
    expanded = matmul(stream_two, expand_mat) + expand_vec
    activated = jax.nn.gelu(expanded, approximate=False).astype(BF)
    third_sum = stream_two.astype(F32) + matmul(activated, reduce_mat) + reduce_vec
    normed_three, inv_three = layer_stats(third_sum)
    output = (normed_three * gain_third + shift_third).astype(BF)

    grad_output = cotangent.reshape(local_rows, feat_width).astype(F32)
    g_shift_third = jnp.sum(grad_output, axis=0)
    g_gain_third = jnp.sum(grad_output * normed_three, axis=0)
    grad_three = layer_back(grad_output * gain_third, normed_three, inv_three)
    reduce_rows = grad_three.astype(BF)
    g_reduce_vec = jnp.sum(grad_three, axis=0)
    g_reduce_mat = left_outer(activated, reduce_rows)
    grad_act = right_trans(reduce_rows, reduce_mat)
    slope = 0.5 * (
        1.0 + jax.scipy.special.erf(expanded * INV_ROOT_TWO)
    ) + expanded * DENSITY_CONST * jnp.exp(-0.5 * expanded * expanded)
    grad_expanded = grad_act * slope
    g_expand_vec = jnp.sum(grad_expanded, axis=0)
    expand_rows = grad_expanded.astype(BF)
    g_expand_mat = left_outer(stream_two, expand_rows)

    def spread(grad, weight):
        return grad.astype(BF).reshape(cube.lead(True) + block_shape(*weight.shape))

    expand_sum, reduce_sum = scatter_all(
        cube,
        [spread(g_reduce_mat, reduce_weight), spread(g_expand_mat, expand_weight)],
        [True, True],
        1,
    )[::-1]

    grad_two = grad_three + right_trans(expand_rows, expand_mat)
    g_shift_second = jnp.sum(grad_two, axis=0)
    g_gain_second = jnp.sum(grad_two * normed_two, axis=0)
    grad_second = layer_back(grad_two * gain_second, normed_two, inv_two)
    merge_rows = grad_second.astype(BF)
    g_merge_vec = jnp.sum(grad_second, axis=0)
    g_merge_mat = left_outer(cross_outb, merge_rows)
    grad_cross = right_trans(merge_rows, merge_mat).astype(BF)
    probe_rows, enc_key_rows, enc_value_rows = attend_call(
        True, None, [probe, enc_keys, enc_values, grad_cross, cross_logs]
    )
    g_probe_vec = jnp.sum(probe_rows.astype(F32), axis=0)
    g_probe_mat = left_outer(stream_one, probe_rows)
    g_lookup_mat = left_outer(enc_all, enc_key_rows)
    g_content_mat = left_outer(enc_all, enc_value_rows)
    g_content_vec = jnp.sum(enc_value_rows.astype(F32), axis=0)
    enc_part = right_trans(enc_key_rows, lookup_mat) + right_trans(enc_value_rows, content_mat)
    grad_one = grad_second + right_trans(probe_rows, probe_mat)
    g_shift_first = jnp.sum(grad_one, axis=0)
    g_gain_first = jnp.sum(grad_one * normed_one, axis=0)
    grad_first = layer_back(grad_one * gain_first, normed_one, inv_one)
    out_rows = grad_first.astype(BF)
    g_out_vec = jnp.sum(grad_first, axis=0)
    g_out_mat = left_outer(self_outb, out_rows)
    grad_self = right_trans(out_rows, out_mat).astype(BF)
    query_rows, key_rows, value_rows = attend_call(
        True, ids, [queries, all_keys, all_values, grad_self, self_logs]
    )
    g_query_vec = jnp.sum(query_rows.astype(F32), axis=0)
    g_value_vec = jnp.sum(value_rows.astype(F32), axis=0)
    g_query_mat = left_outer(flat, query_rows)
    g_key_mat = left_outer(tok_all, key_rows)
    g_value_mat = left_outer(tok_all, value_rows)
    tok_part = right_trans(key_rows, key_mat) + right_trans(value_rows, value_mat)
    tok_own = grad_first + right_trans(query_rows, query_mat)

    wide_grads = jnp.stack(
        [
            g_query_vec, g_value_vec, g_out_vec, g_gain_first, g_shift_first, g_probe_vec, g_content_vec,
            g_merge_vec, g_gain_second, g_shift_second, g_reduce_vec, g_gain_third, g_shift_third,
        ]
    )
    vec_grads = jnp.concatenate(
        [
            wide_grads.reshape(WIDE, n_dev, part).transpose(1, 0, 2).reshape(n_dev, WIDE * part),
            g_expand_vec.reshape(n_dev, long_part),
            jnp.zeros((n_dev, padded - held), F32),
        ],
        axis=1,
    ).reshape(cube.lead(True) + vec_block)
    mats = [
        g_merge_mat, g_probe_mat, g_lookup_mat, g_content_mat, g_out_mat,
        g_query_mat, g_key_mat, g_value_mat,
    ]
    shards = [
        merge_weight, probe_weight, lookup_weight, content_weight, out_weight,
        query_weight, key_weight, value_weight,
    ]
    sums = scatter_all(
        cube,
        [
            enc_part.astype(BF).reshape(cube.n_seq, enc_local, feat_width),
            tok_part.astype(BF).reshape(cube.n_seq, local_rows, feat_width),
        ]
        + [spread(g, w) for g, w in zip(mats, shards)]
        + [vec_grads],
        [False, False] + [True] * (len(mats) + 1),
        2,
    )
    encoded_grad = sums[0]
    tokens_grad = tok_own + sums[1]
    (
        merge_sum, probe_sum, lookup_sum, content_sum, out_sum, query_sum, key_sum, value_sum,
    ) = [s.reshape(w.shape) for s, w in zip(sums[2:10], shards)]
    expand_sum = expand_sum.reshape(expand_weight.shape)
    reduce_sum = reduce_sum.reshape(reduce_weight.shape)
    vec_sum = sums[10].reshape(padded)
    (
        query_vs, value_vs, out_vs, gain1_vs, shift1_vs, probe_vs, content_vs,
        merge_vs, gain2_vs, shift2_vs, reduce_vs, gain3_vs, shift3_vs,
    ) = [vec_sum[i * part : (i + 1) * part] for i in range(WIDE)]
    expand_vs = vec_sum[WIDE * part : held]
    return (
        output[None],
        tokens_grad[None],
        encoded_grad[None],
        query_sum,
        key_sum,
        value_sum,
        out_sum,
        query_vs,
        value_vs,
        out_vs,
        gain1_vs,
        shift1_vs,
        probe_sum,
        lookup_sum,
        content_sum,
        merge_sum,
        probe_vs,
        content_vs,
        merge_vs,
        gain2_vs,
        shift2_vs,
        expand_sum,
        expand_vs,
        reduce_sum,
        reduce_vs,
        gain3_vs,
        shift3_vs,
    )


def solution(mesh):
    rows = P("dp", "seq", None)
    ids = P("dp", None)
    mat = P(("dp", "seq"), None)
    vec = P(("dp", "seq"))
    return jax.shard_map(
        functools.partial(local, Cube(mesh)),
        mesh=mesh,
        in_specs=(
            (rows, rows, rows, ids, ids)
            + (mat, mat, mat, mat, vec, vec, vec, vec, vec)
            + (mat, mat, mat, mat, vec, vec, vec, vec, vec)
            + (mat, vec, mat, vec, vec, vec)
        ),
        out_specs=(
            (rows, rows, rows)
            + (mat, mat, mat, mat, vec, vec, vec, vec, vec)
            + (mat, mat, mat, mat, vec, vec, vec, vec, vec)
            + (mat, vec, mat, vec, vec, vec)
        ),
        check_vma=False,
    )
```

```python
import functools
import itertools
import math

import jax
import jax.numpy as jnp
from jax import lax
from jax.experimental import pallas as pl
from jax.experimental.pallas import tpu as pltpu
from jax.sharding import PartitionSpec as P

H = 16
DH = 64

EPS = 1e-05
NEG = -1000000000.0
INV_ROOT_TWO = 0.7071067811865476
DENSITY_CONST = 0.3989422804014327
MESH = pl.DeviceIdType.MESH
PIECE = 16384
BF = jnp.bfloat16
F32 = jnp.float32


def matmul(left_arg, right_arg):
    return jnp.dot(left_arg, right_arg, preferred_element_type=F32)


def left_outer(left_arg, right_arg):
    return lax.dot_general(
        left_arg, right_arg, (((0,), (0,)), ((), ())), preferred_element_type=F32
    )


def right_trans(left_arg, right_arg):
    return lax.dot_general(
        left_arg, right_arg, (((1,), (1,)), ((), ())), preferred_element_type=F32
    )


def layer_stats(hidden):
    row_mean = jnp.mean(hidden, axis=-1, keepdims=True)
    centered = hidden - row_mean
    inv_std = lax.rsqrt(jnp.mean(centered * centered, axis=-1, keepdims=True) + EPS)
    return (centered * inv_std, inv_std)


def layer_back(grad_norm, normed, inv_std):
    first_mean = jnp.mean(grad_norm, axis=-1, keepdims=True)
    second_mean = jnp.mean(grad_norm * normed, axis=-1, keepdims=True)
    return inv_std * (grad_norm - first_mean - normed * second_mean)


class Cube:
    def __init__(self, mesh):
        self.n_dp = mesh.shape["dp"]
        self.n_seq = mesh.shape["seq"]
        self.dp_bits = self.n_dp.bit_length() - 1
        assert self.n_dp == 1 << self.dp_bits
        self.n_dev = self.n_dp * self.n_seq

    def lead(self, full):
        return ((2,) * self.dp_bits if full else ()) + (self.n_seq,)


class Place:
    def __init__(self, cube):
        self.dp, self.seq = lax.axis_index("dp"), lax.axis_index("seq")
        self.bits, self.flips = [], []
        rest = self.dp
        for bit in range(cube.dp_bits):
            half = rest // 2
            self.bits.append(rest - 2 * half)
            self.flips.append(self.dp + (1 << bit) * (1 - 2 * self.bits[-1]))
            rest = half


def block_shape(rows, cols):
    if rows % 16 == 0:
        return (rows, cols)
    return (16, rows * cols // 16)


def dim_order(cube, variant):
    bits = list(range(1, cube.dp_bits))
    return bits if variant == 0 else bits[::-1]


def meet(cube, here):
    dp, seq = here.dp, here.seq
    barrier = pltpu.get_barrier_semaphore()

    def greet(device):
        pl.semaphore_signal(barrier, inc=1, device_id=device, device_id_type=MESH)

    for bit in range(cube.dp_bits):
        greet((here.flips[bit], seq))
    greet((dp, lax.rem(seq + 1, cube.n_seq)))
    greet((dp, lax.rem(seq + cube.n_seq - 1, cube.n_seq)))
    pl.semaphore_wait(barrier, cube.dp_bits + 2)


def in_slots(pieces, lag):
    depth = max(len(stages) for stages in pieces)
    for slot in range(len(pieces) + lag * (depth - 1)):
        for k in reversed(range(depth)):
            p = slot - lag * k
            if 0 <= p < len(pieces) and k < len(pieces[p]):
                pieces[p][k]()


def remote(source, target, send_sem, recv_sem, device):
    return pltpu.make_async_remote_copy(
        src_ref=source,
        dst_ref=target,
        send_sem=send_sem,
        recv_sem=recv_sem,
        device_id=device,
        device_id_type=MESH,
    )


def gather_stages(cube, here, full, variant, source, target, send_sem, recv_sem, local_sem):
    dp, seq = here.dp, here.seq
    n = cube.n_seq
    order = dim_order(cube, variant)
    every = pl.ds(0, n)
    waits = []

    def region(open_bits, fixed, seq_part):
        if not full:
            return (seq_part,)
        places = []
        for bit in reversed(range(cube.dp_bits)):
            if bit in open_bits:
                places.append(slice(None))
            else:
                places.append(fixed.get(bit, here.bits[bit]))
        return tuple(places) + (seq_part,)

    def move(place, slot, device):
        at = target.at[place]
        return remote(at, at, send_sem.at[slot], recv_sem.at[slot], device)

    own = pltpu.make_async_copy(source, target.at[region((), {}, seq)], local_sem)

    def line(step, way):
        slot = 2 * step + (1 if way > 0 else 0)
        block = seq - way * step
        inside = (seq + way >= 0) & (seq + way < n)
        sends = inside & (block >= 0) & (block < n)
        copy = lambda: move(region((), {}, block), slot, (dp, seq + way))
        came = seq - way * (step + 1)
        gets = (came >= 0) & (came < n)
        arrival = lambda: move(region((), {}, came), slot, (dp, seq - way))
        return sends, copy, gets, arrival

    def line_start(step):
        for way in (1, -1):
            sends, copy, _, _ = line(step, way)
            pl.when(sends)(lambda: copy().start())
            waits.append((sends, copy))

    def line_wait(step):
        for way in (1, -1):
            _, _, gets, arrival = line(step, way)
            pl.when(gets)(lambda: arrival().wait_recv())

    base = 2 * (n - 1)
    cores, arrivals = [], []

    def dims_start(stage):
        if stage < len(order):
            copy = move(
                region(order[:stage], {}, every), base + 2 * stage, (here.flips[order[stage]], seq)
            )
            copy.start()
            waits.append((None, copy))
            arrivals.append(copy)
        if stage == 0:
            fresh = region((), {}, every)
        else:
            last = order[stage - 1]
            fresh = region(order[: stage - 1], {last: 1 - here.bits[last]}, every)
        copy = move(fresh, base + 2 * stage + 1, (here.flips[0], seq))
        copy.start()
        waits.append((None, copy))
        cores.append(copy)

    def first():
        own.wait()
        line_start(0)

    stages = [first]
    for step in range(n - 1):

        def after_line(step=step):
            line_wait(step)
            if step < n - 2:
                line_start(step + 1)
            elif full:
                dims_start(0)

        stages.append(after_line)
    if full:
        for stage in range(len(order)):

            def after_dims(stage=stage):
                arrivals[stage].wait_recv()
                dims_start(stage + 1)

            stages.append(after_dims)

        def last():
            for copy in cores:
                copy.wait_recv()

        stages.append(last)

    def finish():
        for sends, copy in waits:
            if sends is None:
                copy.wait_send()
            else:
                pl.when(sends)(lambda: copy().wait_send())

    return own, stages, finish


def gather_slots(cube):
    return 2 * (cube.n_seq - 1) + 2 * cube.dp_bits


def gather_kernel(cube, pieces, casts, *refs):
    count = 1 + max(piece[0] for piece in pieces)
    ins, outs = list(refs[:count]), refs[count : 2 * count]
    wide, stage = refs[2 * count : -4][: len(casts)], refs[2 * count : -4][len(casts) :]
    send_sem, recv_sem, local_sem, cast_sem = refs[-4:]
    here = Place(cube)
    loads = [
        pltpu.make_async_copy(ins[array], held, cast_sem.at[turn])
        for turn, (array, held) in enumerate(zip(casts, wide))
    ]
    for copy in loads:
        copy.start()
    for array, copy, held, narrow in zip(casts, loads, wide, stage):
        copy.wait()
        narrow[...] = held[...].astype(BF)
        ins[array] = narrow
    plans = []
    for index, (array, full, variant, col, cols) in enumerate(pieces):
        lead = cube.dp_bits * full + 1
        cut = (slice(None), pl.ds(col, cols))
        plans.append(
            gather_stages(
                cube,
                here,
                full,
                variant,
                ins[array].at[cut],
                outs[array].at[(slice(None),) * lead + cut],
                send_sem.at[index],
                recv_sem.at[index],
                local_sem.at[index],
            )
        )
    for own, _, _ in plans:
        own.start()
    meet(cube, here)
    in_slots([stages for _, stages, _ in plans], 3)
    for _, _, finish in plans:
        finish()


def cut_columns(kinds, arrays):
    whole, along = [], []
    for index, (full, array) in enumerate(zip(kinds, arrays)):
        cols = array.shape[-1]
        count = max(1, math.prod(array.shape[-2:]) // (PIECE if full else PIECE))
        while cols % (128 * count):
            count //= 2
        width = cols // count
        for i in range(count):
            if full:
                whole.append((index, True, len(whole) % 2, width * i, width))
            else:
                along.append((index, False, 0, width * i, width))
    placed = [((i + 0.5) / len(whole), 0, piece) for i, piece in enumerate(whole)]
    placed += [((i + 0.5) / len(along), 1, piece) for i, piece in enumerate(along)]
    return tuple(piece for _, _, piece in sorted(placed, key=lambda item: item[:2]))


def gather_all(cube, arrays, kinds, casts, collective_id):
    pieces = cut_columns(kinds, arrays)
    outs = [
        jax.ShapeDtypeStruct(
            cube.lead(full) + array.shape, BF if index in casts else array.dtype
        )
        for index, (array, full) in enumerate(zip(arrays, kinds))
    ]
    slots = gather_slots(cube)
    anywhere = pl.BlockSpec(memory_space=pl.ANY)
    return pl.pallas_call(
        functools.partial(gather_kernel, cube, pieces, casts),
        out_shape=outs,
        in_specs=[anywhere] * len(arrays),
        out_specs=[anywhere] * len(arrays),
        scratch_shapes=[pltpu.VMEM(arrays[index].shape, F32) for index in casts]
        + [pltpu.VMEM(arrays[index].shape, BF) for index in casts]
        + [
            pltpu.SemaphoreType.DMA((len(pieces), slots)),
            pltpu.SemaphoreType.DMA((len(pieces), slots)),
            pltpu.SemaphoreType.DMA((len(pieces),)),
            pltpu.SemaphoreType.DMA((len(casts),)),
        ],
        compiler_params=pltpu.CompilerParams(
            collective_id=collective_id,
            has_side_effects=True,
            vmem_limit_bytes=60 * 1024 * 1024,
        ),
        name="gather_weights",
    )(*arrays)


def add_block(total, part):
    total[...] = (total[...].astype(F32) + part[...].astype(F32)).astype(total.dtype)


def add_rows(pairs, count, rows, cols):
    step = rows
    while step * cols > 32768 and step % 32 == 0:
        step //= 2

    def body(index, carry):
        for total, part in pairs:
            for row in range(0, rows, step):
                at = (index, pl.ds(row, step))
                add_block(total.at[at], part.at[at])
        return carry

    lax.fori_loop(0, count, body, 0)


def scatter_stages(
    cube, here, full, variant, source, out, own, parts, send_sem, recv_sem, local_sem
):
    dp, seq = here.dp, here.seq
    n = cube.n_seq
    order = dim_order(cube, variant) if full else []
    rows, cols = out.shape
    line_part = parts[-1]
    waits = []
    arrivals = []

    def dims(fixed, kept):
        return tuple(
            fixed[bit] if bit in fixed else kept for bit in reversed(range(1, cube.dp_bits))
        )

    mine = {bit: here.bits[bit] for bit in range(1, cube.dp_bits)}
    settled = dims(mine, None) if full else ()
    lead = (slice(None),) * (cube.dp_bits - 1)
    kept = source.at[lead + (here.bits[0],)] if full else source
    local = pltpu.make_async_copy(kept, own, local_sem)

    def push(stage, what, device):
        copy = remote(what, parts[stage], send_sem.at[stage], recv_sem.at[stage], device)
        copy.start()
        waits.append((None, copy))
        arrivals.append(copy)

    base = cube.dp_bits if full else 0

    def line(step, way):
        target = seq + way * (n - 1 - step)
        passes = (target >= 0) & (target < n)
        further = passes & ((seq > 0) if way > 0 else (seq < n - 1))
        slot = n if way < 0 and step == n - 2 else target
        block = own.at[settled + (target,)]
        index = base + 2 * step + (1 if way > 0 else 0)

        def copy():
            return remote(
                block, line_part.at[slot], send_sem.at[index], recv_sem.at[index], (dp, seq + way)
            )

        def arrival():
            at = line_part.at[target]
            return remote(at, at, send_sem.at[index - 2], recv_sem.at[index - 2], (dp, seq - way))

        return target, passes, further, copy, arrival

    def line_step(step):
        for way in (1, -1):
            target, passes, further, copy, arrival = line(step, way)
            if step > 0:

                @pl.when(further)
                def _():
                    arrival().wait_recv()
                    to, of = own.at[settled + (pl.ds(target, 1),)], line_part.at[pl.ds(target, 1)]
                    add_rows([(to, of)], 1, rows, cols)

            pl.when(passes)(lambda: copy().start())
            waits.append((passes, copy))

    def start():
        local.start()
        if full:
            push(0, source.at[lead + (1 - here.bits[0],)], (here.flips[0], seq))

    def after_dims(stage):
        if stage == 0:
            local.wait()
        arrivals[stage].wait_recv()
        closed = order[:stage]
        fixed = {bit: mine[bit] for bit in closed}
        open_bits = [bit for bit in reversed(range(1, cube.dp_bits)) if bit not in closed]

        pairs = []
        for values in itertools.product((0, 1), repeat=len(open_bits)):
            to = dims({**fixed, **dict(zip(open_bits, values))}, None)
            pairs.append((own.at[to], parts[stage].at[values]))
        add_rows(pairs, n, rows, cols)
        if stage < len(order):
            bit = order[stage]
            at = dims({**fixed, bit: 1 - mine[bit]}, slice(None)) + (pl.ds(0, n),)
            push(stage + 1, own.at[at], (here.flips[bit], seq))
        else:
            line_step(0)

    def last():
        where = settled + (seq,)

        def sem(way):
            return recv_sem.at[base + 2 * (n - 2) + (1 if way > 0 else 0)]

        @pl.when(seq > 0)
        def _():
            at = line_part.at[seq]
            remote(at, at, send_sem.at[base], sem(1), (dp, seq - 1)).wait_recv()

        @pl.when(seq < n - 1)
        def _():
            at = line_part.at[n]
            remote(at, at, send_sem.at[base], sem(-1), (dp, seq + 1)).wait_recv()

        @pl.when(seq == 0)
        def _():
            out[...] = own[where].astype(F32) + line_part[n].astype(F32)

        @pl.when(seq == n - 1)
        def _():
            out[...] = own[where].astype(F32) + line_part[n - 1].astype(F32)

        @pl.when((seq > 0) & (seq < n - 1))
        def _():
            both = line_part[seq].astype(F32) + line_part[n].astype(F32)
            out[...] = own[where].astype(F32) + both

    stages = [start]
    if full:
        stages += [functools.partial(after_dims, stage) for stage in range(cube.dp_bits)]
    else:

        def begin():
            local.wait()
            line_step(0)

        stages.append(begin)
    stages += [functools.partial(line_step, step) for step in range(1, n - 1)]
    stages.append(last)

    def finish():
        for passes, copy in waits:
            if passes is None:
                copy.wait_send()
            else:
                pl.when(passes)(lambda: copy().wait_send())

    return stages, finish


def scatter_kernel(cube, pieces, *refs):
    count = 1 + max(piece[0] for piece in pieces)
    ins, outs = refs[:count], refs[count : 2 * count]
    refs = refs[2 * count :]
    send_sem, recv_sem, local_sem = refs[-3:]
    here = Place(cube)
    plans = []
    for index, (array, full, variant, col, cols) in enumerate(pieces):
        held = 2 + (cube.dp_bits if full else 0)
        cut = (slice(None), pl.ds(col, cols))
        plans.append(
            scatter_stages(
                cube,
                here,
                full,
                variant,
                ins[array].at[(slice(None),) * (cube.dp_bits * full + 1) + cut],
                outs[array].at[cut],
                refs[0],
                refs[1:held],
                send_sem.at[index],
                recv_sem.at[index],
                local_sem.at[index],
            )
        )
        refs = refs[held:]
    meet(cube, here)
    in_slots([stages for stages, _ in plans], 4)
    for _, finish in plans:
        finish()


def scatter_shapes(cube, array, full, cols):
    block = (array.shape[-2], cols)
    shapes = []
    if full:
        for stage in range(-1, cube.dp_bits):
            lead = (2,) * (cube.dp_bits - 1 - max(stage, 0)) + (cube.n_seq,)
            shapes.append(lead + block)
    else:
        shapes.append((cube.n_seq,) + block)
    shapes.append((cube.n_seq + 1,) + block)
    return shapes


def scatter_group(cube, arrays, kinds, collective_id):
    pieces = cut_columns(kinds, arrays)
    outs = [jax.ShapeDtypeStruct(array.shape[-2:], F32) for array in arrays]
    scratch = []
    for array, full, _, _, cols in pieces:
        for shape in scatter_shapes(cube, arrays[array], full, cols):
            scratch.append(pltpu.VMEM(shape, arrays[array].dtype))
    slots = 2 * cube.n_seq + cube.dp_bits
    scratch += [
        pltpu.SemaphoreType.DMA((len(pieces), slots)),
        pltpu.SemaphoreType.DMA((len(pieces), slots)),
        pltpu.SemaphoreType.DMA((len(pieces),)),
    ]
    return pl.pallas_call(
        functools.partial(scatter_kernel, cube, pieces),
        out_shape=outs,
        in_specs=[pl.BlockSpec(memory_space=pl.ANY)] * len(arrays),
        out_specs=[pl.BlockSpec(memory_space=pltpu.VMEM)] * len(arrays),
        scratch_shapes=scratch,
        compiler_params=pltpu.CompilerParams(
            collective_id=collective_id,
            has_side_effects=True,
            vmem_limit_bytes=60 * 1024 * 1024,
        ),
        name="scatter_grads",
    )(*arrays)


def scatter_all(cube, arrays, kinds, collective_id):
    groups, room = [[]], 0
    for index, (array, full) in enumerate(zip(arrays, kinds)):
        shapes = scatter_shapes(cube, array, full, array.shape[-1])
        need = sum(math.prod(shape) for shape in shapes) * array.dtype.itemsize
        need += 4 * math.prod(array.shape[-2:])
        if groups[-1] and room + need > 54 * 1024 * 1024:
            groups.append([])
            room = 0
        groups[-1].append(index)
        room += need
    sums = []
    for turn, group in enumerate(groups):
        sums += scatter_group(
            cube, [arrays[i] for i in group], [kinds[i] for i in group], collective_id + turn
        )
    return sums


def hand_out_kernel(count, parts, *refs):
    sums, vec, part_sum, part_own = refs[:count], refs[count], refs[count + 1], refs[count + 2]
    refs = refs[count + 3 :]
    outs, vec_outs, part_out = refs[:count], refs[count : count + len(parts)], refs[count + len(parts)]
    held, sem = refs[-1 - count : -1], refs[-1]
    ins = [
        pltpu.make_async_copy(one, mid, sem.at[0, turn])
        for turn, (one, mid) in enumerate(zip(sums, held))
    ]
    copies = [
        pltpu.make_async_copy(mid, out, sem.at[1, turn])
        for turn, (mid, out) in enumerate(zip(held, outs))
    ]
    for copy in ins:
        copy.start()
    for row, (size, out) in enumerate(zip(parts, vec_outs)):
        out[...] = vec[row, 0:size]
    part_out[...] = part_own[...] + part_sum[...]
    for before, copy in zip(ins, copies):
        before.wait()
        copy.start()
    for copy in copies:
        copy.wait()


def hand_out(sums, vec, parts, part_sum, part_own):
    anywhere = pl.BlockSpec(memory_space=pl.ANY)
    inside = pl.BlockSpec(memory_space=pltpu.VMEM)
    count = len(sums)
    return pl.pallas_call(
        functools.partial(hand_out_kernel, count, parts),
        out_shape=[jax.ShapeDtypeStruct(one.shape, F32) for one in sums]
        + [jax.ShapeDtypeStruct((size,), F32) for size in parts]
        + [jax.ShapeDtypeStruct(part_sum.shape, F32)],
        in_specs=[anywhere] * count + [inside] * 3,
        out_specs=[anywhere] * count + [inside] * (len(parts) + 1),
        scratch_shapes=[pltpu.VMEM(one.shape, F32) for one in sums]
        + [pltpu.SemaphoreType.DMA((2, count))],
        compiler_params=pltpu.CompilerParams(vmem_limit_bytes=60 * 1024 * 1024),
        name="hand_out",
    )(*sums, vec, part_sum, part_own)


def write_bias(bias, key_ids, query_ids):
    same = key_ids[:, 0:1] == query_ids[0:1, :]
    early = key_ids[:, 1:2] <= query_ids[1:2, :]
    bias[...] = jnp.where(same & early, 0.0, NEG)


def one_head(array, head):
    lane = lax.broadcasted_iota(jnp.int32, array.shape, 1)
    keep = (lane < DH) if head == 0 else (lane >= DH)
    return jnp.where(keep, array, jnp.zeros_like(array))


def attend_kernel(masked, *refs):
    if masked:
        key_ids, query_ids, query_ref, key_ref, value_ref, out_ref, log_ref, bias = refs
        pl.when(pl.program_id(0) == 0)(lambda: write_bias(bias, key_ids[...], query_ids[...]))
    else:
        query_ref, key_ref, value_ref, out_ref, log_ref = refs
    query, key = query_ref[...], key_ref[...]
    value_t = value_ref[...].T
    outs, logs = [], []
    for head in range(2):
        scores = right_trans(key, one_head(query, head))
        if masked:
            scores = scores + bias[...]
        top = jnp.max(scores, axis=0, keepdims=True)
        expon = jnp.exp(scores - top)
        total = jnp.sum(expon, axis=0, keepdims=True)
        got = matmul(value_t[head * DH : (head + 1) * DH], expon.astype(BF))
        outs.append(got * (1.0 / total))
        logs.append(top + jnp.log(total))
    out_ref[...] = jnp.concatenate(outs, axis=0).T.astype(BF)
    log_ref[0] = jnp.concatenate(logs, axis=0)


def attend_back_kernel(masked, *refs):
    if masked:
        key_ids, query_ids, query_ref, key_ref, value_ref, grad_ref, log_ref = refs[:7]
        dq_ref, dk_ref, dv_ref, bias = refs[7:]
        pl.when(pl.program_id(0) == 0)(lambda: write_bias(bias, key_ids[...], query_ids[...]))
    else:
        query_ref, key_ref, value_ref, grad_ref, log_ref, dq_ref, dk_ref, dv_ref = refs
    query, key, value, grad = query_ref[...], key_ref[...], value_ref[...], grad_ref[...]
    key_t = key.T
    dq, dk, dv = [], None, None
    for head in range(2):
        query_head, grad_head = one_head(query, head), one_head(grad, head)
        scores = right_trans(key, query_head)
        if masked:
            scores = scores + bias[...]
        probs = jnp.exp(scores - log_ref[0, head : head + 1, :])
        grad_probs = right_trans(value, grad_head)
        delta = jnp.sum(probs * grad_probs, axis=0, keepdims=True)
        grad_scores = (probs * (grad_probs - delta)).astype(BF)
        dq.append(matmul(key_t[head * DH : (head + 1) * DH], grad_scores))
        dk_head = matmul(grad_scores, query_head)
        dv_head = matmul(probs.astype(BF), grad_head)
        dk = dk_head if dk is None else dk + dk_head
        dv = dv_head if dv is None else dv + dv_head
    scale = DH ** (-0.5)
    dq_ref[...] = (jnp.concatenate(dq, axis=0).T.astype(BF).astype(F32) * scale).astype(BF)
    dk_ref[...] = dk.astype(BF)
    dv_ref[...] = dv.astype(BF)


def attend_call(back, ids, arrays):
    rows, width = arrays[0].shape
    keys = arrays[1].shape[0]
    pair = 2 * DH
    steps = width // pair
    masked = ids is not None
    by_query = pl.BlockSpec((rows, pair), lambda i: (0, i))
    by_key = pl.BlockSpec((keys, pair), lambda i: (0, i))
    logs = pl.BlockSpec((1, 2, rows), lambda i: (i, 0, 0))
    in_specs = [by_query, by_key, by_key]
    if masked:
        in_specs = [
            pl.BlockSpec((keys, 2), lambda i: (0, 0)),
            pl.BlockSpec((2, rows), lambda i: (0, 0)),
        ] + in_specs
        arrays = list(ids) + list(arrays)
    log_shape = jax.ShapeDtypeStruct((steps, 2, rows), F32)
    query_shape = jax.ShapeDtypeStruct((rows, width), BF)
    key_shape = jax.ShapeDtypeStruct((keys, width), BF)
    if back:
        in_specs += [by_query, logs]
        out_specs, out_shape = [by_query, by_key, by_key], [query_shape, key_shape, key_shape]
    else:
        out_specs, out_shape = [by_query, logs], [query_shape, log_shape]
    products = 7 if back else 2
    return pl.pallas_call(
        functools.partial(attend_back_kernel if back else attend_kernel, masked),
        grid=(steps,),
        in_specs=in_specs,
        out_specs=out_specs,
        out_shape=out_shape,
        scratch_shapes=[pltpu.VMEM((keys, rows), F32)] if masked else [],
        cost_estimate=pl.CostEstimate(
            flops=2 * products * rows * keys * width,
            bytes_accessed=2 * width * (rows + keys) * products,
            transcendentals=rows * keys * width // DH,
        ),
        compiler_params=pltpu.CompilerParams(vmem_limit_bytes=48 * 1024 * 1024),
        name="attend_back" if back else "attend",
    )(*arrays)


WIDE = 13


def local(
    cube,
    tokens,
    encoded,
    cotangent,
    doc_ids,
    block_ids,
    query_weight,
    key_weight,
    value_weight,
    out_weight,
    query_bias,
    value_bias,
    out_bias,
    first_gain,
    first_shift,
    probe_weight,
    lookup_weight,
    content_weight,
    merge_weight,
    probe_bias,
    content_bias,
    merge_bias,
    second_gain,
    second_shift,
    expand_weight,
    expand_bias,
    reduce_weight,
    reduce_bias,
    third_gain,
    third_shift,
):
    seq_count, local_rows, feat_width = tokens.shape
    assert seq_count == 1
    enc_local = encoded.shape[1]
    scale = DH ** (-0.5)
    flat = tokens.reshape(local_rows, feat_width)
    enc_flat = encoded.reshape(enc_local, feat_width)

    weights = [
        query_weight, key_weight, value_weight, out_weight, probe_weight,
        lookup_weight, content_weight, merge_weight, expand_weight, reduce_weight,
    ]
    vectors = [
        query_bias, value_bias, out_bias, first_gain, first_shift, probe_bias, content_bias,
        merge_bias, second_gain, second_shift, reduce_bias, third_gain, third_shift,
    ]
    part = vectors[0].shape[0]
    long_part = expand_bias.shape[0]
    held = WIDE * part + long_part
    padded = -(-held // 1024) * 1024
    vec_block = (8, padded // 8)
    packed = jnp.concatenate(vectors + [expand_bias, jnp.zeros((padded - held,), F32)])
    blocks = [w.reshape(block_shape(*w.shape)) for w in weights[:9]]
    kinds = [False, False] + [True] * (len(blocks) + 1)
    gathered = gather_all(
        cube,
        [flat, enc_flat] + blocks + [packed.reshape(vec_block)],
        kinds,
        tuple(range(2, 2 + len(blocks))),
        0,
    )
    late, vec_all = lax.optimization_barrier((reduce_weight.astype(BF), gathered[11]))
    reduce_mat = lax.all_gather(late, ("dp", "seq"), axis=0, tiled=True)
    n_dev = cube.n_dev
    tok_all = gathered[0].reshape(cube.n_seq * local_rows, feat_width)
    enc_all = gathered[1].reshape(cube.n_seq * enc_local, feat_width)
    (
        query_mat, key_mat, value_mat, out_mat, probe_mat,
        lookup_mat, content_mat, merge_mat, expand_mat,
    ) = [
        g.reshape(w.shape[0] * n_dev, w.shape[1]) for g, w in zip(gathered[2:11], weights)
    ]
    vec_all = vec_all.reshape(n_dev, padded)
    wide_all = (
        vec_all[:, : WIDE * part].reshape(n_dev, WIDE, part).transpose(1, 0, 2).reshape(WIDE, -1)
    )
    (
        query_vec, value_vec, out_vec, gain_first, shift_first, probe_vec, content_vec,
        merge_vec, gain_second, shift_second, reduce_vec, gain_third, shift_third,
    ) = [wide_all[i] for i in range(WIDE)]
    expand_vec = vec_all[:, WIDE * part : held].reshape(-1)

    offset = lax.axis_index("seq") * local_rows
    query_doc = lax.dynamic_slice_in_dim(doc_ids, offset, local_rows, 1)
    query_block = lax.dynamic_slice_in_dim(block_ids, offset, local_rows, 1)
    ids = (
        jnp.concatenate([doc_ids, block_ids], axis=0).T,
        jnp.concatenate([query_doc, query_block], axis=0),
    )
    token_float = flat.astype(F32)
    queries = ((matmul(flat, query_mat) + query_vec) * scale).astype(BF)
    all_keys = matmul(tok_all, key_mat).astype(BF)
    all_values = (matmul(tok_all, value_mat) + value_vec).astype(BF)
    self_outb, self_logs = attend_call(False, ids, [queries, all_keys, all_values])
    first_sum = token_float + matmul(self_outb, out_mat) + out_vec
    normed_one, inv_one = layer_stats(first_sum)
    stream_one = (normed_one * gain_first + shift_first).astype(BF)
    probe = ((matmul(stream_one, probe_mat) + probe_vec) * scale).astype(BF)
    enc_keys = matmul(enc_all, lookup_mat).astype(BF)
    enc_values = (matmul(enc_all, content_mat) + content_vec).astype(BF)
    cross_outb, cross_logs = attend_call(False, None, [probe, enc_keys, enc_values])
    second_sum = stream_one.astype(F32) + matmul(cross_outb, merge_mat) + merge_vec
    normed_two, inv_two = layer_stats(second_sum)
    stream_two = (normed_two * gain_second + shift_second).astype(BF)
    expanded = matmul(stream_two, expand_mat) + expand_vec
    activated = jax.nn.gelu(expanded, approximate=False).astype(BF)
    third_sum = stream_two.astype(F32) + matmul(activated, reduce_mat) + reduce_vec
    normed_three, inv_three = layer_stats(third_sum)
    output = (normed_three * gain_third + shift_third).astype(BF)

    grad_output = cotangent.reshape(local_rows, feat_width).astype(F32)
    g_shift_third = jnp.sum(grad_output, axis=0)
    g_gain_third = jnp.sum(grad_output * normed_three, axis=0)
    grad_three = layer_back(grad_output * gain_third, normed_three, inv_three)
    reduce_rows = grad_three.astype(BF)
    g_reduce_vec = jnp.sum(grad_three, axis=0)
    g_reduce_mat = left_outer(activated, reduce_rows).astype(BF)
    reduce_part = g_reduce_mat.reshape((cube.n_dp, cube.n_seq) + reduce_weight.shape)
    reduce_part = lax.psum_scatter(reduce_part, "dp", scatter_dimension=0, tiled=True)
    reduce_part = lax.psum_scatter(reduce_part, "seq", scatter_dimension=1, tiled=True)
    reduce_sum = reduce_part.astype(F32)
    grad_act = right_trans(reduce_rows, reduce_mat)
    slope = 0.5 * (
        1.0 + jax.scipy.special.erf(expanded * INV_ROOT_TWO)
    ) + expanded * DENSITY_CONST * jnp.exp(-0.5 * expanded * expanded)
    grad_expanded = grad_act * slope
    g_expand_vec = jnp.sum(grad_expanded, axis=0)
    expand_rows = grad_expanded.astype(BF)
    g_expand_mat = left_outer(stream_two, expand_rows)

    def spread(grad, weight):
        return grad.astype(BF).reshape(cube.lead(True) + block_shape(*weight.shape))

    grad_two = grad_three + right_trans(expand_rows, expand_mat)
    g_shift_second = jnp.sum(grad_two, axis=0)
    g_gain_second = jnp.sum(grad_two * normed_two, axis=0)
    grad_second = layer_back(grad_two * gain_second, normed_two, inv_two)
    merge_rows = grad_second.astype(BF)
    g_merge_vec = jnp.sum(grad_second, axis=0)
    g_merge_mat = left_outer(cross_outb, merge_rows)
    grad_cross = right_trans(merge_rows, merge_mat).astype(BF)
    probe_rows, enc_key_rows, enc_value_rows = attend_call(
        True, None, [probe, enc_keys, enc_values, grad_cross, cross_logs]
    )
    g_probe_vec = jnp.sum(probe_rows.astype(F32), axis=0)
    g_probe_mat = left_outer(stream_one, probe_rows)
    g_lookup_mat = left_outer(enc_all, enc_key_rows)
    g_content_mat = left_outer(enc_all, enc_value_rows)
    g_content_vec = jnp.sum(enc_value_rows.astype(F32), axis=0)
    enc_part = right_trans(enc_key_rows, lookup_mat) + right_trans(enc_value_rows, content_mat)
    grad_one = grad_second + right_trans(probe_rows, probe_mat)
    g_shift_first = jnp.sum(grad_one, axis=0)
    g_gain_first = jnp.sum(grad_one * normed_one, axis=0)
    grad_first = layer_back(grad_one * gain_first, normed_one, inv_one)
    out_rows = grad_first.astype(BF)
    g_out_vec = jnp.sum(grad_first, axis=0)
    g_out_mat = left_outer(self_outb, out_rows)
    grad_self = right_trans(out_rows, out_mat).astype(BF)
    query_rows, key_rows, value_rows = attend_call(
        True, ids, [queries, all_keys, all_values, grad_self, self_logs]
    )
    g_query_vec = jnp.sum(query_rows.astype(F32), axis=0)
    g_value_vec = jnp.sum(value_rows.astype(F32), axis=0)
    g_query_mat = left_outer(flat, query_rows)
    g_key_mat = left_outer(tok_all, key_rows)
    g_value_mat = left_outer(tok_all, value_rows)
    tok_part = right_trans(key_rows, key_mat) + right_trans(value_rows, value_mat)
    tok_own = grad_first + right_trans(query_rows, query_mat)

    wide_grads = jnp.stack(
        [
            g_query_vec, g_value_vec, g_out_vec, g_gain_first, g_shift_first, g_probe_vec, g_content_vec,
            g_merge_vec, g_gain_second, g_shift_second, g_reduce_vec, g_gain_third, g_shift_third,
        ]
    )
    lanes = 128
    vec_grads = jnp.pad(
        wide_grads.reshape(WIDE, n_dev, part).transpose(1, 0, 2), ((0, 0), (0, 0), (0, lanes - part))
    )
    long_row = jnp.pad(g_expand_vec.reshape(n_dev, 1, long_part), ((0, 0), (0, 0), (0, lanes - long_part)))
    vec_grads = jnp.concatenate([vec_grads, long_row, jnp.zeros((n_dev, 2, lanes), F32)], axis=1)
    vec_grads = vec_grads.reshape(cube.lead(True) + (WIDE + 3, lanes))
    mats = [
        g_expand_mat, g_merge_mat, g_probe_mat, g_lookup_mat, g_content_mat, g_out_mat,
        g_query_mat, g_key_mat, g_value_mat,
    ]
    shards = [
        expand_weight, merge_weight, probe_weight, lookup_weight, content_weight, out_weight,
        query_weight, key_weight, value_weight,
    ]
    sums = scatter_all(
        cube,
        [
            enc_part.astype(BF).reshape(cube.n_seq, enc_local, feat_width),
            tok_part.astype(BF).reshape(cube.n_seq, local_rows, feat_width),
        ]
        + [spread(g, w) for g, w in zip(mats, shards)]
        + [vec_grads],
        [False, False] + [True] * (len(mats) + 1),
        1,
    )
    done = hand_out(
        [sums[0]] + list(sums[2:11]), sums[11], (part,) * WIDE + (long_part,), sums[1], tok_own
    )
    encoded_grad = done[0]
    (
        expand_sum, merge_sum, probe_sum, lookup_sum, content_sum, out_sum, query_sum, key_sum, value_sum,
    ) = [one.reshape(w.shape) for one, w in zip(done[1:10], shards)]
    reduce_sum = reduce_sum.reshape(reduce_weight.shape)
    (
        query_vs, value_vs, out_vs, gain1_vs, shift1_vs, probe_vs, content_vs,
        merge_vs, gain2_vs, shift2_vs, reduce_vs, gain3_vs, shift3_vs, expand_vs,
    ) = done[10:24]
    tokens_grad = done[24]
    return (
        output[None],
        tokens_grad[None],
        encoded_grad[None],
        query_sum,
        key_sum,
        value_sum,
        out_sum,
        query_vs,
        value_vs,
        out_vs,
        gain1_vs,
        shift1_vs,
        probe_sum,
        lookup_sum,
        content_sum,
        merge_sum,
        probe_vs,
        content_vs,
        merge_vs,
        gain2_vs,
        shift2_vs,
        expand_sum,
        expand_vs,
        reduce_sum,
        reduce_vs,
        gain3_vs,
        shift3_vs,
    )


def solution(mesh):
    rows = P("dp", "seq", None)
    ids = P("dp", None)
    mat = P(("dp", "seq"), None)
    vec = P(("dp", "seq"))
    return jax.shard_map(
        functools.partial(local, Cube(mesh)),
        mesh=mesh,
        in_specs=(
            (rows, rows, rows, ids, ids)
            + (mat, mat, mat, mat, vec, vec, vec, vec, vec)
            + (mat, mat, mat, mat, vec, vec, vec, vec, vec)
            + (mat, vec, mat, vec, vec, vec)
        ),
        out_specs=(
            (rows, rows, rows)
            + (mat, mat, mat, mat, vec, vec, vec, vec, vec)
            + (mat, mat, mat, mat, vec, vec, vec, vec, vec)
            + (mat, vec, mat, vec, vec, vec)
        ),
        check_vma=False,
    )
```

```python
import functools
import itertools
import math

import jax
import jax.numpy as jnp
from jax import lax
from jax.experimental import pallas as pl
from jax.experimental.pallas import tpu as pltpu
from jax.sharding import PartitionSpec as P

H = 16
DH = 64

EPS = 1e-05
NEG = -1000000000.0
INV_ROOT_TWO = 0.7071067811865476
DENSITY_CONST = 0.3989422804014327
MESH = pl.DeviceIdType.MESH
PIECE = 16384
BF = jnp.bfloat16
F32 = jnp.float32


def matmul(left_arg, right_arg):
    return jnp.dot(left_arg, right_arg, preferred_element_type=F32)


def left_outer(left_arg, right_arg):
    return lax.dot_general(
        left_arg, right_arg, (((0,), (0,)), ((), ())), preferred_element_type=F32
    )


def right_trans(left_arg, right_arg):
    return lax.dot_general(
        left_arg, right_arg, (((1,), (1,)), ((), ())), preferred_element_type=F32
    )


def layer_stats(hidden):
    row_mean = jnp.mean(hidden, axis=-1, keepdims=True)
    centered = hidden - row_mean
    inv_std = lax.rsqrt(jnp.mean(centered * centered, axis=-1, keepdims=True) + EPS)
    return (centered * inv_std, inv_std)


def layer_back(grad_norm, normed, inv_std):
    first_mean = jnp.mean(grad_norm, axis=-1, keepdims=True)
    second_mean = jnp.mean(grad_norm * normed, axis=-1, keepdims=True)
    return inv_std * (grad_norm - first_mean - normed * second_mean)


class Cube:
    def __init__(self, mesh):
        self.n_dp = mesh.shape["dp"]
        self.n_seq = mesh.shape["seq"]
        self.dp_bits = self.n_dp.bit_length() - 1
        assert self.n_dp == 1 << self.dp_bits
        self.n_dev = self.n_dp * self.n_seq

    def lead(self, full):
        return ((2,) * self.dp_bits if full else ()) + (self.n_seq,)


class Place:
    def __init__(self, cube):
        self.dp, self.seq = lax.axis_index("dp"), lax.axis_index("seq")
        self.bits, self.flips = [], []
        rest = self.dp
        for bit in range(cube.dp_bits):
            half = rest // 2
            self.bits.append(rest - 2 * half)
            self.flips.append(self.dp + (1 << bit) * (1 - 2 * self.bits[-1]))
            rest = half


def block_shape(rows, cols):
    if rows % 16 == 0:
        return (rows, cols)
    return (16, rows * cols // 16)


def dim_order(cube, variant):
    bits = list(range(1, cube.dp_bits))
    return bits if variant == 0 else bits[::-1]


def meet(cube, here):
    dp, seq = here.dp, here.seq
    barrier = pltpu.get_barrier_semaphore()

    def greet(device):
        pl.semaphore_signal(barrier, inc=1, device_id=device, device_id_type=MESH)

    for bit in range(cube.dp_bits):
        greet((here.flips[bit], seq))
    greet((dp, lax.rem(seq + 1, cube.n_seq)))
    greet((dp, lax.rem(seq + cube.n_seq - 1, cube.n_seq)))
    pl.semaphore_wait(barrier, cube.dp_bits + 2)


def in_slots(pieces, lag):
    depth = max(len(stages) for stages in pieces)
    for slot in range(len(pieces) + lag * (depth - 1)):
        for k in reversed(range(depth)):
            p = slot - lag * k
            if 0 <= p < len(pieces) and k < len(pieces[p]):
                pieces[p][k]()


def remote(source, target, send_sem, recv_sem, device):
    return pltpu.make_async_remote_copy(
        src_ref=source,
        dst_ref=target,
        send_sem=send_sem,
        recv_sem=recv_sem,
        device_id=device,
        device_id_type=MESH,
    )


def gather_stages(cube, here, full, variant, source, target, send_sem, recv_sem, local_sem):
    dp, seq = here.dp, here.seq
    n = cube.n_seq
    order = dim_order(cube, variant)
    every = pl.ds(0, n)
    waits = []

    def region(open_bits, fixed, seq_part):
        if not full:
            return (seq_part,)
        places = []
        for bit in reversed(range(cube.dp_bits)):
            if bit in open_bits:
                places.append(slice(None))
            else:
                places.append(fixed.get(bit, here.bits[bit]))
        return tuple(places) + (seq_part,)

    def move(place, slot, device):
        at = target.at[place]
        return remote(at, at, send_sem.at[slot], recv_sem.at[slot], device)

    own = pltpu.make_async_copy(source, target.at[region((), {}, seq)], local_sem)

    def line(step, way):
        slot = 2 * step + (1 if way > 0 else 0)
        block = seq - way * step
        inside = (seq + way >= 0) & (seq + way < n)
        sends = inside & (block >= 0) & (block < n)
        copy = lambda: move(region((), {}, block), slot, (dp, seq + way))
        came = seq - way * (step + 1)
        gets = (came >= 0) & (came < n)
        arrival = lambda: move(region((), {}, came), slot, (dp, seq - way))
        return sends, copy, gets, arrival

    def line_start(step):
        for way in (1, -1):
            sends, copy, _, _ = line(step, way)
            pl.when(sends)(lambda: copy().start())
            waits.append((sends, copy))

    def line_wait(step):
        for way in (1, -1):
            _, _, gets, arrival = line(step, way)
            pl.when(gets)(lambda: arrival().wait_recv())

    base = 2 * (n - 1)
    cores, arrivals = [], []

    def dims_start(stage):
        if stage < len(order):
            copy = move(
                region(order[:stage], {}, every), base + 2 * stage, (here.flips[order[stage]], seq)
            )
            copy.start()
            waits.append((None, copy))
            arrivals.append(copy)
        if stage == 0:
            fresh = region((), {}, every)
        else:
            last = order[stage - 1]
            fresh = region(order[: stage - 1], {last: 1 - here.bits[last]}, every)
        copy = move(fresh, base + 2 * stage + 1, (here.flips[0], seq))
        copy.start()
        waits.append((None, copy))
        cores.append(copy)

    def first():
        own.wait()
        line_start(0)

    stages = [first]
    for step in range(n - 1):

        def after_line(step=step):
            line_wait(step)
            if step < n - 2:
                line_start(step + 1)
            elif full:
                dims_start(0)

        stages.append(after_line)
    if full:
        for stage in range(len(order)):

            def after_dims(stage=stage):
                arrivals[stage].wait_recv()
                dims_start(stage + 1)

            stages.append(after_dims)

        def last():
            for copy in cores:
                copy.wait_recv()

        stages.append(last)

    def finish():
        for sends, copy in waits:
            if sends is None:
                copy.wait_send()
            else:
                pl.when(sends)(lambda: copy().wait_send())

    return own, stages, finish


def gather_slots(cube):
    return 2 * (cube.n_seq - 1) + 2 * cube.dp_bits


def gather_kernel(cube, pieces, casts, *refs):
    count = 1 + max(piece[0] for piece in pieces)
    ins, outs = list(refs[:count]), refs[count : 2 * count]
    wide, stage = refs[2 * count : -4][: len(casts)], refs[2 * count : -4][len(casts) :]
    send_sem, recv_sem, local_sem, cast_sem = refs[-4:]
    here = Place(cube)
    loads = [
        pltpu.make_async_copy(ins[array], held, cast_sem.at[turn])
        for turn, (array, held) in enumerate(zip(casts, wide))
    ]
    for copy in loads:
        copy.start()
    for array, copy, held, narrow in zip(casts, loads, wide, stage):
        copy.wait()
        narrow[...] = held[...].astype(BF)
        ins[array] = narrow
    plans = []
    for index, (array, full, variant, col, cols) in enumerate(pieces):
        lead = cube.dp_bits * full + 1
        cut = (slice(None), pl.ds(col, cols))
        plans.append(
            gather_stages(
                cube,
                here,
                full,
                variant,
                ins[array].at[cut],
                outs[array].at[(slice(None),) * lead + cut],
                send_sem.at[index],
                recv_sem.at[index],
                local_sem.at[index],
            )
        )
    for own, _, _ in plans:
        own.start()
    meet(cube, here)
    in_slots([stages for _, stages, _ in plans], 3)
    for _, _, finish in plans:
        finish()


def cut_columns(kinds, arrays):
    whole, along = [], []
    for index, (full, array) in enumerate(zip(kinds, arrays)):
        cols = array.shape[-1]
        count = max(1, math.prod(array.shape[-2:]) // (PIECE if full else PIECE))
        while cols % (128 * count):
            count //= 2
        width = cols // count
        for i in range(count):
            if full:
                whole.append((index, True, len(whole) % 2, width * i, width))
            else:
                along.append((index, False, 0, width * i, width))
    placed = [((i + 0.5) / len(whole), 0, piece) for i, piece in enumerate(whole)]
    placed += [((i + 0.5) / len(along), 1, piece) for i, piece in enumerate(along)]
    return tuple(piece for _, _, piece in sorted(placed, key=lambda item: item[:2]))


def gather_all(cube, arrays, kinds, casts, collective_id):
    pieces = cut_columns(kinds, arrays)
    outs = [
        jax.ShapeDtypeStruct(
            cube.lead(full) + array.shape, BF if index in casts else array.dtype
        )
        for index, (array, full) in enumerate(zip(arrays, kinds))
    ]
    slots = gather_slots(cube)
    anywhere = pl.BlockSpec(memory_space=pl.ANY)
    return pl.pallas_call(
        functools.partial(gather_kernel, cube, pieces, casts),
        out_shape=outs,
        in_specs=[anywhere] * len(arrays),
        out_specs=[anywhere] * len(arrays),
        scratch_shapes=[pltpu.VMEM(arrays[index].shape, F32) for index in casts]
        + [pltpu.VMEM(arrays[index].shape, BF) for index in casts]
        + [
            pltpu.SemaphoreType.DMA((len(pieces), slots)),
            pltpu.SemaphoreType.DMA((len(pieces), slots)),
            pltpu.SemaphoreType.DMA((len(pieces),)),
            pltpu.SemaphoreType.DMA((len(casts),)),
        ],
        compiler_params=pltpu.CompilerParams(
            collective_id=collective_id,
            has_side_effects=True,
            vmem_limit_bytes=60 * 1024 * 1024,
        ),
        name="gather_weights",
    )(*arrays)


def add_block(total, part):
    total[...] = (total[...].astype(F32) + part[...].astype(F32)).astype(total.dtype)


def add_rows(pairs, count, rows, cols):
    step = rows
    while step * cols > 32768 and step % 32 == 0:
        step //= 2

    def body(index, carry):
        for total, part in pairs:
            for row in range(0, rows, step):
                at = (index, pl.ds(row, step))
                add_block(total.at[at], part.at[at])
        return carry

    lax.fori_loop(0, count, body, 0)


def scatter_stages(
    cube, here, full, variant, source, out, own, parts, send_sem, recv_sem, local_sem, factors=None
):
    dp, seq = here.dp, here.seq
    n = cube.n_seq
    order = dim_order(cube, variant) if full else []
    rows, cols = out.shape
    line_part = parts[-1]
    waits = []
    arrivals = []

    def dims(fixed, kept):
        return tuple(
            fixed[bit] if bit in fixed else kept for bit in reversed(range(1, cube.dp_bits))
        )

    mine = {bit: here.bits[bit] for bit in range(1, cube.dp_bits)}
    settled = dims(mine, None) if full else ()
    lead = (slice(None),) * (cube.dp_bits - 1)
    if factors is None:
        kept = source.at[lead + (here.bits[0],)] if full else source
        local = pltpu.make_async_copy(kept, own, local_sem)

    def halves(core):
        left, right = factors[:2]
        for number, at in enumerate(itertools.product((0, 1), repeat=cube.dp_bits - 1)):
            first = pl.multiple_of((2 * number + core) * (n * rows), 128)
            block = left_outer(left[:, pl.ds(first, n * rows)], right.read())
            yield at, block.reshape(n, rows, cols)

    def push(stage, what, device):
        copy = remote(what, parts[stage], send_sem.at[stage], recv_sem.at[stage], device)
        copy.start()
        waits.append((None, copy))
        arrivals.append(copy)

    base = cube.dp_bits if full else 0

    def line(step, way):
        target = seq + way * (n - 1 - step)
        passes = (target >= 0) & (target < n)
        further = passes & ((seq > 0) if way > 0 else (seq < n - 1))
        slot = n if way < 0 and step == n - 2 else target
        block = own.at[settled + (target,)]
        index = base + 2 * step + (1 if way > 0 else 0)

        def copy():
            return remote(
                block, line_part.at[slot], send_sem.at[index], recv_sem.at[index], (dp, seq + way)
            )

        def arrival():
            at = line_part.at[target]
            return remote(at, at, send_sem.at[index - 2], recv_sem.at[index - 2], (dp, seq - way))

        return target, passes, further, copy, arrival

    def line_step(step):
        for way in (1, -1):
            target, passes, further, copy, arrival = line(step, way)
            if step > 0:

                @pl.when(further)
                def _():
                    arrival().wait_recv()
                    to, of = own.at[settled + (pl.ds(target, 1),)], line_part.at[pl.ds(target, 1)]
                    add_rows([(to, of)], 1, rows, cols)

            pl.when(passes)(lambda: copy().start())
            waits.append((passes, copy))

    def start():
        if factors is not None:
            _, _, ready, ring = factors
            ready()
            buffer = ring()
            for at, block in halves(1 - here.bits[0]):
                buffer[at] = block.astype(buffer.dtype)
            push(0, buffer, (here.flips[0], seq))
            ring(arrivals[0])
            waits.pop()
            return
        local.start()
        if full:
            push(0, source.at[lead + (1 - here.bits[0],)], (here.flips[0], seq))

    def after_dims(stage):
        if stage == 0 and factors is None:
            local.wait()
        arrivals[stage].wait_recv()
        if stage == 0 and factors is not None:
            for at, block in halves(here.bits[0]):
                own[at] = (block + own[at].astype(F32)).astype(own.dtype)
        closed = order[:stage]
        fixed = {bit: mine[bit] for bit in closed}
        open_bits = [bit for bit in reversed(range(1, cube.dp_bits)) if bit not in closed]

        pairs = []
        for values in itertools.product((0, 1), repeat=len(open_bits)):
            to = dims({**fixed, **dict(zip(open_bits, values))}, None)
            pairs.append((own.at[to], parts[stage].at[values]))
        if stage > 0 or factors is None:
            add_rows(pairs, n, rows, cols)
        if stage < len(order):
            bit = order[stage]
            at = dims({**fixed, bit: 1 - mine[bit]}, slice(None)) + (pl.ds(0, n),)
            push(stage + 1, own.at[at], (here.flips[bit], seq))
        else:
            line_step(0)

    def last():
        where = settled + (seq,)

        def sem(way):
            return recv_sem.at[base + 2 * (n - 2) + (1 if way > 0 else 0)]

        @pl.when(seq > 0)
        def _():
            at = line_part.at[seq]
            remote(at, at, send_sem.at[base], sem(1), (dp, seq - 1)).wait_recv()

        @pl.when(seq < n - 1)
        def _():
            at = line_part.at[n]
            remote(at, at, send_sem.at[base], sem(-1), (dp, seq + 1)).wait_recv()

        @pl.when(seq == 0)
        def _():
            out[...] = own[where].astype(F32) + line_part[n].astype(F32)

        @pl.when(seq == n - 1)
        def _():
            out[...] = own[where].astype(F32) + line_part[n - 1].astype(F32)

        @pl.when((seq > 0) & (seq < n - 1))
        def _():
            both = line_part[seq].astype(F32) + line_part[n].astype(F32)
            out[...] = own[where].astype(F32) + both

    stages = [start]
    if full:
        stages += [functools.partial(after_dims, stage) for stage in range(cube.dp_bits)]
    else:

        def begin():
            local.wait()
            line_step(0)

        stages.append(begin)
    stages += [functools.partial(line_step, step) for step in range(1, n - 1)]
    stages.append(last)

    def finish():
        for passes, copy in waits:
            if passes is None:
                copy.wait_send()
            else:
                pl.when(passes)(lambda: copy().wait_send())

    return stages, finish


class Product:
    def __init__(self, left, right, block):
        self.left, self.right, self.dtype = left, right, jnp.dtype(BF)
        self.shape = tuple(block)


class Ring:
    def __init__(self, buffers, depth):
        self.buffers, self.depth, self.copies = buffers, depth, []

    def __call__(self, copy=None):
        if copy is not None:
            self.copies.append(copy)
            return None
        turn = len(self.copies)
        if turn >= self.depth:
            self.copies[turn - self.depth].wait_send()
        return self.buffers.at[turn % self.depth]

    def finish(self):
        for copy in self.copies[-self.depth :]:
            copy.wait_send()


RING = 6


def scatter_kernel(cube, pieces, products, operands, *refs):
    count = 1 + max(piece[0] for piece in pieces)
    arrays = [index for index in range(count) if index not in products]
    ins = dict(zip(arrays, refs))
    refs = refs[len(arrays) :]
    sources, refs = refs[:operands], refs[operands:]
    outs, refs = refs[:count], refs[count:]
    send_sem, recv_sem, local_sem = refs[-3:]
    refs = refs[:-3]
    here = Place(cube)
    ring = None
    if operands:
        held, buffers, load_sem = refs[-2 - operands : -2], refs[-2], refs[-1]
        loads = [
            pltpu.make_async_copy(source, to, load_sem.at[turn])
            for turn, (source, to) in enumerate(zip(sources, held))
        ]
        for copy in loads:
            copy.start()
        ring = Ring(buffers, RING)
        waited = set()

        def ready(places):
            for place in places:
                if place not in waited:
                    loads[place].wait()
                    waited.add(place)

    plans = []
    for index, (array, full, variant, col, cols) in enumerate(pieces):
        cut = (slice(None), pl.ds(col, cols))
        if array in products:
            places = products[array]
            own, taken = refs[0], 1 + cube.dp_bits
            parts, source = refs[:taken], None
            left, right = held[places[0]], held[places[1]]
            factors = (left, ColumnsOf(right, col, cols), functools.partial(ready, places), ring)
        else:
            taken = 2 + (cube.dp_bits if full else 0)
            own, parts, factors = refs[0], refs[1:taken], None
            source = ins[array].at[(slice(None),) * (cube.dp_bits * full + 1) + cut]
        plans.append(
            scatter_stages(
                cube,
                here,
                full,
                variant,
                source,
                outs[array].at[cut],
                own,
                parts,
                send_sem.at[index],
                recv_sem.at[index],
                local_sem.at[index],
                factors,
            )
        )
        refs = refs[taken:]
    meet(cube, here)
    in_slots([stages for stages, _ in plans], 4)
    for _, finish in plans:
        finish()
    if ring is not None:
        ring.finish()


def scatter_shapes(cube, array, full, cols):
    block = (array.shape[-2], cols)
    shapes = []
    if full:
        for stage in range(0 if isinstance(array, Product) else -1, cube.dp_bits):
            lead = (2,) * (cube.dp_bits - 1 - max(stage, 0)) + (cube.n_seq,)
            shapes.append(lead + block)
    else:
        shapes.append((cube.n_seq,) + block)
    shapes.append((cube.n_seq + 1,) + block)
    return shapes


def scatter_group(cube, arrays, kinds, collective_id):
    pieces = cut_columns(kinds, arrays)
    outs = [jax.ShapeDtypeStruct(array.shape[-2:], F32) for array in arrays]
    scratch = []
    for array, full, _, _, cols in pieces:
        for shape in scatter_shapes(cube, arrays[array], full, cols):
            scratch.append(pltpu.VMEM(shape, arrays[array].dtype))
    given, operands, products = [], [], {}
    for index, array in enumerate(arrays):
        if not isinstance(array, Product):
            given.append(array)
            continue
        for factor in (array.left, array.right):
            if not any(factor is one for one in operands):
                operands.append(factor)
        places = [
            [factor is one for one in operands].index(True) for factor in (array.left, array.right)
        ]
        products[index] = tuple(places)
    if operands:
        scratch += [pltpu.VMEM(one.shape, one.dtype) for one in operands]
        halves = {
            scatter_shapes(cube, arrays[piece[0]], True, piece[4])[0]
            for piece in pieces
            if piece[0] in products
        }
        (half,) = halves
        scratch += [
            pltpu.VMEM((RING,) + half, BF),
            pltpu.SemaphoreType.DMA((len(operands),)),
        ]
    slots = 2 * cube.n_seq + cube.dp_bits
    scratch += [
        pltpu.SemaphoreType.DMA((len(pieces), slots)),
        pltpu.SemaphoreType.DMA((len(pieces), slots)),
        pltpu.SemaphoreType.DMA((len(pieces),)),
    ]
    return pl.pallas_call(
        functools.partial(scatter_kernel, cube, pieces, products, len(operands)),
        out_shape=outs,
        in_specs=[pl.BlockSpec(memory_space=pl.ANY)] * (len(given) + len(operands)),
        out_specs=[pl.BlockSpec(memory_space=pltpu.VMEM)] * len(arrays),
        scratch_shapes=scratch,
        compiler_params=pltpu.CompilerParams(
            collective_id=collective_id,
            has_side_effects=True,
            vmem_limit_bytes=60 * 1024 * 1024,
        ),
        name="scatter_grads",
    )(*given, *operands)


def scatter_all(cube, arrays, kinds, collective_id):
    groups, room = [[]], 0
    for index, (array, full) in enumerate(zip(arrays, kinds)):
        shapes = scatter_shapes(cube, array, full, array.shape[-1])
        need = sum(math.prod(shape) for shape in shapes) * array.dtype.itemsize
        need += 4 * math.prod(array.shape[-2:])
        if groups[-1] and room + need > 54 * 1024 * 1024:
            groups.append([])
            room = 0
        groups[-1].append(index)
        room += need
    sums = []
    for turn, group in enumerate(groups):
        sums += scatter_group(
            cube, [arrays[i] for i in group], [kinds[i] for i in group], collective_id + turn
        )
    return sums


class ColumnsOf:
    def __init__(self, ref, col, cols):
        self.ref, self.at = ref, (slice(None), pl.ds(col, cols))

    def read(self):
        return self.ref[self.at]


def hand_out_kernel(count, parts, *refs):
    sums, vec, part_sum, part_own = refs[:count], refs[count], refs[count + 1], refs[count + 2]
    refs = refs[count + 3 :]
    outs, vec_outs, part_out = refs[:count], refs[count : count + len(parts)], refs[count + len(parts)]
    held, sem = refs[-1 - count : -1], refs[-1]
    ins = [
        pltpu.make_async_copy(one, mid, sem.at[0, turn])
        for turn, (one, mid) in enumerate(zip(sums, held))
    ]
    copies = [
        pltpu.make_async_copy(mid, out, sem.at[1, turn])
        for turn, (mid, out) in enumerate(zip(held, outs))
    ]
    for copy in ins:
        copy.start()
    for row, (size, out) in enumerate(zip(parts, vec_outs)):
        out[...] = vec[row, 0:size]
    part_out[...] = part_own[...] + part_sum[...]
    for before, copy in zip(ins, copies):
        before.wait()
        copy.start()
    for copy in copies:
        copy.wait()


def hand_out(sums, vec, parts, part_sum, part_own):
    anywhere = pl.BlockSpec(memory_space=pl.ANY)
    inside = pl.BlockSpec(memory_space=pltpu.VMEM)
    count = len(sums)
    return pl.pallas_call(
        functools.partial(hand_out_kernel, count, parts),
        out_shape=[jax.ShapeDtypeStruct(one.shape, F32) for one in sums]
        + [jax.ShapeDtypeStruct((size,), F32) for size in parts]
        + [jax.ShapeDtypeStruct(part_sum.shape, F32)],
        in_specs=[anywhere] * count + [inside] * 3,
        out_specs=[anywhere] * count + [inside] * (len(parts) + 1),
        scratch_shapes=[pltpu.VMEM(one.shape, F32) for one in sums]
        + [pltpu.SemaphoreType.DMA((2, count))],
        compiler_params=pltpu.CompilerParams(vmem_limit_bytes=60 * 1024 * 1024),
        name="hand_out",
    )(*sums, vec, part_sum, part_own)


def write_bias(bias, key_ids, query_ids):
    same = key_ids[:, 0:1] == query_ids[0:1, :]
    early = key_ids[:, 1:2] <= query_ids[1:2, :]
    bias[...] = jnp.where(same & early, 0.0, NEG)


def one_head(array, head):
    lane = lax.broadcasted_iota(jnp.int32, array.shape, 1)
    keep = (lane < DH) if head == 0 else (lane >= DH)
    return jnp.where(keep, array, jnp.zeros_like(array))


def attend_kernel(masked, *refs):
    if masked:
        key_ids, query_ids, query_ref, key_ref, value_ref, out_ref, log_ref, bias = refs
        pl.when(pl.program_id(0) == 0)(lambda: write_bias(bias, key_ids[...], query_ids[...]))
    else:
        query_ref, key_ref, value_ref, out_ref, log_ref = refs
    query, key = query_ref[...], key_ref[...]
    value_t = value_ref[...].T
    outs, logs = [], []
    for head in range(2):
        scores = right_trans(key, one_head(query, head))
        if masked:
            scores = scores + bias[...]
        top = jnp.max(scores, axis=0, keepdims=True)
        expon = jnp.exp(scores - top)
        total = jnp.sum(expon, axis=0, keepdims=True)
        got = matmul(value_t[head * DH : (head + 1) * DH], expon.astype(BF))
        outs.append(got * (1.0 / total))
        logs.append(top + jnp.log(total))
    out_ref[...] = jnp.concatenate(outs, axis=0).T.astype(BF)
    log_ref[0] = jnp.concatenate(logs, axis=0)


def attend_back_kernel(masked, *refs):
    if masked:
        key_ids, query_ids, query_ref, key_ref, value_ref, grad_ref, log_ref = refs[:7]
        dq_ref, dk_ref, dv_ref, bias = refs[7:]
        pl.when(pl.program_id(0) == 0)(lambda: write_bias(bias, key_ids[...], query_ids[...]))
    else:
        query_ref, key_ref, value_ref, grad_ref, log_ref, dq_ref, dk_ref, dv_ref = refs
    query, key, value, grad = query_ref[...], key_ref[...], value_ref[...], grad_ref[...]
    key_t = key.T
    dq, dk, dv = [], None, None
    for head in range(2):
        query_head, grad_head = one_head(query, head), one_head(grad, head)
        scores = right_trans(key, query_head)
        if masked:
            scores = scores + bias[...]
        probs = jnp.exp(scores - log_ref[0, head : head + 1, :])
        grad_probs = right_trans(value, grad_head)
        delta = jnp.sum(probs * grad_probs, axis=0, keepdims=True)
        grad_scores = (probs * (grad_probs - delta)).astype(BF)
        dq.append(matmul(key_t[head * DH : (head + 1) * DH], grad_scores))
        dk_head = matmul(grad_scores, query_head)
        dv_head = matmul(probs.astype(BF), grad_head)
        dk = dk_head if dk is None else dk + dk_head
        dv = dv_head if dv is None else dv + dv_head
    scale = DH ** (-0.5)
    dq_ref[...] = (jnp.concatenate(dq, axis=0).T.astype(BF).astype(F32) * scale).astype(BF)
    dk_ref[...] = dk.astype(BF)
    dv_ref[...] = dv.astype(BF)


def attend_call(back, ids, arrays):
    rows, width = arrays[0].shape
    keys = arrays[1].shape[0]
    pair = 2 * DH
    steps = width // pair
    masked = ids is not None
    by_query = pl.BlockSpec((rows, pair), lambda i: (0, i))
    by_key = pl.BlockSpec((keys, pair), lambda i: (0, i))
    logs = pl.BlockSpec((1, 2, rows), lambda i: (i, 0, 0))
    in_specs = [by_query, by_key, by_key]
    if masked:
        in_specs = [
            pl.BlockSpec((keys, 2), lambda i: (0, 0)),
            pl.BlockSpec((2, rows), lambda i: (0, 0)),
        ] + in_specs
        arrays = list(ids) + list(arrays)
    log_shape = jax.ShapeDtypeStruct((steps, 2, rows), F32)
    query_shape = jax.ShapeDtypeStruct((rows, width), BF)
    key_shape = jax.ShapeDtypeStruct((keys, width), BF)
    if back:
        in_specs += [by_query, logs]
        out_specs, out_shape = [by_query, by_key, by_key], [query_shape, key_shape, key_shape]
    else:
        out_specs, out_shape = [by_query, logs], [query_shape, log_shape]
    products = 7 if back else 2
    return pl.pallas_call(
        functools.partial(attend_back_kernel if back else attend_kernel, masked),
        grid=(steps,),
        in_specs=in_specs,
        out_specs=out_specs,
        out_shape=out_shape,
        scratch_shapes=[pltpu.VMEM((keys, rows), F32)] if masked else [],
        cost_estimate=pl.CostEstimate(
            flops=2 * products * rows * keys * width,
            bytes_accessed=2 * width * (rows + keys) * products,
            transcendentals=rows * keys * width // DH,
        ),
        compiler_params=pltpu.CompilerParams(vmem_limit_bytes=48 * 1024 * 1024),
        name="attend_back" if back else "attend",
    )(*arrays)


WIDE = 13


def local(
    cube,
    tokens,
    encoded,
    cotangent,
    doc_ids,
    block_ids,
    query_weight,
    key_weight,
    value_weight,
    out_weight,
    query_bias,
    value_bias,
    out_bias,
    first_gain,
    first_shift,
    probe_weight,
    lookup_weight,
    content_weight,
    merge_weight,
    probe_bias,
    content_bias,
    merge_bias,
    second_gain,
    second_shift,
    expand_weight,
    expand_bias,
    reduce_weight,
    reduce_bias,
    third_gain,
    third_shift,
):
    seq_count, local_rows, feat_width = tokens.shape
    assert seq_count == 1
    enc_local = encoded.shape[1]
    scale = DH ** (-0.5)
    flat = tokens.reshape(local_rows, feat_width)
    enc_flat = encoded.reshape(enc_local, feat_width)

    weights = [
        query_weight, key_weight, value_weight, out_weight, probe_weight,
        lookup_weight, content_weight, merge_weight, expand_weight, reduce_weight,
    ]
    vectors = [
        query_bias, value_bias, out_bias, first_gain, first_shift, probe_bias, content_bias,
        merge_bias, second_gain, second_shift, reduce_bias, third_gain, third_shift,
    ]
    part = vectors[0].shape[0]
    long_part = expand_bias.shape[0]
    held = WIDE * part + long_part
    padded = -(-held // 1024) * 1024
    vec_block = (8, padded // 8)
    packed = jnp.concatenate(vectors + [expand_bias, jnp.zeros((padded - held,), F32)])
    blocks = [w.reshape(block_shape(*w.shape)) for w in weights[:9]]
    kinds = [False, False] + [True] * (len(blocks) + 1)
    gathered = gather_all(
        cube,
        [flat, enc_flat] + blocks + [packed.reshape(vec_block)],
        kinds,
        tuple(range(2, 2 + len(blocks))),
        0,
    )
    late, vec_all = lax.optimization_barrier((reduce_weight.astype(BF), gathered[11]))
    reduce_mat = lax.all_gather(late, ("dp", "seq"), axis=0, tiled=True)
    n_dev = cube.n_dev
    tok_all = gathered[0].reshape(cube.n_seq * local_rows, feat_width)
    enc_all = gathered[1].reshape(cube.n_seq * enc_local, feat_width)
    (
        query_mat, key_mat, value_mat, out_mat, probe_mat,
        lookup_mat, content_mat, merge_mat, expand_mat,
    ) = [
        g.reshape(w.shape[0] * n_dev, w.shape[1]) for g, w in zip(gathered[2:11], weights)
    ]
    vec_all = vec_all.reshape(n_dev, padded)
    wide_all = (
        vec_all[:, : WIDE * part].reshape(n_dev, WIDE, part).transpose(1, 0, 2).reshape(WIDE, -1)
    )
    (
        query_vec, value_vec, out_vec, gain_first, shift_first, probe_vec, content_vec,
        merge_vec, gain_second, shift_second, reduce_vec, gain_third, shift_third,
    ) = [wide_all[i] for i in range(WIDE)]
    expand_vec = vec_all[:, WIDE * part : held].reshape(-1)

    offset = lax.axis_index("seq") * local_rows
    query_doc = lax.dynamic_slice_in_dim(doc_ids, offset, local_rows, 1)
    query_block = lax.dynamic_slice_in_dim(block_ids, offset, local_rows, 1)
    ids = (
        jnp.concatenate([doc_ids, block_ids], axis=0).T,
        jnp.concatenate([query_doc, query_block], axis=0),
    )
    token_float = flat.astype(F32)
    queries = ((matmul(flat, query_mat) + query_vec) * scale).astype(BF)
    all_keys = matmul(tok_all, key_mat).astype(BF)
    all_values = (matmul(tok_all, value_mat) + value_vec).astype(BF)
    self_outb, self_logs = attend_call(False, ids, [queries, all_keys, all_values])
    first_sum = token_float + matmul(self_outb, out_mat) + out_vec
    normed_one, inv_one = layer_stats(first_sum)
    stream_one = (normed_one * gain_first + shift_first).astype(BF)
    probe = ((matmul(stream_one, probe_mat) + probe_vec) * scale).astype(BF)
    enc_keys = matmul(enc_all, lookup_mat).astype(BF)
    enc_values = (matmul(enc_all, content_mat) + content_vec).astype(BF)
    cross_outb, cross_logs = attend_call(False, None, [probe, enc_keys, enc_values])
    second_sum = stream_one.astype(F32) + matmul(cross_outb, merge_mat) + merge_vec
    normed_two, inv_two = layer_stats(second_sum)
    stream_two = (normed_two * gain_second + shift_second).astype(BF)
    expanded = matmul(stream_two, expand_mat) + expand_vec
    activated = jax.nn.gelu(expanded, approximate=False).astype(BF)
    third_sum = stream_two.astype(F32) + matmul(activated, reduce_mat) + reduce_vec
    normed_three, inv_three = layer_stats(third_sum)
    output = (normed_three * gain_third + shift_third).astype(BF)

    grad_output = cotangent.reshape(local_rows, feat_width).astype(F32)
    g_shift_third = jnp.sum(grad_output, axis=0)
    g_gain_third = jnp.sum(grad_output * normed_three, axis=0)
    grad_three = layer_back(grad_output * gain_third, normed_three, inv_three)
    reduce_rows = grad_three.astype(BF)
    g_reduce_vec = jnp.sum(grad_three, axis=0)
    g_reduce_mat = left_outer(activated, reduce_rows).astype(BF)
    reduce_part = g_reduce_mat.reshape((cube.n_dp, cube.n_seq) + reduce_weight.shape)
    reduce_part = lax.psum_scatter(reduce_part, "dp", scatter_dimension=0, tiled=True)
    reduce_part = lax.psum_scatter(reduce_part, "seq", scatter_dimension=1, tiled=True)
    reduce_sum = reduce_part.astype(F32)
    grad_act = right_trans(reduce_rows, reduce_mat)
    slope = 0.5 * (
        1.0 + jax.scipy.special.erf(expanded * INV_ROOT_TWO)
    ) + expanded * DENSITY_CONST * jnp.exp(-0.5 * expanded * expanded)
    grad_expanded = grad_act * slope
    g_expand_vec = jnp.sum(grad_expanded, axis=0)
    expand_rows = grad_expanded.astype(BF)

    def gradient(left, right, weight):
        block = block_shape(*weight.shape)
        if block == weight.shape and cube.n_seq * block[0] % 128 == 0:
            return Product(left, right, block)
        return left_outer(left, right).astype(BF).reshape(cube.lead(True) + block)

    g_expand_mat = gradient(stream_two, expand_rows, expand_weight)
    grad_two = grad_three + right_trans(expand_rows, expand_mat)
    g_shift_second = jnp.sum(grad_two, axis=0)
    g_gain_second = jnp.sum(grad_two * normed_two, axis=0)
    grad_second = layer_back(grad_two * gain_second, normed_two, inv_two)
    merge_rows = grad_second.astype(BF)
    g_merge_vec = jnp.sum(grad_second, axis=0)
    g_merge_mat = gradient(cross_outb, merge_rows, merge_weight)
    grad_cross = right_trans(merge_rows, merge_mat).astype(BF)
    probe_rows, enc_key_rows, enc_value_rows = attend_call(
        True, None, [probe, enc_keys, enc_values, grad_cross, cross_logs]
    )
    g_probe_vec = jnp.sum(probe_rows.astype(F32), axis=0)
    g_probe_mat = gradient(stream_one, probe_rows, probe_weight)
    g_lookup_mat = gradient(enc_all, enc_key_rows, lookup_weight)
    g_content_mat = gradient(enc_all, enc_value_rows, content_weight)
    g_content_vec = jnp.sum(enc_value_rows.astype(F32), axis=0)
    enc_part = right_trans(enc_key_rows, lookup_mat) + right_trans(enc_value_rows, content_mat)
    grad_one = grad_second + right_trans(probe_rows, probe_mat)
    g_shift_first = jnp.sum(grad_one, axis=0)
    g_gain_first = jnp.sum(grad_one * normed_one, axis=0)
    grad_first = layer_back(grad_one * gain_first, normed_one, inv_one)
    out_rows = grad_first.astype(BF)
    g_out_vec = jnp.sum(grad_first, axis=0)
    g_out_mat = gradient(self_outb, out_rows, out_weight)
    grad_self = right_trans(out_rows, out_mat).astype(BF)
    query_rows, key_rows, value_rows = attend_call(
        True, ids, [queries, all_keys, all_values, grad_self, self_logs]
    )
    g_query_vec = jnp.sum(query_rows.astype(F32), axis=0)
    g_value_vec = jnp.sum(value_rows.astype(F32), axis=0)
    g_query_mat = gradient(flat, query_rows, query_weight)
    g_key_mat = gradient(tok_all, key_rows, key_weight)
    g_value_mat = gradient(tok_all, value_rows, value_weight)
    tok_part = right_trans(key_rows, key_mat) + right_trans(value_rows, value_mat)
    tok_own = grad_first + right_trans(query_rows, query_mat)

    wide_grads = jnp.stack(
        [
            g_query_vec, g_value_vec, g_out_vec, g_gain_first, g_shift_first, g_probe_vec, g_content_vec,
            g_merge_vec, g_gain_second, g_shift_second, g_reduce_vec, g_gain_third, g_shift_third,
        ]
    )
    lanes = 128
    vec_grads = jnp.pad(
        wide_grads.reshape(WIDE, n_dev, part).transpose(1, 0, 2), ((0, 0), (0, 0), (0, lanes - part))
    )
    long_row = jnp.pad(g_expand_vec.reshape(n_dev, 1, long_part), ((0, 0), (0, 0), (0, lanes - long_part)))
    vec_grads = jnp.concatenate([vec_grads, long_row, jnp.zeros((n_dev, 2, lanes), F32)], axis=1)
    vec_grads = vec_grads.reshape(cube.lead(True) + (WIDE + 3, lanes))
    mats = [
        g_expand_mat, g_merge_mat, g_probe_mat, g_lookup_mat, g_content_mat, g_out_mat,
        g_query_mat, g_key_mat, g_value_mat,
    ]
    shards = [
        expand_weight, merge_weight, probe_weight, lookup_weight, content_weight, out_weight,
        query_weight, key_weight, value_weight,
    ]
    sums = scatter_all(
        cube,
        [
            enc_part.astype(BF).reshape(cube.n_seq, enc_local, feat_width),
            tok_part.astype(BF).reshape(cube.n_seq, local_rows, feat_width),
        ]
        + mats
        + [vec_grads],
        [False, False] + [True] * (len(mats) + 1),
        1,
    )
    done = hand_out(
        [sums[0]] + list(sums[2:11]), sums[11], (part,) * WIDE + (long_part,), sums[1], tok_own
    )
    encoded_grad = done[0]
    (
        expand_sum, merge_sum, probe_sum, lookup_sum, content_sum, out_sum, query_sum, key_sum, value_sum,
    ) = [one.reshape(w.shape) for one, w in zip(done[1:10], shards)]
    reduce_sum = reduce_sum.reshape(reduce_weight.shape)
    (
        query_vs, value_vs, out_vs, gain1_vs, shift1_vs, probe_vs, content_vs,
        merge_vs, gain2_vs, shift2_vs, reduce_vs, gain3_vs, shift3_vs, expand_vs,
    ) = done[10:24]
    tokens_grad = done[24]
    return (
        output[None],
        tokens_grad[None],
        encoded_grad[None],
        query_sum,
        key_sum,
        value_sum,
        out_sum,
        query_vs,
        value_vs,
        out_vs,
        gain1_vs,
        shift1_vs,
        probe_sum,
        lookup_sum,
        content_sum,
        merge_sum,
        probe_vs,
        content_vs,
        merge_vs,
        gain2_vs,
        shift2_vs,
        expand_sum,
        expand_vs,
        reduce_sum,
        reduce_vs,
        gain3_vs,
        shift3_vs,
    )


def solution(mesh):
    rows = P("dp", "seq", None)
    ids = P("dp", None)
    mat = P(("dp", "seq"), None)
    vec = P(("dp", "seq"))
    return jax.shard_map(
        functools.partial(local, Cube(mesh)),
        mesh=mesh,
        in_specs=(
            (rows, rows, rows, ids, ids)
            + (mat, mat, mat, mat, vec, vec, vec, vec, vec)
            + (mat, mat, mat, mat, vec, vec, vec, vec, vec)
            + (mat, vec, mat, vec, vec, vec)
        ),
        out_specs=(
            (rows, rows, rows)
            + (mat, mat, mat, mat, vec, vec, vec, vec, vec)
            + (mat, mat, mat, mat, vec, vec, vec, vec, vec)
            + (mat, vec, mat, vec, vec, vec)
        ),
        check_vma=False,
    )
```

```python
import functools
import itertools
import math

import jax
import jax.numpy as jnp
from jax import lax
from jax.experimental import pallas as pl
from jax.experimental.pallas import tpu as pltpu
from jax.sharding import PartitionSpec as P

H = 16
DH = 64

EPS = 1e-05
NEG = -1000000000.0
INV_ROOT_TWO = 0.7071067811865476
DENSITY_CONST = 0.3989422804014327
MESH = pl.DeviceIdType.MESH
PIECE = 16384
BF = jnp.bfloat16
F32 = jnp.float32


def matmul(left_arg, right_arg):
    return jnp.dot(left_arg, right_arg, preferred_element_type=F32)


def left_outer(left_arg, right_arg):
    return lax.dot_general(
        left_arg, right_arg, (((0,), (0,)), ((), ())), preferred_element_type=F32
    )


def right_trans(left_arg, right_arg):
    return lax.dot_general(
        left_arg, right_arg, (((1,), (1,)), ((), ())), preferred_element_type=F32
    )


def layer_stats(hidden):
    row_mean = jnp.mean(hidden, axis=-1, keepdims=True)
    centered = hidden - row_mean
    inv_std = lax.rsqrt(jnp.mean(centered * centered, axis=-1, keepdims=True) + EPS)
    return (centered * inv_std, inv_std)


def layer_back(grad_norm, normed, inv_std):
    first_mean = jnp.mean(grad_norm, axis=-1, keepdims=True)
    second_mean = jnp.mean(grad_norm * normed, axis=-1, keepdims=True)
    return inv_std * (grad_norm - first_mean - normed * second_mean)


class Cube:
    def __init__(self, mesh):
        self.n_dp = mesh.shape["dp"]
        self.n_seq = mesh.shape["seq"]
        self.dp_bits = self.n_dp.bit_length() - 1
        assert self.n_dp == 1 << self.dp_bits
        self.n_dev = self.n_dp * self.n_seq

    def lead(self, full):
        return ((2,) * self.dp_bits if full else ()) + (self.n_seq,)


class Place:
    def __init__(self, cube):
        self.dp, self.seq = lax.axis_index("dp"), lax.axis_index("seq")
        self.bits, self.flips = [], []
        rest = self.dp
        for bit in range(cube.dp_bits):
            half = rest // 2
            self.bits.append(rest - 2 * half)
            self.flips.append(self.dp + (1 << bit) * (1 - 2 * self.bits[-1]))
            rest = half


def block_shape(rows, cols):
    if rows % 16 == 0:
        return (rows, cols)
    return (16, rows * cols // 16)


def dim_order(cube, variant):
    bits = list(range(1, cube.dp_bits))
    return bits if variant == 0 else bits[::-1]


def meet(cube, here):
    dp, seq = here.dp, here.seq
    barrier = pltpu.get_barrier_semaphore()

    def greet(device):
        pl.semaphore_signal(barrier, inc=1, device_id=device, device_id_type=MESH)

    for bit in range(cube.dp_bits):
        greet((here.flips[bit], seq))
    greet((dp, lax.rem(seq + 1, cube.n_seq)))
    greet((dp, lax.rem(seq + cube.n_seq - 1, cube.n_seq)))
    pl.semaphore_wait(barrier, cube.dp_bits + 2)


def in_slots(pieces, lag):
    depth = max(len(stages) for stages in pieces)
    for slot in range(len(pieces) + lag * (depth - 1)):
        for k in reversed(range(depth)):
            p = slot - lag * k
            if 0 <= p < len(pieces) and k < len(pieces[p]):
                pieces[p][k]()


def remote(source, target, send_sem, recv_sem, device):
    return pltpu.make_async_remote_copy(
        src_ref=source,
        dst_ref=target,
        send_sem=send_sem,
        recv_sem=recv_sem,
        device_id=device,
        device_id_type=MESH,
    )


def gather_stages(cube, here, full, variant, source, target, send_sem, recv_sem, local_sem):
    dp, seq = here.dp, here.seq
    n = cube.n_seq
    order = dim_order(cube, variant)
    every = pl.ds(0, n)
    waits = []

    def region(open_bits, fixed, seq_part):
        if not full:
            return (seq_part,)
        places = []
        for bit in reversed(range(cube.dp_bits)):
            if bit in open_bits:
                places.append(slice(None))
            else:
                places.append(fixed.get(bit, here.bits[bit]))
        return tuple(places) + (seq_part,)

    def move(place, slot, device):
        at = target.at[place]
        return remote(at, at, send_sem.at[slot], recv_sem.at[slot], device)

    own = pltpu.make_async_copy(source, target.at[region((), {}, seq)], local_sem)

    def line(step, way):
        slot = 2 * step + (1 if way > 0 else 0)
        block = seq - way * step
        inside = (seq + way >= 0) & (seq + way < n)
        sends = inside & (block >= 0) & (block < n)
        copy = lambda: move(region((), {}, block), slot, (dp, seq + way))
        came = seq - way * (step + 1)
        gets = (came >= 0) & (came < n)
        arrival = lambda: move(region((), {}, came), slot, (dp, seq - way))
        return sends, copy, gets, arrival

    def line_start(step):
        for way in (1, -1):
            sends, copy, _, _ = line(step, way)
            pl.when(sends)(lambda: copy().start())
            waits.append((sends, copy))

    def line_wait(step):
        for way in (1, -1):
            _, _, gets, arrival = line(step, way)
            pl.when(gets)(lambda: arrival().wait_recv())

    base = 2 * (n - 1)
    cores, arrivals = [], []

    def dims_start(stage):
        if stage < len(order):
            copy = move(
                region(order[:stage], {}, every), base + 2 * stage, (here.flips[order[stage]], seq)
            )
            copy.start()
            waits.append((None, copy))
            arrivals.append(copy)
        if stage == 0:
            fresh = region((), {}, every)
        else:
            last = order[stage - 1]
            fresh = region(order[: stage - 1], {last: 1 - here.bits[last]}, every)
        copy = move(fresh, base + 2 * stage + 1, (here.flips[0], seq))
        copy.start()
        waits.append((None, copy))
        cores.append(copy)

    def first():
        own.wait()
        line_start(0)

    stages = [first]
    for step in range(n - 1):

        def after_line(step=step):
            line_wait(step)
            if step < n - 2:
                line_start(step + 1)
            elif full:
                dims_start(0)

        stages.append(after_line)
    if full:
        for stage in range(len(order)):

            def after_dims(stage=stage):
                arrivals[stage].wait_recv()
                dims_start(stage + 1)

            stages.append(after_dims)

        def last():
            for copy in cores:
                copy.wait_recv()

        stages.append(last)

    def finish():
        for sends, copy in waits:
            if sends is None:
                copy.wait_send()
            else:
                pl.when(sends)(lambda: copy().wait_send())

    return own, stages, finish


def gather_slots(cube):
    return 2 * (cube.n_seq - 1) + 2 * cube.dp_bits


def gather_kernel(cube, pieces, casts, *refs):
    count = 1 + max(piece[0] for piece in pieces)
    ins, outs = list(refs[:count]), refs[count : 2 * count]
    wide, stage = refs[2 * count : -4][: len(casts)], refs[2 * count : -4][len(casts) :]
    send_sem, recv_sem, local_sem, cast_sem = refs[-4:]
    here = Place(cube)
    loads = [
        pltpu.make_async_copy(ins[array], held, cast_sem.at[turn])
        for turn, (array, held) in enumerate(zip(casts, wide))
    ]
    for copy in loads:
        copy.start()
    for array, copy, held, narrow in zip(casts, loads, wide, stage):
        copy.wait()
        narrow[...] = held[...].astype(BF)
        ins[array] = narrow
    plans = []
    for index, (array, full, variant, col, cols) in enumerate(pieces):
        lead = cube.dp_bits * full + 1
        cut = (slice(None), pl.ds(col, cols))
        plans.append(
            gather_stages(
                cube,
                here,
                full,
                variant,
                ins[array].at[cut],
                outs[array].at[(slice(None),) * lead + cut],
                send_sem.at[index],
                recv_sem.at[index],
                local_sem.at[index],
            )
        )
    for own, _, _ in plans:
        own.start()
    meet(cube, here)
    in_slots([stages for _, stages, _ in plans], 3)
    for _, _, finish in plans:
        finish()


def cut_columns(kinds, arrays, first, last):
    whole, along = [], []
    for index, (full, array) in enumerate(zip(kinds, arrays)):
        cols = array.shape[-1]
        count = max(1, math.prod(array.shape[-2:]) // (PIECE if full else PIECE))
        while cols % (128 * count):
            count //= 2
        width = cols // count
        for i in range(count):
            if full:
                whole.append((index, True, len(whole) % 2, width * i, width))
            else:
                along.append((index, False, 0, width * i, width))
    placed = [((i + 0.5) / len(whole), 0, piece) for i, piece in enumerate(whole)]
    reach = (last - first) / max(len(along), 1)
    placed += [(first + (i + 0.5) * reach, 1, piece) for i, piece in enumerate(along)]
    return tuple(piece for _, _, piece in sorted(placed, key=lambda item: item[:2]))


def gather_all(cube, arrays, kinds, casts, collective_id):
    pieces = cut_columns(kinds, arrays, 0.3, 1.0)
    outs = [
        jax.ShapeDtypeStruct(
            cube.lead(full) + array.shape, BF if index in casts else array.dtype
        )
        for index, (array, full) in enumerate(zip(arrays, kinds))
    ]
    slots = gather_slots(cube)
    anywhere = pl.BlockSpec(memory_space=pl.ANY)
    return pl.pallas_call(
        functools.partial(gather_kernel, cube, pieces, casts),
        out_shape=outs,
        in_specs=[anywhere] * len(arrays),
        out_specs=[anywhere] * len(arrays),
        scratch_shapes=[pltpu.VMEM(arrays[index].shape, F32) for index in casts]
        + [pltpu.VMEM(arrays[index].shape, BF) for index in casts]
        + [
            pltpu.SemaphoreType.DMA((len(pieces), slots)),
            pltpu.SemaphoreType.DMA((len(pieces), slots)),
            pltpu.SemaphoreType.DMA((len(pieces),)),
            pltpu.SemaphoreType.DMA((len(casts),)),
        ],
        compiler_params=pltpu.CompilerParams(
            collective_id=collective_id,
            has_side_effects=True,
            vmem_limit_bytes=60 * 1024 * 1024,
        ),
        name="gather_weights",
    )(*arrays)


def add_block(total, part):
    total[...] = (total[...].astype(F32) + part[...].astype(F32)).astype(total.dtype)


def add_rows(pairs, count, rows, cols):
    step = rows
    while step * cols > 32768 and step % 32 == 0:
        step //= 2

    def body(index, carry):
        for total, part in pairs:
            for row in range(0, rows, step):
                at = (index, pl.ds(row, step))
                add_block(total.at[at], part.at[at])
        return carry

    lax.fori_loop(0, count, body, 0)


def scatter_stages(
    cube, here, full, variant, source, out, own, parts, send_sem, recv_sem, local_sem, factors=None
):
    dp, seq = here.dp, here.seq
    n = cube.n_seq
    order = dim_order(cube, variant) if full else []
    rows, cols = out.shape
    line_part = parts[-1]
    waits = []
    arrivals = []

    def dims(fixed, kept):
        return tuple(
            fixed[bit] if bit in fixed else kept for bit in reversed(range(1, cube.dp_bits))
        )

    mine = {bit: here.bits[bit] for bit in range(1, cube.dp_bits)}
    settled = dims(mine, None) if full else ()
    lead = (slice(None),) * (cube.dp_bits - 1)
    if factors is None:
        kept = source.at[lead + (here.bits[0],)] if full else source
        local = pltpu.make_async_copy(kept, own, local_sem)

    def halves(core):
        left, right = factors[:2]
        for number, at in enumerate(itertools.product((0, 1), repeat=cube.dp_bits - 1)):
            first = pl.multiple_of((2 * number + core) * (n * rows), 128)
            block = left_outer(left[:, pl.ds(first, n * rows)], right.read())
            yield at, block.reshape(n, rows, cols)

    def push(stage, what, device):
        copy = remote(what, parts[stage], send_sem.at[stage], recv_sem.at[stage], device)
        copy.start()
        waits.append((None, copy))
        arrivals.append(copy)

    base = cube.dp_bits if full else 0

    def line(step, way):
        target = seq + way * (n - 1 - step)
        passes = (target >= 0) & (target < n)
        further = passes & ((seq > 0) if way > 0 else (seq < n - 1))
        slot = n if way < 0 and step == n - 2 else target
        block = own.at[settled + (target,)]
        index = base + 2 * step + (1 if way > 0 else 0)

        def copy():
            return remote(
                block, line_part.at[slot], send_sem.at[index], recv_sem.at[index], (dp, seq + way)
            )

        def arrival():
            at = line_part.at[target]
            return remote(at, at, send_sem.at[index - 2], recv_sem.at[index - 2], (dp, seq - way))

        return target, passes, further, copy, arrival

    def line_step(step):
        for way in (1, -1):
            target, passes, further, copy, arrival = line(step, way)
            if step > 0:

                @pl.when(further)
                def _():
                    arrival().wait_recv()
                    to, of = own.at[settled + (pl.ds(target, 1),)], line_part.at[pl.ds(target, 1)]
                    add_rows([(to, of)], 1, rows, cols)

            pl.when(passes)(lambda: copy().start())
            waits.append((passes, copy))

    def start():
        if factors is not None:
            _, _, ready, ring = factors
            ready()
            buffer = ring()
            for at, block in halves(1 - here.bits[0]):
                buffer[at] = block.astype(buffer.dtype)
            push(0, buffer, (here.flips[0], seq))
            ring(arrivals[0])
            waits.pop()
            return
        local.start()
        if full:
            push(0, source.at[lead + (1 - here.bits[0],)], (here.flips[0], seq))

    def after_dims(stage):
        if stage == 0 and factors is None:
            local.wait()
        arrivals[stage].wait_recv()
        if stage == 0 and factors is not None:
            for at, block in halves(here.bits[0]):
                own[at] = (block + own[at].astype(F32)).astype(own.dtype)
        closed = order[:stage]
        fixed = {bit: mine[bit] for bit in closed}
        open_bits = [bit for bit in reversed(range(1, cube.dp_bits)) if bit not in closed]

        pairs = []
        for values in itertools.product((0, 1), repeat=len(open_bits)):
            to = dims({**fixed, **dict(zip(open_bits, values))}, None)
            pairs.append((own.at[to], parts[stage].at[values]))
        if stage > 0 or factors is None:
            add_rows(pairs, n, rows, cols)
        if stage < len(order):
            bit = order[stage]
            at = dims({**fixed, bit: 1 - mine[bit]}, slice(None)) + (pl.ds(0, n),)
            push(stage + 1, own.at[at], (here.flips[bit], seq))
        else:
            line_step(0)

    def last():
        where = settled + (seq,)

        def sem(way):
            return recv_sem.at[base + 2 * (n - 2) + (1 if way > 0 else 0)]

        @pl.when(seq > 0)
        def _():
            at = line_part.at[seq]
            remote(at, at, send_sem.at[base], sem(1), (dp, seq - 1)).wait_recv()

        @pl.when(seq < n - 1)
        def _():
            at = line_part.at[n]
            remote(at, at, send_sem.at[base], sem(-1), (dp, seq + 1)).wait_recv()

        @pl.when(seq == 0)
        def _():
            out[...] = own[where].astype(F32) + line_part[n].astype(F32)

        @pl.when(seq == n - 1)
        def _():
            out[...] = own[where].astype(F32) + line_part[n - 1].astype(F32)

        @pl.when((seq > 0) & (seq < n - 1))
        def _():
            both = line_part[seq].astype(F32) + line_part[n].astype(F32)
            out[...] = own[where].astype(F32) + both

    stages = [start]
    if full:
        stages += [functools.partial(after_dims, stage) for stage in range(cube.dp_bits)]
    else:

        def begin():
            local.wait()
            line_step(0)

        stages.append(begin)
    stages += [functools.partial(line_step, step) for step in range(1, n - 1)]
    stages.append(last)

    def finish():
        for passes, copy in waits:
            if passes is None:
                copy.wait_send()
            else:
                pl.when(passes)(lambda: copy().wait_send())

    return stages, finish


class Product:
    def __init__(self, left, right, block):
        self.left, self.right, self.dtype = left, right, jnp.dtype(BF)
        self.shape = tuple(block)


class Ring:
    def __init__(self, buffers, depth):
        self.buffers, self.depth, self.copies = buffers, depth, []

    def __call__(self, copy=None):
        if copy is not None:
            self.copies.append(copy)
            return None
        turn = len(self.copies)
        if turn >= self.depth:
            self.copies[turn - self.depth].wait_send()
        return self.buffers.at[turn % self.depth]

    def finish(self):
        for copy in self.copies[-self.depth :]:
            copy.wait_send()


RING = 6


def scatter_kernel(cube, pieces, products, operands, *refs):
    count = 1 + max(piece[0] for piece in pieces)
    arrays = [index for index in range(count) if index not in products]
    ins = dict(zip(arrays, refs))
    refs = refs[len(arrays) :]
    sources, refs = refs[:operands], refs[operands:]
    outs, refs = refs[:count], refs[count:]
    send_sem, recv_sem, local_sem = refs[-3:]
    refs = refs[:-3]
    here = Place(cube)
    ring = None
    if operands:
        held, buffers, load_sem = refs[-2 - operands : -2], refs[-2], refs[-1]
        loads = [
            pltpu.make_async_copy(source, to, load_sem.at[turn])
            for turn, (source, to) in enumerate(zip(sources, held))
        ]
        for copy in loads:
            copy.start()
        ring = Ring(buffers, RING)
        waited = set()

        def ready(places):
            for place in places:
                if place not in waited:
                    loads[place].wait()
                    waited.add(place)

    plans = []
    for index, (array, full, variant, col, cols) in enumerate(pieces):
        cut = (slice(None), pl.ds(col, cols))
        if array in products:
            places = products[array]
            own, taken = refs[0], 1 + cube.dp_bits
            parts, source = refs[:taken], None
            left, right = held[places[0]], held[places[1]]
            factors = (left, ColumnsOf(right, col, cols), functools.partial(ready, places), ring)
        else:
            taken = 2 + (cube.dp_bits if full else 0)
            own, parts, factors = refs[0], refs[1:taken], None
            source = ins[array].at[(slice(None),) * (cube.dp_bits * full + 1) + cut]
        plans.append(
            scatter_stages(
                cube,
                here,
                full,
                variant,
                source,
                outs[array].at[cut],
                own,
                parts,
                send_sem.at[index],
                recv_sem.at[index],
                local_sem.at[index],
                factors,
            )
        )
        refs = refs[taken:]
    meet(cube, here)
    in_slots([stages for stages, _ in plans], 4)
    for _, finish in plans:
        finish()
    if ring is not None:
        ring.finish()


def scatter_shapes(cube, array, full, cols):
    block = (array.shape[-2], cols)
    shapes = []
    if full:
        for stage in range(0 if isinstance(array, Product) else -1, cube.dp_bits):
            lead = (2,) * (cube.dp_bits - 1 - max(stage, 0)) + (cube.n_seq,)
            shapes.append(lead + block)
    else:
        shapes.append((cube.n_seq,) + block)
    shapes.append((cube.n_seq + 1,) + block)
    return shapes


def scatter_group(cube, arrays, kinds, collective_id):
    pieces = cut_columns(kinds, arrays, 0.0, 0.6)
    outs = [jax.ShapeDtypeStruct(array.shape[-2:], F32) for array in arrays]
    scratch = []
    for array, full, _, _, cols in pieces:
        for shape in scatter_shapes(cube, arrays[array], full, cols):
            scratch.append(pltpu.VMEM(shape, arrays[array].dtype))
    given, operands, products = [], [], {}
    for index, array in enumerate(arrays):
        if not isinstance(array, Product):
            given.append(array)
            continue
        for factor in (array.left, array.right):
            if not any(factor is one for one in operands):
                operands.append(factor)
        places = [
            [factor is one for one in operands].index(True) for factor in (array.left, array.right)
        ]
        products[index] = tuple(places)
    if operands:
        scratch += [pltpu.VMEM(one.shape, one.dtype) for one in operands]
        halves = {
            scatter_shapes(cube, arrays[piece[0]], True, piece[4])[0]
            for piece in pieces
            if piece[0] in products
        }
        (half,) = halves
        scratch += [
            pltpu.VMEM((RING,) + half, BF),
            pltpu.SemaphoreType.DMA((len(operands),)),
        ]
    slots = 2 * cube.n_seq + cube.dp_bits
    scratch += [
        pltpu.SemaphoreType.DMA((len(pieces), slots)),
        pltpu.SemaphoreType.DMA((len(pieces), slots)),
        pltpu.SemaphoreType.DMA((len(pieces),)),
    ]
    return pl.pallas_call(
        functools.partial(scatter_kernel, cube, pieces, products, len(operands)),
        out_shape=outs,
        in_specs=[pl.BlockSpec(memory_space=pl.ANY)] * (len(given) + len(operands)),
        out_specs=[pl.BlockSpec(memory_space=pltpu.VMEM)] * len(arrays),
        scratch_shapes=scratch,
        compiler_params=pltpu.CompilerParams(
            collective_id=collective_id,
            has_side_effects=True,
            vmem_limit_bytes=60 * 1024 * 1024,
        ),
        name="scatter_grads",
    )(*given, *operands)


def scatter_all(cube, arrays, kinds, collective_id):
    groups, room = [[]], 0
    for index, (array, full) in enumerate(zip(arrays, kinds)):
        shapes = scatter_shapes(cube, array, full, array.shape[-1])
        need = sum(math.prod(shape) for shape in shapes) * array.dtype.itemsize
        need += 4 * math.prod(array.shape[-2:])
        if groups[-1] and room + need > 54 * 1024 * 1024:
            groups.append([])
            room = 0
        groups[-1].append(index)
        room += need
    sums = []
    for turn, group in enumerate(groups):
        sums += scatter_group(
            cube, [arrays[i] for i in group], [kinds[i] for i in group], collective_id + turn
        )
    return sums


class ColumnsOf:
    def __init__(self, ref, col, cols):
        self.ref, self.at = ref, (slice(None), pl.ds(col, cols))

    def read(self):
        return self.ref[self.at]


def hand_out_kernel(count, parts, *refs):
    sums, vec, part_sum, part_own = refs[:count], refs[count], refs[count + 1], refs[count + 2]
    refs = refs[count + 3 :]
    outs, vec_outs, part_out = refs[:count], refs[count : count + len(parts)], refs[count + len(parts)]
    held, sem = refs[-1 - count : -1], refs[-1]
    ins = [
        pltpu.make_async_copy(one, mid, sem.at[0, turn])
        for turn, (one, mid) in enumerate(zip(sums, held))
    ]
    copies = [
        pltpu.make_async_copy(mid, out, sem.at[1, turn])
        for turn, (mid, out) in enumerate(zip(held, outs))
    ]
    for copy in ins:
        copy.start()
    for row, (size, out) in enumerate(zip(parts, vec_outs)):
        out[...] = vec[row, 0:size]
    part_out[...] = part_own[...] + part_sum[...]
    for before, copy in zip(ins, copies):
        before.wait()
        copy.start()
    for copy in copies:
        copy.wait()


def hand_out(sums, vec, parts, part_sum, part_own):
    anywhere = pl.BlockSpec(memory_space=pl.ANY)
    inside = pl.BlockSpec(memory_space=pltpu.VMEM)
    count = len(sums)
    return pl.pallas_call(
        functools.partial(hand_out_kernel, count, parts),
        out_shape=[jax.ShapeDtypeStruct(one.shape, F32) for one in sums]
        + [jax.ShapeDtypeStruct((size,), F32) for size in parts]
        + [jax.ShapeDtypeStruct(part_sum.shape, F32)],
        in_specs=[anywhere] * count + [inside] * 3,
        out_specs=[anywhere] * count + [inside] * (len(parts) + 1),
        scratch_shapes=[pltpu.VMEM(one.shape, F32) for one in sums]
        + [pltpu.SemaphoreType.DMA((2, count))],
        compiler_params=pltpu.CompilerParams(vmem_limit_bytes=60 * 1024 * 1024),
        name="hand_out",
    )(*sums, vec, part_sum, part_own)


def write_bias(bias, key_ids, query_ids):
    same = key_ids[:, 0:1] == query_ids[0:1, :]
    early = key_ids[:, 1:2] <= query_ids[1:2, :]
    bias[...] = jnp.where(same & early, 0.0, NEG)


def one_head(array, head):
    lane = lax.broadcasted_iota(jnp.int32, array.shape, 1)
    keep = (lane < DH) if head == 0 else (lane >= DH)
    return jnp.where(keep, array, jnp.zeros_like(array))


def attend_kernel(masked, *refs):
    if masked:
        key_ids, query_ids, query_ref, key_ref, value_ref, out_ref, log_ref, bias = refs
        pl.when(pl.program_id(0) == 0)(lambda: write_bias(bias, key_ids[...], query_ids[...]))
    else:
        query_ref, key_ref, value_ref, out_ref, log_ref = refs
    query, key = query_ref[...], key_ref[...]
    value_t = value_ref[...].T
    outs, logs = [], []
    for head in range(2):
        scores = right_trans(key, one_head(query, head))
        if masked:
            scores = scores + bias[...]
        top = jnp.max(scores, axis=0, keepdims=True)
        expon = jnp.exp(scores - top)
        total = jnp.sum(expon, axis=0, keepdims=True)
        got = matmul(value_t[head * DH : (head + 1) * DH], expon.astype(BF))
        outs.append(got * (1.0 / total))
        logs.append(top + jnp.log(total))
    out_ref[...] = jnp.concatenate(outs, axis=0).T.astype(BF)
    log_ref[0] = jnp.concatenate(logs, axis=0)


def attend_back_kernel(masked, *refs):
    if masked:
        key_ids, query_ids, query_ref, key_ref, value_ref, grad_ref, got_ref, log_ref = refs[:8]
        dq_ref, dk_ref, dv_ref, probs, slopes, bias = refs[8:]
        pl.when(pl.program_id(0) == 0)(lambda: write_bias(bias, key_ids[...], query_ids[...]))
    else:
        query_ref, key_ref, value_ref, grad_ref, got_ref, log_ref = refs[:6]
        dq_ref, dk_ref, dv_ref, probs, slopes = refs[6:]
    query, grad = query_ref[...], grad_ref[...]
    keys = key_ref.shape[0]
    key_t = key_ref[...].T
    both = (grad.astype(F32) * got_ref[...].astype(F32)).T
    span = math.gcd(keys, 128)
    dq, dk, dv = [], None, None
    for head in range(2):
        query_head, grad_head = one_head(query, head), one_head(grad, head)
        delta = jnp.sum(both[head * DH : (head + 1) * DH], axis=0, keepdims=True)
        log = log_ref[0, head : head + 1, :]
        for first in range(0, keys, span):
            at = pl.ds(first, span)
            scores = right_trans(key_ref[at, :], query_head)
            if masked:
                scores = scores + bias[at, :]
            prob = jnp.exp(scores - log)
            grad_probs = right_trans(value_ref[at, :], grad_head)
            probs[at, :] = prob.astype(BF)
            slopes[at, :] = (prob * (grad_probs - delta)).astype(BF)
        dq.append(matmul(key_t[head * DH : (head + 1) * DH], slopes[...]))
        dk_head = matmul(slopes[...], query_head)
        dv_head = matmul(probs[...], grad_head)
        dk = dk_head if dk is None else dk + dk_head
        dv = dv_head if dv is None else dv + dv_head
    scale = DH ** (-0.5)
    dq_ref[...] = (jnp.concatenate(dq, axis=0).T.astype(BF).astype(F32) * scale).astype(BF)
    dk_ref[...] = dk.astype(BF)
    dv_ref[...] = dv.astype(BF)


def attend_call(back, ids, arrays):
    rows, width = arrays[0].shape
    keys = arrays[1].shape[0]
    pair = 2 * DH
    steps = width // pair
    masked = ids is not None
    by_query = pl.BlockSpec((rows, pair), lambda i: (0, i))
    by_key = pl.BlockSpec((keys, pair), lambda i: (0, i))
    logs = pl.BlockSpec((1, 2, rows), lambda i: (i, 0, 0))
    in_specs = [by_query, by_key, by_key]
    if masked:
        in_specs = [
            pl.BlockSpec((keys, 2), lambda i: (0, 0)),
            pl.BlockSpec((2, rows), lambda i: (0, 0)),
        ] + in_specs
        arrays = list(ids) + list(arrays)
    log_shape = jax.ShapeDtypeStruct((steps, 2, rows), F32)
    query_shape = jax.ShapeDtypeStruct((rows, width), BF)
    key_shape = jax.ShapeDtypeStruct((keys, width), BF)
    if back:
        in_specs += [by_query, by_query, logs]
        out_specs, out_shape = [by_query, by_key, by_key], [query_shape, key_shape, key_shape]
    else:
        out_specs, out_shape = [by_query, logs], [query_shape, log_shape]
    products = 7 if back else 2
    return pl.pallas_call(
        functools.partial(attend_back_kernel if back else attend_kernel, masked),
        grid=(steps,),
        in_specs=in_specs,
        out_specs=out_specs,
        out_shape=out_shape,
        scratch_shapes=[pltpu.VMEM((keys, rows), BF)] * (2 * back)
        + [pltpu.VMEM((keys, rows), F32)] * masked,
        cost_estimate=pl.CostEstimate(
            flops=2 * products * rows * keys * width,
            bytes_accessed=2 * width * (rows + keys) * products,
            transcendentals=rows * keys * width // DH,
        ),
        compiler_params=pltpu.CompilerParams(vmem_limit_bytes=48 * 1024 * 1024),
        name="attend_back" if back else "attend",
    )(*arrays)


WIDE = 13


def local(
    cube,
    tokens,
    encoded,
    cotangent,
    doc_ids,
    block_ids,
    query_weight,
    key_weight,
    value_weight,
    out_weight,
    query_bias,
    value_bias,
    out_bias,
    first_gain,
    first_shift,
    probe_weight,
    lookup_weight,
    content_weight,
    merge_weight,
    probe_bias,
    content_bias,
    merge_bias,
    second_gain,
    second_shift,
    expand_weight,
    expand_bias,
    reduce_weight,
    reduce_bias,
    third_gain,
    third_shift,
):
    seq_count, local_rows, feat_width = tokens.shape
    assert seq_count == 1
    enc_local = encoded.shape[1]
    scale = DH ** (-0.5)
    flat = tokens.reshape(local_rows, feat_width)
    enc_flat = encoded.reshape(enc_local, feat_width)

    weights = [
        query_weight, key_weight, value_weight, out_weight, probe_weight,
        lookup_weight, content_weight, merge_weight, expand_weight, reduce_weight,
    ]
    vectors = [
        query_bias, value_bias, out_bias, first_gain, first_shift, probe_bias, content_bias,
        merge_bias, second_gain, second_shift, reduce_bias, third_gain, third_shift,
    ]
    part = vectors[0].shape[0]
    long_part = expand_bias.shape[0]
    held = WIDE * part + long_part
    padded = -(-held // 1024) * 1024
    vec_block = (8, padded // 8)
    packed = jnp.concatenate(vectors + [expand_bias, jnp.zeros((padded - held,), F32)])
    blocks = [w.reshape(block_shape(*w.shape)) for w in weights[:9]]
    kinds = [False, False] + [True] * (len(blocks) + 1)
    gathered = gather_all(
        cube,
        [flat, enc_flat] + blocks + [packed.reshape(vec_block)],
        kinds,
        tuple(range(2, 2 + len(blocks))),
        0,
    )
    late, vec_all = lax.optimization_barrier((reduce_weight.astype(BF), gathered[11]))
    reduce_mat = lax.all_gather(late, ("dp", "seq"), axis=0, tiled=True)
    n_dev = cube.n_dev
    tok_all = gathered[0].reshape(cube.n_seq * local_rows, feat_width)
    enc_all = gathered[1].reshape(cube.n_seq * enc_local, feat_width)
    (
        query_mat, key_mat, value_mat, out_mat, probe_mat,
        lookup_mat, content_mat, merge_mat, expand_mat,
    ) = [
        g.reshape(w.shape[0] * n_dev, w.shape[1]) for g, w in zip(gathered[2:11], weights)
    ]
    vec_all = vec_all.reshape(n_dev, padded)
    wide_all = (
        vec_all[:, : WIDE * part].reshape(n_dev, WIDE, part).transpose(1, 0, 2).reshape(WIDE, -1)
    )
    (
        query_vec, value_vec, out_vec, gain_first, shift_first, probe_vec, content_vec,
        merge_vec, gain_second, shift_second, reduce_vec, gain_third, shift_third,
    ) = [wide_all[i] for i in range(WIDE)]
    expand_vec = vec_all[:, WIDE * part : held].reshape(-1)

    offset = lax.axis_index("seq") * local_rows
    query_doc = lax.dynamic_slice_in_dim(doc_ids, offset, local_rows, 1)
    query_block = lax.dynamic_slice_in_dim(block_ids, offset, local_rows, 1)
    ids = (
        jnp.concatenate([doc_ids, block_ids], axis=0).T,
        jnp.concatenate([query_doc, query_block], axis=0),
    )
    token_float = flat.astype(F32)
    queries = ((matmul(flat, query_mat) + query_vec) * scale).astype(BF)
    all_keys = matmul(tok_all, key_mat).astype(BF)
    all_values = (matmul(tok_all, value_mat) + value_vec).astype(BF)
    self_outb, self_logs = attend_call(False, ids, [queries, all_keys, all_values])
    first_sum = token_float + matmul(self_outb, out_mat) + out_vec
    normed_one, inv_one = layer_stats(first_sum)
    stream_one = (normed_one * gain_first + shift_first).astype(BF)
    probe = ((matmul(stream_one, probe_mat) + probe_vec) * scale).astype(BF)
    enc_keys = matmul(enc_all, lookup_mat).astype(BF)
    enc_values = (matmul(enc_all, content_mat) + content_vec).astype(BF)
    cross_outb, cross_logs = attend_call(False, None, [probe, enc_keys, enc_values])
    second_sum = stream_one.astype(F32) + matmul(cross_outb, merge_mat) + merge_vec
    normed_two, inv_two = layer_stats(second_sum)
    stream_two = (normed_two * gain_second + shift_second).astype(BF)
    expanded = matmul(stream_two, expand_mat) + expand_vec
    activated = jax.nn.gelu(expanded, approximate=False).astype(BF)
    third_sum = stream_two.astype(F32) + matmul(activated, reduce_mat) + reduce_vec
    normed_three, inv_three = layer_stats(third_sum)
    output = (normed_three * gain_third + shift_third).astype(BF)

    grad_output = cotangent.reshape(local_rows, feat_width).astype(F32)
    g_shift_third = jnp.sum(grad_output, axis=0)
    g_gain_third = jnp.sum(grad_output * normed_three, axis=0)
    grad_three = layer_back(grad_output * gain_third, normed_three, inv_three)
    reduce_rows = grad_three.astype(BF)
    g_reduce_vec = jnp.sum(grad_three, axis=0)
    g_reduce_mat = left_outer(activated, reduce_rows).astype(BF)
    reduce_part = g_reduce_mat.reshape((cube.n_dp, cube.n_seq) + reduce_weight.shape)
    reduce_part = lax.psum_scatter(reduce_part, "dp", scatter_dimension=0, tiled=True)
    grad_act = right_trans(reduce_rows, reduce_mat)
    slope = 0.5 * (
        1.0 + jax.scipy.special.erf(expanded * INV_ROOT_TWO)
    ) + expanded * DENSITY_CONST * jnp.exp(-0.5 * expanded * expanded)
    grad_expanded = grad_act * slope
    g_expand_vec = jnp.sum(grad_expanded, axis=0)
    expand_rows = grad_expanded.astype(BF)

    def gradient(left, right, weight):
        block = block_shape(*weight.shape)
        if block == weight.shape and cube.n_seq * block[0] % 128 == 0:
            return Product(left, right, block)
        return left_outer(left, right).astype(BF).reshape(cube.lead(True) + block)

    g_expand_mat = gradient(stream_two, expand_rows, expand_weight)
    grad_two = grad_three + right_trans(expand_rows, expand_mat)
    g_shift_second = jnp.sum(grad_two, axis=0)
    g_gain_second = jnp.sum(grad_two * normed_two, axis=0)
    grad_second = layer_back(grad_two * gain_second, normed_two, inv_two)
    merge_rows = grad_second.astype(BF)
    g_merge_vec = jnp.sum(grad_second, axis=0)
    g_merge_mat = gradient(cross_outb, merge_rows, merge_weight)
    grad_cross = right_trans(merge_rows, merge_mat).astype(BF)
    probe_rows, enc_key_rows, enc_value_rows = attend_call(
        True, None, [probe, enc_keys, enc_values, grad_cross, cross_outb, cross_logs]
    )
    g_probe_vec = jnp.sum(probe_rows.astype(F32), axis=0)
    g_probe_mat = gradient(stream_one, probe_rows, probe_weight)
    g_lookup_mat = gradient(enc_all, enc_key_rows, lookup_weight)
    g_content_mat = gradient(enc_all, enc_value_rows, content_weight)
    g_content_vec = jnp.sum(enc_value_rows.astype(F32), axis=0)
    enc_part = right_trans(enc_key_rows, lookup_mat) + right_trans(enc_value_rows, content_mat)
    grad_one = grad_second + right_trans(probe_rows, probe_mat)
    g_shift_first = jnp.sum(grad_one, axis=0)
    g_gain_first = jnp.sum(grad_one * normed_one, axis=0)
    grad_first = layer_back(grad_one * gain_first, normed_one, inv_one)
    out_rows = grad_first.astype(BF)
    g_out_vec = jnp.sum(grad_first, axis=0)
    g_out_mat = gradient(self_outb, out_rows, out_weight)
    grad_self = right_trans(out_rows, out_mat).astype(BF)
    query_rows, key_rows, value_rows = attend_call(
        True, ids, [queries, all_keys, all_values, grad_self, self_outb, self_logs]
    )
    g_query_vec = jnp.sum(query_rows.astype(F32), axis=0)
    g_value_vec = jnp.sum(value_rows.astype(F32), axis=0)
    g_query_mat = gradient(flat, query_rows, query_weight)
    g_key_mat = gradient(tok_all, key_rows, key_weight)
    g_value_mat = gradient(tok_all, value_rows, value_weight)
    tok_part = right_trans(key_rows, key_mat) + right_trans(value_rows, value_mat)
    tok_own = grad_first + right_trans(query_rows, query_mat)
    tok_part, reduce_part = lax.optimization_barrier((tok_part.astype(BF), reduce_part))
    reduce_part = lax.psum_scatter(reduce_part, "seq", scatter_dimension=1, tiled=True)
    reduce_sum = reduce_part.astype(F32)

    wide_grads = jnp.stack(
        [
            g_query_vec, g_value_vec, g_out_vec, g_gain_first, g_shift_first, g_probe_vec, g_content_vec,
            g_merge_vec, g_gain_second, g_shift_second, g_reduce_vec, g_gain_third, g_shift_third,
        ]
    )
    lanes = 128
    vec_grads = jnp.pad(
        wide_grads.reshape(WIDE, n_dev, part).transpose(1, 0, 2), ((0, 0), (0, 0), (0, lanes - part))
    )
    long_row = jnp.pad(g_expand_vec.reshape(n_dev, 1, long_part), ((0, 0), (0, 0), (0, lanes - long_part)))
    vec_grads = jnp.concatenate([vec_grads, long_row, jnp.zeros((n_dev, 2, lanes), F32)], axis=1)
    vec_grads = vec_grads.reshape(cube.lead(True) + (WIDE + 3, lanes))
    mats = [
        g_expand_mat, g_merge_mat, g_probe_mat, g_lookup_mat, g_content_mat, g_out_mat,
        g_query_mat, g_key_mat, g_value_mat,
    ]
    shards = [
        expand_weight, merge_weight, probe_weight, lookup_weight, content_weight, out_weight,
        query_weight, key_weight, value_weight,
    ]
    sums = scatter_all(
        cube,
        [
            enc_part.astype(BF).reshape(cube.n_seq, enc_local, feat_width),
            tok_part.reshape(cube.n_seq, local_rows, feat_width),
        ]
        + mats
        + [vec_grads],
        [False, False] + [True] * (len(mats) + 1),
        1,
    )
    done = hand_out(
        [sums[0]] + list(sums[2:11]), sums[11], (part,) * WIDE + (long_part,), sums[1], tok_own
    )
    encoded_grad = done[0]
    (
        expand_sum, merge_sum, probe_sum, lookup_sum, content_sum, out_sum, query_sum, key_sum, value_sum,
    ) = [one.reshape(w.shape) for one, w in zip(done[1:10], shards)]
    reduce_sum = reduce_sum.reshape(reduce_weight.shape)
    (
        query_vs, value_vs, out_vs, gain1_vs, shift1_vs, probe_vs, content_vs,
        merge_vs, gain2_vs, shift2_vs, reduce_vs, gain3_vs, shift3_vs, expand_vs,
    ) = done[10:24]
    tokens_grad = done[24]
    return (
        output[None],
        tokens_grad[None],
        encoded_grad[None],
        query_sum,
        key_sum,
        value_sum,
        out_sum,
        query_vs,
        value_vs,
        out_vs,
        gain1_vs,
        shift1_vs,
        probe_sum,
        lookup_sum,
        content_sum,
        merge_sum,
        probe_vs,
        content_vs,
        merge_vs,
        gain2_vs,
        shift2_vs,
        expand_sum,
        expand_vs,
        reduce_sum,
        reduce_vs,
        gain3_vs,
        shift3_vs,
    )


def solution(mesh):
    rows = P("dp", "seq", None)
    ids = P("dp", None)
    mat = P(("dp", "seq"), None)
    vec = P(("dp", "seq"))
    return jax.shard_map(
        functools.partial(local, Cube(mesh)),
        mesh=mesh,
        in_specs=(
            (rows, rows, rows, ids, ids)
            + (mat, mat, mat, mat, vec, vec, vec, vec, vec)
            + (mat, mat, mat, mat, vec, vec, vec, vec, vec)
            + (mat, vec, mat, vec, vec, vec)
        ),
        out_specs=(
            (rows, rows, rows)
            + (mat, mat, mat, mat, vec, vec, vec, vec, vec)
            + (mat, mat, mat, mat, vec, vec, vec, vec, vec)
            + (mat, vec, mat, vec, vec, vec)
        ),
        check_vma=False,
    )
```

```python
import functools
import itertools
import math

import jax
import jax.numpy as jnp
from jax import lax
from jax.experimental import pallas as pl
from jax.experimental.pallas import tpu as pltpu
from jax.sharding import PartitionSpec as P

H = 16
DH = 64

EPS = 1e-05
NEG = -1000000000.0
INV_ROOT_TWO = 0.7071067811865476
DENSITY_CONST = 0.3989422804014327
MESH = pl.DeviceIdType.MESH
PIECE = 16384
BF = jnp.bfloat16
F32 = jnp.float32


def matmul(left_arg, right_arg):
    return jnp.dot(left_arg, right_arg, preferred_element_type=F32)


def left_outer(left_arg, right_arg):
    return lax.dot_general(
        left_arg, right_arg, (((0,), (0,)), ((), ())), preferred_element_type=F32
    )


def right_trans(left_arg, right_arg):
    return lax.dot_general(
        left_arg, right_arg, (((1,), (1,)), ((), ())), preferred_element_type=F32
    )


def layer_stats(hidden):
    row_mean = jnp.mean(hidden, axis=-1, keepdims=True)
    centered = hidden - row_mean
    inv_std = lax.rsqrt(jnp.mean(centered * centered, axis=-1, keepdims=True) + EPS)
    return (centered * inv_std, inv_std)


def layer_back(grad_norm, normed, inv_std):
    first_mean = jnp.mean(grad_norm, axis=-1, keepdims=True)
    second_mean = jnp.mean(grad_norm * normed, axis=-1, keepdims=True)
    return inv_std * (grad_norm - first_mean - normed * second_mean)


class Cube:
    def __init__(self, mesh):
        self.n_dp = mesh.shape["dp"]
        self.n_seq = mesh.shape["seq"]
        self.dp_bits = self.n_dp.bit_length() - 1
        assert self.n_dp == 1 << self.dp_bits
        self.n_dev = self.n_dp * self.n_seq

    def lead(self, full):
        return ((2,) * self.dp_bits if full else ()) + (self.n_seq,)


class Place:
    def __init__(self, cube):
        self.dp, self.seq = lax.axis_index("dp"), lax.axis_index("seq")
        self.bits, self.flips = [], []
        rest = self.dp
        for bit in range(cube.dp_bits):
            half = rest // 2
            self.bits.append(rest - 2 * half)
            self.flips.append(self.dp + (1 << bit) * (1 - 2 * self.bits[-1]))
            rest = half


def block_shape(rows, cols):
    if rows % 16 == 0:
        return (rows, cols)
    return (16, rows * cols // 16)


def dim_order(cube, variant):
    bits = list(range(1, cube.dp_bits))
    return bits if variant == 0 else bits[::-1]


def meet(cube, here):
    dp, seq = here.dp, here.seq
    barrier = pltpu.get_barrier_semaphore()

    def greet(device):
        pl.semaphore_signal(barrier, inc=1, device_id=device, device_id_type=MESH)

    for bit in range(cube.dp_bits):
        greet((here.flips[bit], seq))
    greet((dp, lax.rem(seq + 1, cube.n_seq)))
    greet((dp, lax.rem(seq + cube.n_seq - 1, cube.n_seq)))
    pl.semaphore_wait(barrier, cube.dp_bits + 2)


def in_slots(pieces, lag):
    depth = max(len(stages) for stages in pieces)
    for slot in range(len(pieces) + lag * (depth - 1)):
        for k in reversed(range(depth)):
            p = slot - lag * k
            if 0 <= p < len(pieces) and k < len(pieces[p]):
                pieces[p][k]()


def remote(source, target, send_sem, recv_sem, device):
    return pltpu.make_async_remote_copy(
        src_ref=source,
        dst_ref=target,
        send_sem=send_sem,
        recv_sem=recv_sem,
        device_id=device,
        device_id_type=MESH,
    )


def gather_stages(cube, here, full, variant, source, target, send_sem, recv_sem, local_sem):
    dp, seq = here.dp, here.seq
    n = cube.n_seq
    order = dim_order(cube, variant)
    every = pl.ds(0, n)
    waits = []

    def region(open_bits, fixed, seq_part):
        if not full:
            return (seq_part,)
        places = []
        for bit in reversed(range(cube.dp_bits)):
            if bit in open_bits:
                places.append(slice(None))
            else:
                places.append(fixed.get(bit, here.bits[bit]))
        return tuple(places) + (seq_part,)

    def move(place, slot, device):
        at = target.at[place]
        return remote(at, at, send_sem.at[slot], recv_sem.at[slot], device)

    own = pltpu.make_async_copy(source, target.at[region((), {}, seq)], local_sem)

    def line(step, way):
        slot = 2 * step + (1 if way > 0 else 0)
        block = seq - way * step
        inside = (seq + way >= 0) & (seq + way < n)
        sends = inside & (block >= 0) & (block < n)
        copy = lambda: move(region((), {}, block), slot, (dp, seq + way))
        came = seq - way * (step + 1)
        gets = (came >= 0) & (came < n)
        arrival = lambda: move(region((), {}, came), slot, (dp, seq - way))
        return sends, copy, gets, arrival

    def line_start(step):
        for way in (1, -1):
            sends, copy, _, _ = line(step, way)
            pl.when(sends)(lambda: copy().start())
            waits.append((sends, copy))

    def line_wait(step):
        for way in (1, -1):
            _, _, gets, arrival = line(step, way)
            pl.when(gets)(lambda: arrival().wait_recv())

    base = 2 * (n - 1)
    cores, arrivals = [], []

    def dims_start(stage):
        if stage < len(order):
            copy = move(
                region(order[:stage], {}, every), base + 2 * stage, (here.flips[order[stage]], seq)
            )
            copy.start()
            waits.append((None, copy))
            arrivals.append(copy)
        if stage == 0:
            fresh = region((), {}, every)
        else:
            last = order[stage - 1]
            fresh = region(order[: stage - 1], {last: 1 - here.bits[last]}, every)
        copy = move(fresh, base + 2 * stage + 1, (here.flips[0], seq))
        copy.start()
        waits.append((None, copy))
        cores.append(copy)

    def first():
        own.wait()
        line_start(0)

    stages = [first]
    for step in range(n - 1):

        def after_line(step=step):
            line_wait(step)
            if step < n - 2:
                line_start(step + 1)
            elif full:
                dims_start(0)

        stages.append(after_line)
    if full:
        for stage in range(len(order)):

            def after_dims(stage=stage):
                arrivals[stage].wait_recv()
                dims_start(stage + 1)

            stages.append(after_dims)

        def last():
            for copy in cores:
                copy.wait_recv()

        stages.append(last)

    def finish():
        for sends, copy in waits:
            if sends is None:
                copy.wait_send()
            else:
                pl.when(sends)(lambda: copy().wait_send())

    return own, stages, finish


def gather_slots(cube):
    return 2 * (cube.n_seq - 1) + 2 * cube.dp_bits


def gather_kernel(cube, pieces, casts, *refs):
    count = 1 + max(piece[0] for piece in pieces)
    ins, stays, outs, stays_out = list(refs[:count]), refs[count], refs[count + 1 : -6][:count], refs[2 * count + 1]
    rest = refs[2 * count + 2 : -6]
    wide, stage = rest[: len(casts)], rest[len(casts) :]
    stays_wide, stays_narrow, send_sem, recv_sem, local_sem, cast_sem = refs[-6:]
    here = Place(cube)
    stays_in = pltpu.make_async_copy(stays, stays_wide, cast_sem.at[len(casts)])
    stays_back = pltpu.make_async_copy(stays_narrow, stays_out, cast_sem.at[len(casts) + 1])
    loads = [
        pltpu.make_async_copy(ins[array], held, cast_sem.at[turn])
        for turn, (array, held) in enumerate(zip(casts, wide))
    ]
    for copy in loads:
        copy.start()
    for array, copy, held, narrow in zip(casts, loads, wide, stage):
        copy.wait()
        narrow[...] = held[...].astype(BF)
        ins[array] = narrow
    plans = []
    for index, (array, full, variant, col, cols) in enumerate(pieces):
        lead = cube.dp_bits * full + 1
        cut = (slice(None), pl.ds(col, cols))
        plans.append(
            gather_stages(
                cube,
                here,
                full,
                variant,
                ins[array].at[cut],
                outs[array].at[(slice(None),) * lead + cut],
                send_sem.at[index],
                recv_sem.at[index],
                local_sem.at[index],
            )
        )
    for own, _, _ in plans:
        own.start()
    stays_in.start()
    meet(cube, here)
    in_slots([stages for _, stages, _ in plans], 3)
    stays_in.wait()
    stays_narrow[...] = stays_wide[...].astype(BF)
    stays_back.start()
    for _, _, finish in plans:
        finish()
    stays_back.wait()


def cut_columns(kinds, arrays, first, last):
    whole, along = [], []
    for index, (full, array) in enumerate(zip(kinds, arrays)):
        cols = array.shape[-1]
        count = max(1, math.prod(array.shape[-2:]) // (PIECE if full else PIECE))
        while cols % (128 * count):
            count //= 2
        width = cols // count
        for i in range(count):
            if full:
                whole.append((index, True, len(whole) % 2, width * i, width))
            else:
                along.append((index, False, 0, width * i, width))
    placed = [((i + 0.5) / len(whole), 0, piece) for i, piece in enumerate(whole)]
    reach = (last - first) / max(len(along), 1)
    placed += [(first + (i + 0.5) * reach, 1, piece) for i, piece in enumerate(along)]
    return tuple(piece for _, _, piece in sorted(placed, key=lambda item: item[:2]))


def gather_all(cube, arrays, kinds, casts, stays, collective_id):
    pieces = cut_columns(kinds, arrays, 0.3, 1.0)
    outs = [
        jax.ShapeDtypeStruct(
            cube.lead(full) + array.shape, BF if index in casts else array.dtype
        )
        for index, (array, full) in enumerate(zip(arrays, kinds))
    ]
    slots = gather_slots(cube)
    anywhere = pl.BlockSpec(memory_space=pl.ANY)
    return pl.pallas_call(
        functools.partial(gather_kernel, cube, pieces, casts),
        out_shape=outs + [jax.ShapeDtypeStruct(stays.shape, BF)],
        in_specs=[anywhere] * (len(arrays) + 1),
        out_specs=[anywhere] * (len(arrays) + 1),
        scratch_shapes=[pltpu.VMEM(arrays[index].shape, F32) for index in casts]
        + [pltpu.VMEM(arrays[index].shape, BF) for index in casts]
        + [pltpu.VMEM(stays.shape, F32), pltpu.VMEM(stays.shape, BF)]
        + [
            pltpu.SemaphoreType.DMA((len(pieces), slots)),
            pltpu.SemaphoreType.DMA((len(pieces), slots)),
            pltpu.SemaphoreType.DMA((len(pieces),)),
            pltpu.SemaphoreType.DMA((len(casts) + 2,)),
        ],
        compiler_params=pltpu.CompilerParams(
            collective_id=collective_id,
            has_side_effects=True,
            vmem_limit_bytes=60 * 1024 * 1024,
        ),
        name="gather_weights",
    )(*arrays, stays)


def add_block(total, part):
    total[...] = (total[...].astype(F32) + part[...].astype(F32)).astype(total.dtype)


def add_rows(pairs, count, rows, cols):
    step = rows
    while step * cols > 32768 and step % 32 == 0:
        step //= 2

    def body(index, carry):
        for total, part in pairs:
            for row in range(0, rows, step):
                at = (index, pl.ds(row, step))
                add_block(total.at[at], part.at[at])
        return carry

    lax.fori_loop(0, count, body, 0)


def scatter_stages(
    cube, here, full, variant, source, out, own, parts, send_sem, recv_sem, local_sem, factors=None
):
    dp, seq = here.dp, here.seq
    n = cube.n_seq
    order = dim_order(cube, variant) if full else []
    rows, cols = out.shape
    line_part = parts[-1]
    waits = []
    arrivals = []

    def dims(fixed, kept):
        return tuple(
            fixed[bit] if bit in fixed else kept for bit in reversed(range(1, cube.dp_bits))
        )

    mine = {bit: here.bits[bit] for bit in range(1, cube.dp_bits)}
    settled = dims(mine, None) if full else ()
    lead = (slice(None),) * (cube.dp_bits - 1)
    if factors is None:
        kept = source.at[lead + (here.bits[0],)] if full else source
        local = pltpu.make_async_copy(kept, own, local_sem)

    def halves(core):
        left, right = factors[:2]
        for number, at in enumerate(itertools.product((0, 1), repeat=cube.dp_bits - 1)):
            first = pl.multiple_of((2 * number + core) * (n * rows), 128)
            block = left_outer(left[:, pl.ds(first, n * rows)], right.read())
            yield at, block.reshape(n, rows, cols)

    def push(stage, what, device):
        copy = remote(what, parts[stage], send_sem.at[stage], recv_sem.at[stage], device)
        copy.start()
        waits.append((None, copy))
        arrivals.append(copy)

    base = cube.dp_bits if full else 0

    def line(step, way):
        target = seq + way * (n - 1 - step)
        passes = (target >= 0) & (target < n)
        further = passes & ((seq > 0) if way > 0 else (seq < n - 1))
        slot = n if way < 0 and step == n - 2 else target
        block = own.at[settled + (target,)]
        index = base + 2 * step + (1 if way > 0 else 0)

        def copy():
            return remote(
                block, line_part.at[slot], send_sem.at[index], recv_sem.at[index], (dp, seq + way)
            )

        def arrival():
            at = line_part.at[target]
            return remote(at, at, send_sem.at[index - 2], recv_sem.at[index - 2], (dp, seq - way))

        return target, passes, further, copy, arrival

    def line_step(step):
        for way in (1, -1):
            target, passes, further, copy, arrival = line(step, way)
            if step > 0:

                @pl.when(further)
                def _():
                    arrival().wait_recv()
                    to, of = own.at[settled + (pl.ds(target, 1),)], line_part.at[pl.ds(target, 1)]
                    add_rows([(to, of)], 1, rows, cols)

            pl.when(passes)(lambda: copy().start())
            waits.append((passes, copy))

    def start():
        if factors is not None:
            _, _, ready, ring = factors
            ready()
            buffer = ring()
            for at, block in halves(1 - here.bits[0]):
                buffer[at] = block.astype(buffer.dtype)
            push(0, buffer, (here.flips[0], seq))
            ring(arrivals[0])
            waits.pop()
            return
        local.start()
        if full:
            push(0, source.at[lead + (1 - here.bits[0],)], (here.flips[0], seq))

    def after_dims(stage):
        if stage == 0 and factors is None:
            local.wait()
        arrivals[stage].wait_recv()
        if stage == 0 and factors is not None:
            for at, block in halves(here.bits[0]):
                own[at] = (block + own[at].astype(F32)).astype(own.dtype)
        closed = order[:stage]
        fixed = {bit: mine[bit] for bit in closed}
        open_bits = [bit for bit in reversed(range(1, cube.dp_bits)) if bit not in closed]

        pairs = []
        for values in itertools.product((0, 1), repeat=len(open_bits)):
            to = dims({**fixed, **dict(zip(open_bits, values))}, None)
            pairs.append((own.at[to], parts[stage].at[values]))
        if stage > 0 or factors is None:
            add_rows(pairs, n, rows, cols)
        if stage < len(order):
            bit = order[stage]
            at = dims({**fixed, bit: 1 - mine[bit]}, slice(None)) + (pl.ds(0, n),)
            push(stage + 1, own.at[at], (here.flips[bit], seq))
        else:
            line_step(0)

    def last():
        where = settled + (seq,)

        def sem(way):
            return recv_sem.at[base + 2 * (n - 2) + (1 if way > 0 else 0)]

        @pl.when(seq > 0)
        def _():
            at = line_part.at[seq]
            remote(at, at, send_sem.at[base], sem(1), (dp, seq - 1)).wait_recv()

        @pl.when(seq < n - 1)
        def _():
            at = line_part.at[n]
            remote(at, at, send_sem.at[base], sem(-1), (dp, seq + 1)).wait_recv()

        @pl.when(seq == 0)
        def _():
            out[...] = own[where].astype(F32) + line_part[n].astype(F32)

        @pl.when(seq == n - 1)
        def _():
            out[...] = own[where].astype(F32) + line_part[n - 1].astype(F32)

        @pl.when((seq > 0) & (seq < n - 1))
        def _():
            both = line_part[seq].astype(F32) + line_part[n].astype(F32)
            out[...] = own[where].astype(F32) + both

    stages = [start]
    if full:
        stages += [functools.partial(after_dims, stage) for stage in range(cube.dp_bits)]
    else:

        def begin():
            local.wait()
            line_step(0)

        stages.append(begin)
    stages += [functools.partial(line_step, step) for step in range(1, n - 1)]
    stages.append(last)

    def finish():
        for passes, copy in waits:
            if passes is None:
                copy.wait_send()
            else:
                pl.when(passes)(lambda: copy().wait_send())

    return stages, finish


class Product:
    def __init__(self, left, right, block):
        self.left, self.right, self.dtype = left, right, jnp.dtype(BF)
        self.shape = tuple(block)


class Ring:
    def __init__(self, buffers, depth):
        self.buffers, self.depth, self.copies = buffers, depth, []

    def __call__(self, copy=None):
        if copy is not None:
            self.copies.append(copy)
            return None
        turn = len(self.copies)
        if turn >= self.depth:
            self.copies[turn - self.depth].wait_send()
        return self.buffers.at[turn % self.depth]

    def finish(self):
        for copy in self.copies[-self.depth :]:
            copy.wait_send()


RING = 6


def scatter_kernel(cube, pieces, products, operands, *refs):
    count = 1 + max(piece[0] for piece in pieces)
    arrays = [index for index in range(count) if index not in products]
    ins = dict(zip(arrays, refs))
    refs = refs[len(arrays) :]
    sources, refs = refs[:operands], refs[operands:]
    outs, refs = refs[:count], refs[count:]
    send_sem, recv_sem, local_sem = refs[-3:]
    refs = refs[:-3]
    here = Place(cube)
    ring = None
    if operands:
        held, buffers, load_sem = refs[-2 - operands : -2], refs[-2], refs[-1]
        loads = [
            pltpu.make_async_copy(source, to, load_sem.at[turn])
            for turn, (source, to) in enumerate(zip(sources, held))
        ]
        for copy in loads:
            copy.start()
        ring = Ring(buffers, RING)
        waited = set()

        def ready(places):
            for place in places:
                if place not in waited:
                    loads[place].wait()
                    waited.add(place)

    plans = []
    for index, (array, full, variant, col, cols) in enumerate(pieces):
        cut = (slice(None), pl.ds(col, cols))
        if array in products:
            places = products[array]
            own, taken = refs[0], 1 + cube.dp_bits
            parts, source = refs[:taken], None
            left, right = held[places[0]], held[places[1]]
            factors = (left, ColumnsOf(right, col, cols), functools.partial(ready, places), ring)
        else:
            taken = 2 + (cube.dp_bits if full else 0)
            own, parts, factors = refs[0], refs[1:taken], None
            source = ins[array].at[(slice(None),) * (cube.dp_bits * full + 1) + cut]
        plans.append(
            scatter_stages(
                cube,
                here,
                full,
                variant,
                source,
                outs[array].at[cut],
                own,
                parts,
                send_sem.at[index],
                recv_sem.at[index],
                local_sem.at[index],
                factors,
            )
        )
        refs = refs[taken:]
    meet(cube, here)
    in_slots([stages for stages, _ in plans], 4)
    for _, finish in plans:
        finish()
    if ring is not None:
        ring.finish()


def scatter_shapes(cube, array, full, cols):
    block = (array.shape[-2], cols)
    shapes = []
    if full:
        for stage in range(0 if isinstance(array, Product) else -1, cube.dp_bits):
            lead = (2,) * (cube.dp_bits - 1 - max(stage, 0)) + (cube.n_seq,)
            shapes.append(lead + block)
    else:
        shapes.append((cube.n_seq,) + block)
    shapes.append((cube.n_seq + 1,) + block)
    return shapes


def scatter_group(cube, arrays, kinds, collective_id):
    pieces = cut_columns(kinds, arrays, 0.0, 0.6)
    outs = [jax.ShapeDtypeStruct(array.shape[-2:], F32) for array in arrays]
    scratch = []
    for array, full, _, _, cols in pieces:
        for shape in scatter_shapes(cube, arrays[array], full, cols):
            scratch.append(pltpu.VMEM(shape, arrays[array].dtype))
    given, operands, products = [], [], {}
    for index, array in enumerate(arrays):
        if not isinstance(array, Product):
            given.append(array)
            continue
        for factor in (array.left, array.right):
            if not any(factor is one for one in operands):
                operands.append(factor)
        places = [
            [factor is one for one in operands].index(True) for factor in (array.left, array.right)
        ]
        products[index] = tuple(places)
    if operands:
        scratch += [pltpu.VMEM(one.shape, one.dtype) for one in operands]
        halves = {
            scatter_shapes(cube, arrays[piece[0]], True, piece[4])[0]
            for piece in pieces
            if piece[0] in products
        }
        (half,) = halves
        scratch += [
            pltpu.VMEM((RING,) + half, BF),
            pltpu.SemaphoreType.DMA((len(operands),)),
        ]
    slots = 2 * cube.n_seq + cube.dp_bits
    scratch += [
        pltpu.SemaphoreType.DMA((len(pieces), slots)),
        pltpu.SemaphoreType.DMA((len(pieces), slots)),
        pltpu.SemaphoreType.DMA((len(pieces),)),
    ]
    return pl.pallas_call(
        functools.partial(scatter_kernel, cube, pieces, products, len(operands)),
        out_shape=outs,
        in_specs=[pl.BlockSpec(memory_space=pl.ANY)] * (len(given) + len(operands)),
        out_specs=[pl.BlockSpec(memory_space=pltpu.VMEM)] * len(arrays),
        scratch_shapes=scratch,
        compiler_params=pltpu.CompilerParams(
            collective_id=collective_id,
            has_side_effects=True,
            vmem_limit_bytes=60 * 1024 * 1024,
        ),
        name="scatter_grads",
    )(*given, *operands)


def scatter_all(cube, arrays, kinds, collective_id):
    groups, room = [[]], 0
    for index, (array, full) in enumerate(zip(arrays, kinds)):
        shapes = scatter_shapes(cube, array, full, array.shape[-1])
        need = sum(math.prod(shape) for shape in shapes) * array.dtype.itemsize
        need += 4 * math.prod(array.shape[-2:])
        if groups[-1] and room + need > 54 * 1024 * 1024:
            groups.append([])
            room = 0
        groups[-1].append(index)
        room += need
    sums = []
    for turn, group in enumerate(groups):
        sums += scatter_group(
            cube, [arrays[i] for i in group], [kinds[i] for i in group], collective_id + turn
        )
    return sums


class ColumnsOf:
    def __init__(self, ref, col, cols):
        self.ref, self.at = ref, (slice(None), pl.ds(col, cols))

    def read(self):
        return self.ref[self.at]


def hand_out_kernel(count, parts, *refs):
    sums, vec, part_sum, part_own, narrow = refs[:count], *refs[count : count + 4]
    refs = refs[count + 4 :]
    outs, vec_outs, refs = refs[:count], refs[count : count + len(parts)], refs[count + len(parts) :]
    part_out, wide = refs[:2]
    held, sem = refs[-1 - count : -1], refs[-1]
    ins = [
        pltpu.make_async_copy(one, mid, sem.at[0, turn])
        for turn, (one, mid) in enumerate(zip(sums, held))
    ]
    copies = [
        pltpu.make_async_copy(mid, out, sem.at[1, turn])
        for turn, (mid, out) in enumerate(zip(held, outs))
    ]
    for copy in ins:
        copy.start()
    for row, (size, out) in enumerate(zip(parts, vec_outs)):
        out[...] = vec[row, 0:size]
    part_out[...] = part_own[...] + part_sum[...]
    wide[...] = narrow[...].astype(F32)
    for before, copy in zip(ins, copies):
        before.wait()
        copy.start()
    for copy in copies:
        copy.wait()


def hand_out(sums, vec, parts, part_sum, part_own, narrow):
    anywhere = pl.BlockSpec(memory_space=pl.ANY)
    inside = pl.BlockSpec(memory_space=pltpu.VMEM)
    count = len(sums)
    return pl.pallas_call(
        functools.partial(hand_out_kernel, count, parts),
        out_shape=[jax.ShapeDtypeStruct(one.shape, F32) for one in sums]
        + [jax.ShapeDtypeStruct((size,), F32) for size in parts]
        + [jax.ShapeDtypeStruct(part_sum.shape, F32), jax.ShapeDtypeStruct(narrow.shape, F32)],
        in_specs=[anywhere] * count + [inside] * 4,
        out_specs=[anywhere] * count + [inside] * (len(parts) + 2),
        scratch_shapes=[pltpu.VMEM(one.shape, F32) for one in sums]
        + [pltpu.SemaphoreType.DMA((2, count))],
        compiler_params=pltpu.CompilerParams(vmem_limit_bytes=60 * 1024 * 1024),
        name="hand_out",
    )(*sums, vec, part_sum, part_own, narrow)


def write_bias(bias, key_ids, query_ids):
    same = key_ids[:, 0:1] == query_ids[0:1, :]
    early = key_ids[:, 1:2] <= query_ids[1:2, :]
    bias[...] = jnp.where(same & early, 0.0, NEG)


def one_head(array, head):
    lane = lax.broadcasted_iota(jnp.int32, array.shape, 1)
    keep = (lane < DH) if head == 0 else (lane >= DH)
    return jnp.where(keep, array, jnp.zeros_like(array))


def attend_kernel(masked, *refs):
    if masked:
        key_ids, query_ids, query_ref, key_ref, value_ref, out_ref, log_ref, bias = refs
        pl.when(pl.program_id(0) == 0)(lambda: write_bias(bias, key_ids[...], query_ids[...]))
    else:
        query_ref, key_ref, value_ref, out_ref, log_ref = refs
    query, key = query_ref[...], key_ref[...]
    value_t = value_ref[...].T
    outs, logs = [], []
    for head in range(2):
        scores = right_trans(key, one_head(query, head))
        if masked:
            scores = scores + bias[...]
        top = jnp.max(scores, axis=0, keepdims=True)
        expon = jnp.exp(scores - top)
        total = jnp.sum(expon, axis=0, keepdims=True)
        got = matmul(value_t[head * DH : (head + 1) * DH], expon.astype(BF))
        outs.append(got * (1.0 / total))
        logs.append(top + jnp.log(total))
    out_ref[...] = jnp.concatenate(outs, axis=0).T.astype(BF)
    log_ref[0] = jnp.concatenate(logs, axis=0)


def attend_back_kernel(masked, *refs):
    if masked:
        key_ids, query_ids, query_ref, key_ref, value_ref, grad_ref, got_ref, log_ref = refs[:8]
        dq_ref, dk_ref, dv_ref, probs, slopes, bias = refs[8:]
        pl.when(pl.program_id(0) == 0)(lambda: write_bias(bias, key_ids[...], query_ids[...]))
    else:
        query_ref, key_ref, value_ref, grad_ref, got_ref, log_ref = refs[:6]
        dq_ref, dk_ref, dv_ref, probs, slopes = refs[6:]
    query, grad = query_ref[...], grad_ref[...]
    keys = key_ref.shape[0]
    key_t = key_ref[...].T
    both = (grad.astype(F32) * got_ref[...].astype(F32)).T
    span = math.gcd(keys, 128)
    dq, dk, dv = [], None, None
    for head in range(2):
        query_head, grad_head = one_head(query, head), one_head(grad, head)
        delta = jnp.sum(both[head * DH : (head + 1) * DH], axis=0, keepdims=True)
        log = log_ref[0, head : head + 1, :]
        for first in range(0, keys, span):
            at = pl.ds(first, span)
            scores = right_trans(key_ref[at, :], query_head)
            if masked:
                scores = scores + bias[at, :]
            prob = jnp.exp(scores - log)
            grad_probs = right_trans(value_ref[at, :], grad_head)
            probs[at, :] = prob.astype(BF)
            slopes[at, :] = (prob * (grad_probs - delta)).astype(BF)
        dq.append(matmul(key_t[head * DH : (head + 1) * DH], slopes[...]))
        dk_head = matmul(slopes[...], query_head)
        dv_head = matmul(probs[...], grad_head)
        dk = dk_head if dk is None else dk + dk_head
        dv = dv_head if dv is None else dv + dv_head
    scale = DH ** (-0.5)
    dq_ref[...] = (jnp.concatenate(dq, axis=0).T.astype(BF).astype(F32) * scale).astype(BF)
    dk_ref[...] = dk.astype(BF)
    dv_ref[...] = dv.astype(BF)


def attend_call(back, ids, arrays):
    rows, width = arrays[0].shape
    keys = arrays[1].shape[0]
    pair = 2 * DH
    steps = width // pair
    masked = ids is not None
    by_query = pl.BlockSpec((rows, pair), lambda i: (0, i))
    by_key = pl.BlockSpec((keys, pair), lambda i: (0, i))
    logs = pl.BlockSpec((1, 2, rows), lambda i: (i, 0, 0))
    in_specs = [by_query, by_key, by_key]
    if masked:
        in_specs = [
            pl.BlockSpec((keys, 2), lambda i: (0, 0)),
            pl.BlockSpec((2, rows), lambda i: (0, 0)),
        ] + in_specs
        arrays = list(ids) + list(arrays)
    log_shape = jax.ShapeDtypeStruct((steps, 2, rows), F32)
    query_shape = jax.ShapeDtypeStruct((rows, width), BF)
    key_shape = jax.ShapeDtypeStruct((keys, width), BF)
    if back:
        in_specs += [by_query, by_query, logs]
        out_specs, out_shape = [by_query, by_key, by_key], [query_shape, key_shape, key_shape]
    else:
        out_specs, out_shape = [by_query, logs], [query_shape, log_shape]
    products = 7 if back else 2
    return pl.pallas_call(
        functools.partial(attend_back_kernel if back else attend_kernel, masked),
        grid=(steps,),
        in_specs=in_specs,
        out_specs=out_specs,
        out_shape=out_shape,
        scratch_shapes=[pltpu.VMEM((keys, rows), BF)] * (2 * back)
        + [pltpu.VMEM((keys, rows), F32)] * masked,
        cost_estimate=pl.CostEstimate(
            flops=2 * products * rows * keys * width,
            bytes_accessed=2 * width * (rows + keys) * products,
            transcendentals=rows * keys * width // DH,
        ),
        compiler_params=pltpu.CompilerParams(vmem_limit_bytes=48 * 1024 * 1024),
        name="attend_back" if back else "attend",
    )(*arrays)


def close_kernel(steps, act_ref, weight_ref, stream_ref, cot_ref, vec_ref, *refs):
    out_ref, grad_ref, rows_ref, sums_ref, weight_grad_ref, total = refs
    step = pl.program_id(0)
    span = act_ref.shape[1] // steps

    def columns(index):
        return act_ref[:, pl.ds(pl.multiple_of(index * span, span), span)]

    @pl.when(step == 0)
    def _():
        total[...] = stream_ref[...].astype(F32) + vec_ref[0:1, :]

    @pl.when(step < steps)
    def _():
        total[...] += matmul(columns(step), weight_ref[...])

    @pl.when(step == steps - 1)
    def _():
        normed, inv_std = layer_stats(total[...])
        gain = vec_ref[1:2, :]
        out_ref[...] = (normed * gain + vec_ref[2:3, :]).astype(BF)
        cot = cot_ref[...].astype(F32)
        grad = layer_back(cot * gain, normed, inv_std)
        grad_ref[...] = grad
        rows_ref[...] = grad.astype(BF)
        sums_ref[0:1, :] = jnp.sum(cot, axis=0, keepdims=True)
        sums_ref[1:2, :] = jnp.sum(cot * normed, axis=0, keepdims=True)
        sums_ref[2:3, :] = jnp.sum(grad, axis=0, keepdims=True)

    @pl.when(step >= steps)
    def _():
        weight_grad_ref[...] = left_outer(columns(step - steps), rows_ref[...]).astype(BF)


def close_layer(activated, weight, stream, cotangent, bias, gain, shift):
    rows, hidden = activated.shape
    width = stream.shape[1]
    steps = 4
    whole = lambda shape: pl.BlockSpec(shape, lambda i: (0, 0))
    vecs = jnp.stack([bias, gain, shift])
    return pl.pallas_call(
        functools.partial(close_kernel, steps),
        grid=(2 * steps,),
        in_specs=[
            whole((rows, hidden)),
            pl.BlockSpec((hidden // steps, width), lambda i: (jnp.minimum(i, steps - 1), 0)),
            whole((rows, width)),
            whole((rows, width)),
            whole((3, width)),
        ],
        out_specs=[
            whole((rows, width)),
            whole((rows, width)),
            whole((rows, width)),
            whole((3, width)),
            pl.BlockSpec((hidden // steps, width), lambda i: (jnp.maximum(i - steps, 0), 0)),
        ],
        out_shape=[
            jax.ShapeDtypeStruct((rows, width), BF),
            jax.ShapeDtypeStruct((rows, width), F32),
            jax.ShapeDtypeStruct((rows, width), BF),
            jax.ShapeDtypeStruct((3, width), F32),
            jax.ShapeDtypeStruct((hidden, width), BF),
        ],
        scratch_shapes=[pltpu.VMEM((rows, width), F32)],
        cost_estimate=pl.CostEstimate(
            flops=4 * rows * hidden * width,
            bytes_accessed=4 * hidden * width + 12 * rows * width,
            transcendentals=rows,
        ),
        compiler_params=pltpu.CompilerParams(vmem_limit_bytes=58 * 1024 * 1024),
        name="close_layer",
    )(activated, weight, stream, cotangent, vecs)


WIDE = 13


def local(
    cube,
    tokens,
    encoded,
    cotangent,
    doc_ids,
    block_ids,
    query_weight,
    key_weight,
    value_weight,
    out_weight,
    query_bias,
    value_bias,
    out_bias,
    first_gain,
    first_shift,
    probe_weight,
    lookup_weight,
    content_weight,
    merge_weight,
    probe_bias,
    content_bias,
    merge_bias,
    second_gain,
    second_shift,
    expand_weight,
    expand_bias,
    reduce_weight,
    reduce_bias,
    third_gain,
    third_shift,
):
    seq_count, local_rows, feat_width = tokens.shape
    assert seq_count == 1
    enc_local = encoded.shape[1]
    scale = DH ** (-0.5)
    flat = tokens.reshape(local_rows, feat_width)
    enc_flat = encoded.reshape(enc_local, feat_width)

    weights = [
        query_weight, key_weight, value_weight, out_weight, probe_weight,
        lookup_weight, content_weight, merge_weight, expand_weight, reduce_weight,
    ]
    vectors = [
        query_bias, value_bias, out_bias, first_gain, first_shift, probe_bias, content_bias,
        merge_bias, second_gain, second_shift, reduce_bias, third_gain, third_shift,
    ]
    part = vectors[0].shape[0]
    long_part = expand_bias.shape[0]
    held = WIDE * part + long_part
    padded = -(-held // 1024) * 1024
    vec_block = (8, padded // 8)
    packed = jnp.concatenate(vectors + [expand_bias, jnp.zeros((padded - held,), F32)])
    blocks = [w.reshape(block_shape(*w.shape)) for w in weights[:9]]
    kinds = [False, False] + [True] * (len(blocks) + 1)
    gathered = gather_all(
        cube,
        [flat, enc_flat] + blocks + [packed.reshape(vec_block)],
        kinds,
        tuple(range(2, 2 + len(blocks))),
        reduce_weight,
        0,
    )
    late, vec_all = lax.optimization_barrier((gathered[12], gathered[11]))
    reduce_mat = lax.all_gather(late, ("dp", "seq"), axis=0, tiled=True)
    n_dev = cube.n_dev
    tok_all = gathered[0].reshape(cube.n_seq * local_rows, feat_width)
    enc_all = gathered[1].reshape(cube.n_seq * enc_local, feat_width)
    (
        query_mat, key_mat, value_mat, out_mat, probe_mat,
        lookup_mat, content_mat, merge_mat, expand_mat,
    ) = [
        g.reshape(w.shape[0] * n_dev, w.shape[1]) for g, w in zip(gathered[2:11], weights)
    ]
    vec_all = vec_all.reshape(n_dev, padded)
    wide_all = (
        vec_all[:, : WIDE * part].reshape(n_dev, WIDE, part).transpose(1, 0, 2).reshape(WIDE, -1)
    )
    (
        query_vec, value_vec, out_vec, gain_first, shift_first, probe_vec, content_vec,
        merge_vec, gain_second, shift_second, reduce_vec, gain_third, shift_third,
    ) = [wide_all[i] for i in range(WIDE)]
    expand_vec = vec_all[:, WIDE * part : held].reshape(-1)

    offset = lax.axis_index("seq") * local_rows
    query_doc = lax.dynamic_slice_in_dim(doc_ids, offset, local_rows, 1)
    query_block = lax.dynamic_slice_in_dim(block_ids, offset, local_rows, 1)
    ids = (
        jnp.concatenate([doc_ids, block_ids], axis=0).T,
        jnp.concatenate([query_doc, query_block], axis=0),
    )
    token_float = flat.astype(F32)
    queries = ((matmul(flat, query_mat) + query_vec) * scale).astype(BF)
    all_keys = matmul(tok_all, key_mat).astype(BF)
    all_values = (matmul(tok_all, value_mat) + value_vec).astype(BF)
    self_outb, self_logs = attend_call(False, ids, [queries, all_keys, all_values])
    first_sum = token_float + matmul(self_outb, out_mat) + out_vec
    normed_one, inv_one = layer_stats(first_sum)
    stream_one = (normed_one * gain_first + shift_first).astype(BF)
    probe = ((matmul(stream_one, probe_mat) + probe_vec) * scale).astype(BF)
    enc_keys = matmul(enc_all, lookup_mat).astype(BF)
    enc_values = (matmul(enc_all, content_mat) + content_vec).astype(BF)
    cross_outb, cross_logs = attend_call(False, None, [probe, enc_keys, enc_values])
    second_sum = stream_one.astype(F32) + matmul(cross_outb, merge_mat) + merge_vec
    normed_two, inv_two = layer_stats(second_sum)
    stream_two = (normed_two * gain_second + shift_second).astype(BF)
    expanded = matmul(stream_two, expand_mat) + expand_vec
    below = 0.5 * (1.0 + jax.scipy.special.erf(expanded * INV_ROOT_TWO))
    activated = (expanded * below).astype(BF)
    slope = below + expanded * DENSITY_CONST * jnp.exp(-0.5 * expanded * expanded)
    slope, activated, reduce_mat = lax.optimization_barrier((slope, activated, reduce_mat))
    output, grad_three, reduce_rows, third_sums, g_reduce_mat = close_layer(
        activated,
        reduce_mat,
        stream_two,
        cotangent.reshape(local_rows, feat_width),
        reduce_vec,
        gain_third,
        shift_third,
    )
    g_shift_third, g_gain_third, g_reduce_vec = third_sums[0], third_sums[1], third_sums[2]
    reduce_part = g_reduce_mat.reshape((cube.n_dp, cube.n_seq) + reduce_weight.shape)
    reduce_part = lax.psum_scatter(reduce_part, "dp", scatter_dimension=0, tiled=True)
    grad_act = right_trans(reduce_rows, reduce_mat)
    grad_expanded = grad_act * slope
    g_expand_vec = jnp.sum(grad_expanded, axis=0)
    expand_rows = grad_expanded.astype(BF)

    def gradient(left, right, weight):
        block = block_shape(*weight.shape)
        if block == weight.shape and cube.n_seq * block[0] % 128 == 0:
            return Product(left, right, block)
        return left_outer(left, right).astype(BF).reshape(cube.lead(True) + block)

    g_expand_mat = gradient(stream_two, expand_rows, expand_weight)
    grad_two = grad_three + right_trans(expand_rows, expand_mat)
    g_shift_second = jnp.sum(grad_two, axis=0)
    g_gain_second = jnp.sum(grad_two * normed_two, axis=0)
    grad_second = layer_back(grad_two * gain_second, normed_two, inv_two)
    merge_rows = grad_second.astype(BF)
    g_merge_vec = jnp.sum(grad_second, axis=0)
    g_merge_mat = gradient(cross_outb, merge_rows, merge_weight)
    grad_cross = right_trans(merge_rows, merge_mat).astype(BF)
    probe_rows, enc_key_rows, enc_value_rows = attend_call(
        True, None, [probe, enc_keys, enc_values, grad_cross, cross_outb, cross_logs]
    )
    g_probe_vec = jnp.sum(probe_rows.astype(F32), axis=0)
    g_probe_mat = gradient(stream_one, probe_rows, probe_weight)
    g_lookup_mat = gradient(enc_all, enc_key_rows, lookup_weight)
    g_content_mat = gradient(enc_all, enc_value_rows, content_weight)
    g_content_vec = jnp.sum(enc_value_rows.astype(F32), axis=0)
    enc_part = right_trans(enc_key_rows, lookup_mat) + right_trans(enc_value_rows, content_mat)
    grad_one = grad_second + right_trans(probe_rows, probe_mat)
    g_shift_first = jnp.sum(grad_one, axis=0)
    g_gain_first = jnp.sum(grad_one * normed_one, axis=0)
    grad_first = layer_back(grad_one * gain_first, normed_one, inv_one)
    out_rows = grad_first.astype(BF)
    g_out_vec = jnp.sum(grad_first, axis=0)
    g_out_mat = gradient(self_outb, out_rows, out_weight)
    grad_self = right_trans(out_rows, out_mat).astype(BF)
    query_rows, key_rows, value_rows = attend_call(
        True, ids, [queries, all_keys, all_values, grad_self, self_outb, self_logs]
    )
    g_query_vec = jnp.sum(query_rows.astype(F32), axis=0)
    g_value_vec = jnp.sum(value_rows.astype(F32), axis=0)
    g_query_mat = gradient(flat, query_rows, query_weight)
    g_key_mat = gradient(tok_all, key_rows, key_weight)
    g_value_mat = gradient(tok_all, value_rows, value_weight)
    tok_part = right_trans(key_rows, key_mat) + right_trans(value_rows, value_mat)
    tok_own = grad_first + right_trans(query_rows, query_mat)
    tok_part = tok_part.astype(BF)
    enc_part = enc_part.astype(BF)

    wide_grads = jnp.stack(
        [
            g_query_vec, g_value_vec, g_out_vec, g_gain_first, g_shift_first, g_probe_vec, g_content_vec,
            g_merge_vec, g_gain_second, g_shift_second, g_reduce_vec, g_gain_third, g_shift_third,
        ]
    )
    lanes = 128
    vec_grads = jnp.pad(
        wide_grads.reshape(WIDE, n_dev, part).transpose(1, 0, 2), ((0, 0), (0, 0), (0, lanes - part))
    )
    long_row = jnp.pad(g_expand_vec.reshape(n_dev, 1, long_part), ((0, 0), (0, 0), (0, lanes - long_part)))
    vec_grads = jnp.concatenate([vec_grads, long_row, jnp.zeros((n_dev, 2, lanes), F32)], axis=1)
    vec_grads = vec_grads.reshape(cube.lead(True) + (WIDE + 3, lanes))
    mats = [
        g_expand_mat, g_merge_mat, g_probe_mat, g_lookup_mat, g_content_mat, g_out_mat,
        g_query_mat, g_key_mat, g_value_mat,
    ]
    shards = [
        expand_weight, merge_weight, probe_weight, lookup_weight, content_weight, out_weight,
        query_weight, key_weight, value_weight,
    ]
    tok_part, enc_part, tok_own, vec_grads, reduce_part = lax.optimization_barrier(
        (tok_part, enc_part, tok_own, vec_grads, reduce_part)
    )
    reduce_part = lax.psum_scatter(reduce_part, "seq", scatter_dimension=1, tiled=True)
    sums = scatter_all(
        cube,
        [
            enc_part.reshape(cube.n_seq, enc_local, feat_width),
            tok_part.reshape(cube.n_seq, local_rows, feat_width),
        ]
        + mats
        + [vec_grads],
        [False, False] + [True] * (len(mats) + 1),
        1,
    )
    done = hand_out(
        [sums[0]] + list(sums[2:11]),
        sums[11],
        (part,) * WIDE + (long_part,),
        sums[1],
        tok_own,
        reduce_part.reshape(reduce_weight.shape),
    )
    encoded_grad = done[0]
    (
        expand_sum, merge_sum, probe_sum, lookup_sum, content_sum, out_sum, query_sum, key_sum, value_sum,
    ) = [one.reshape(w.shape) for one, w in zip(done[1:10], shards)]
    (
        query_vs, value_vs, out_vs, gain1_vs, shift1_vs, probe_vs, content_vs,
        merge_vs, gain2_vs, shift2_vs, reduce_vs, gain3_vs, shift3_vs, expand_vs,
    ) = done[10:24]
    tokens_grad, reduce_sum = done[24:26]
    return (
        output[None],
        tokens_grad[None],
        encoded_grad[None],
        query_sum,
        key_sum,
        value_sum,
        out_sum,
        query_vs,
        value_vs,
        out_vs,
        gain1_vs,
        shift1_vs,
        probe_sum,
        lookup_sum,
        content_sum,
        merge_sum,
        probe_vs,
        content_vs,
        merge_vs,
        gain2_vs,
        shift2_vs,
        expand_sum,
        expand_vs,
        reduce_sum,
        reduce_vs,
        gain3_vs,
        shift3_vs,
    )


def solution(mesh):
    rows = P("dp", "seq", None)
    ids = P("dp", None)
    mat = P(("dp", "seq"), None)
    vec = P(("dp", "seq"))
    return jax.shard_map(
        functools.partial(local, Cube(mesh)),
        mesh=mesh,
        in_specs=(
            (rows, rows, rows, ids, ids)
            + (mat, mat, mat, mat, vec, vec, vec, vec, vec)
            + (mat, mat, mat, mat, vec, vec, vec, vec, vec)
            + (mat, vec, mat, vec, vec, vec)
        ),
        out_specs=(
            (rows, rows, rows)
            + (mat, mat, mat, mat, vec, vec, vec, vec, vec)
            + (mat, mat, mat, mat, vec, vec, vec, vec, vec)
            + (mat, vec, mat, vec, vec, vec)
        ),
        check_vma=False,
    )
```

```python
import functools
import itertools
import math

import jax
import jax.numpy as jnp
from jax import lax
from jax.experimental import pallas as pl
from jax.experimental.pallas import tpu as pltpu
from jax.sharding import PartitionSpec as P

H = 16
DH = 64

EPS = 1e-05
NEG = -1000000000.0
INV_ROOT_TWO = 0.7071067811865476
DENSITY_CONST = 0.3989422804014327
MESH = pl.DeviceIdType.MESH
PIECE = 16384
BF = jnp.bfloat16
F32 = jnp.float32


def matmul(left_arg, right_arg):
    return jnp.dot(left_arg, right_arg, preferred_element_type=F32)


def left_outer(left_arg, right_arg):
    return lax.dot_general(
        left_arg, right_arg, (((0,), (0,)), ((), ())), preferred_element_type=F32
    )


def right_trans(left_arg, right_arg):
    return lax.dot_general(
        left_arg, right_arg, (((1,), (1,)), ((), ())), preferred_element_type=F32
    )


def layer_stats(hidden):
    row_mean = jnp.mean(hidden, axis=-1, keepdims=True)
    centered = hidden - row_mean
    inv_std = lax.rsqrt(jnp.mean(centered * centered, axis=-1, keepdims=True) + EPS)
    return (centered * inv_std, inv_std)


def layer_back(grad_norm, normed, inv_std):
    first_mean = jnp.mean(grad_norm, axis=-1, keepdims=True)
    second_mean = jnp.mean(grad_norm * normed, axis=-1, keepdims=True)
    return inv_std * (grad_norm - first_mean - normed * second_mean)


class Cube:
    def __init__(self, mesh):
        self.n_dp = mesh.shape["dp"]
        self.n_seq = mesh.shape["seq"]
        self.dp_bits = self.n_dp.bit_length() - 1
        assert self.n_dp == 1 << self.dp_bits
        self.n_dev = self.n_dp * self.n_seq

    def lead(self, full):
        return ((2,) * self.dp_bits if full else ()) + (self.n_seq,)


class Place:
    def __init__(self, cube):
        self.dp, self.seq = lax.axis_index("dp"), lax.axis_index("seq")
        self.bits, self.flips = [], []
        rest = self.dp
        for bit in range(cube.dp_bits):
            half = rest // 2
            self.bits.append(rest - 2 * half)
            self.flips.append(self.dp + (1 << bit) * (1 - 2 * self.bits[-1]))
            rest = half


def block_shape(rows, cols):
    if rows % 16 == 0:
        return (rows, cols)
    return (16, rows * cols // 16)


def dim_order(cube, variant):
    bits = list(range(1, cube.dp_bits))
    return bits if variant == 0 else bits[::-1]


def meet(cube, here):
    dp, seq = here.dp, here.seq
    barrier = pltpu.get_barrier_semaphore()

    def greet(device):
        pl.semaphore_signal(barrier, inc=1, device_id=device, device_id_type=MESH)

    for bit in range(cube.dp_bits):
        greet((here.flips[bit], seq))
    greet((dp, lax.rem(seq + 1, cube.n_seq)))
    greet((dp, lax.rem(seq + cube.n_seq - 1, cube.n_seq)))
    pl.semaphore_wait(barrier, cube.dp_bits + 2)


def in_slots(pieces, lag):
    depth = max(len(stages) for stages in pieces)
    for slot in range(len(pieces) + lag * (depth - 1)):
        for k in reversed(range(depth)):
            p = slot - lag * k
            if 0 <= p < len(pieces) and k < len(pieces[p]):
                pieces[p][k]()


def remote(source, target, send_sem, recv_sem, device):
    return pltpu.make_async_remote_copy(
        src_ref=source,
        dst_ref=target,
        send_sem=send_sem,
        recv_sem=recv_sem,
        device_id=device,
        device_id_type=MESH,
    )


def gather_stages(cube, here, full, variant, source, target, send_sem, recv_sem, local_sem):
    dp, seq = here.dp, here.seq
    n = cube.n_seq
    order = dim_order(cube, variant)
    every = pl.ds(0, n)
    waits = []

    def region(open_bits, fixed, seq_part):
        if not full:
            return (seq_part,)
        places = []
        for bit in reversed(range(cube.dp_bits)):
            if bit in open_bits:
                places.append(slice(None))
            else:
                places.append(fixed.get(bit, here.bits[bit]))
        return tuple(places) + (seq_part,)

    def move(place, slot, device):
        at = target.at[place]
        return remote(at, at, send_sem.at[slot], recv_sem.at[slot], device)

    own = pltpu.make_async_copy(source, target.at[region((), {}, seq)], local_sem)

    def line(step, way):
        slot = 2 * step + (1 if way > 0 else 0)
        block = seq - way * step
        inside = (seq + way >= 0) & (seq + way < n)
        sends = inside & (block >= 0) & (block < n)
        copy = lambda: move(region((), {}, block), slot, (dp, seq + way))
        came = seq - way * (step + 1)
        gets = (came >= 0) & (came < n)
        arrival = lambda: move(region((), {}, came), slot, (dp, seq - way))
        return sends, copy, gets, arrival

    def line_start(step):
        for way in (1, -1):
            sends, copy, _, _ = line(step, way)
            pl.when(sends)(lambda: copy().start())
            waits.append((sends, copy))

    def line_wait(step):
        for way in (1, -1):
            _, _, gets, arrival = line(step, way)
            pl.when(gets)(lambda: arrival().wait_recv())

    base = 2 * (n - 1)
    cores, arrivals = [], []

    def dims_start(stage):
        if stage < len(order):
            copy = move(
                region(order[:stage], {}, every), base + 2 * stage, (here.flips[order[stage]], seq)
            )
            copy.start()
            waits.append((None, copy))
            arrivals.append(copy)
        if stage == 0:
            fresh = region((), {}, every)
        else:
            last = order[stage - 1]
            fresh = region(order[: stage - 1], {last: 1 - here.bits[last]}, every)
        copy = move(fresh, base + 2 * stage + 1, (here.flips[0], seq))
        copy.start()
        waits.append((None, copy))
        cores.append(copy)

    def first():
        own.wait()
        line_start(0)

    stages = [first]
    for step in range(n - 1):

        def after_line(step=step):
            line_wait(step)
            if step < n - 2:
                line_start(step + 1)
            elif full:
                dims_start(0)

        stages.append(after_line)
    if full:
        for stage in range(len(order)):

            def after_dims(stage=stage):
                arrivals[stage].wait_recv()
                dims_start(stage + 1)

            stages.append(after_dims)

        def last():
            for copy in cores:
                copy.wait_recv()

        stages.append(last)

    def finish():
        for sends, copy in waits:
            if sends is None:
                copy.wait_send()
            else:
                pl.when(sends)(lambda: copy().wait_send())

    return own, stages, finish


def gather_slots(cube):
    return 2 * (cube.n_seq - 1) + 2 * cube.dp_bits


def gather_kernel(cube, pieces, casts, *refs):
    count = 1 + max(piece[0] for piece in pieces)
    ins, stays, outs, stays_out = list(refs[:count]), refs[count], refs[count + 1 : -6][:count], refs[2 * count + 1]
    rest = refs[2 * count + 2 : -6]
    wide, stage = rest[: len(casts)], rest[len(casts) :]
    stays_wide, stays_narrow, send_sem, recv_sem, local_sem, cast_sem = refs[-6:]
    here = Place(cube)
    stays_in = pltpu.make_async_copy(stays, stays_wide, cast_sem.at[len(casts)])
    stays_back = pltpu.make_async_copy(stays_narrow, stays_out, cast_sem.at[len(casts) + 1])
    loads = [
        pltpu.make_async_copy(ins[array], held, cast_sem.at[turn])
        for turn, (array, held) in enumerate(zip(casts, wide))
    ]
    for copy in loads:
        copy.start()
    for array, copy, held, narrow in zip(casts, loads, wide, stage):
        copy.wait()
        narrow[...] = held[...].astype(BF)
        ins[array] = narrow
    plans = []
    for index, (array, full, variant, col, cols) in enumerate(pieces):
        lead = cube.dp_bits * full + 1
        cut = (slice(None), pl.ds(col, cols))
        plans.append(
            gather_stages(
                cube,
                here,
                full,
                variant,
                ins[array].at[cut],
                outs[array].at[(slice(None),) * lead + cut],
                send_sem.at[index],
                recv_sem.at[index],
                local_sem.at[index],
            )
        )
    for own, _, _ in plans:
        own.start()
    stays_in.start()
    meet(cube, here)
    in_slots([stages for _, stages, _ in plans], 3)
    stays_in.wait()
    stays_narrow[...] = stays_wide[...].astype(BF)
    stays_back.start()
    for _, _, finish in plans:
        finish()
    stays_back.wait()


def cut_columns(kinds, arrays, first, last):
    whole, along = [], []
    for index, (full, array) in enumerate(zip(kinds, arrays)):
        cols = array.shape[-1]
        count = max(1, math.prod(array.shape[-2:]) // (PIECE if full else PIECE))
        while cols % (128 * count):
            count //= 2
        width = cols // count
        for i in range(count):
            if full:
                whole.append((index, True, len(whole) % 2, width * i, width))
            else:
                along.append((index, False, 0, width * i, width))
    placed = [((i + 0.5) / len(whole), 0, piece) for i, piece in enumerate(whole)]
    reach = (last - first) / max(len(along), 1)
    placed += [(first + (i + 0.5) * reach, 1, piece) for i, piece in enumerate(along)]
    return tuple(piece for _, _, piece in sorted(placed, key=lambda item: item[:2]))


def gather_all(cube, arrays, kinds, casts, stays, collective_id):
    pieces = cut_columns(kinds, arrays, 0.4, 1.0)
    outs = [
        jax.ShapeDtypeStruct(
            cube.lead(full) + array.shape, BF if index in casts else array.dtype
        )
        for index, (array, full) in enumerate(zip(arrays, kinds))
    ]
    slots = gather_slots(cube)
    anywhere = pl.BlockSpec(memory_space=pl.ANY)
    return pl.pallas_call(
        functools.partial(gather_kernel, cube, pieces, casts),
        out_shape=outs + [jax.ShapeDtypeStruct(stays.shape, BF)],
        in_specs=[anywhere] * (len(arrays) + 1),
        out_specs=[anywhere] * (len(arrays) + 1),
        scratch_shapes=[pltpu.VMEM(arrays[index].shape, F32) for index in casts]
        + [pltpu.VMEM(arrays[index].shape, BF) for index in casts]
        + [pltpu.VMEM(stays.shape, F32), pltpu.VMEM(stays.shape, BF)]
        + [
            pltpu.SemaphoreType.DMA((len(pieces), slots)),
            pltpu.SemaphoreType.DMA((len(pieces), slots)),
            pltpu.SemaphoreType.DMA((len(pieces),)),
            pltpu.SemaphoreType.DMA((len(casts) + 2,)),
        ],
        compiler_params=pltpu.CompilerParams(
            collective_id=collective_id,
            has_side_effects=True,
            vmem_limit_bytes=60 * 1024 * 1024,
        ),
        name="gather_weights",
    )(*arrays, stays)


def add_block(total, part):
    total[...] = (total[...].astype(F32) + part[...].astype(F32)).astype(total.dtype)


def add_rows(pairs, count, rows, cols):
    step = rows
    while step * cols > 32768 and step % 32 == 0:
        step //= 2

    def body(index, carry):
        for total, part in pairs:
            for row in range(0, rows, step):
                at = (index, pl.ds(row, step))
                add_block(total.at[at], part.at[at])
        return carry

    lax.fori_loop(0, count, body, 0)


def scatter_stages(
    cube, here, full, variant, source, out, own, parts, send_sem, recv_sem, local_sem, factors=None
):
    dp, seq = here.dp, here.seq
    n = cube.n_seq
    order = dim_order(cube, variant) if full else []
    rows, cols = out.shape
    line_part = parts[-1]
    waits = []
    arrivals = []

    def dims(fixed, kept):
        return tuple(
            fixed[bit] if bit in fixed else kept for bit in reversed(range(1, cube.dp_bits))
        )

    mine = {bit: here.bits[bit] for bit in range(1, cube.dp_bits)}
    settled = dims(mine, None) if full else ()
    lead = (slice(None),) * (cube.dp_bits - 1)
    if factors is None:
        kept = source.at[lead + (here.bits[0],)] if full else source
        local = pltpu.make_async_copy(kept, own, local_sem)

    def halves(core):
        left, right = factors[:2]
        for number, at in enumerate(itertools.product((0, 1), repeat=cube.dp_bits - 1)):
            first = pl.multiple_of((2 * number + core) * (n * rows), 128)
            block = left_outer(left[:, pl.ds(first, n * rows)], right.read())
            yield at, block.reshape(n, rows, cols)

    def push(stage, what, device):
        copy = remote(what, parts[stage], send_sem.at[stage], recv_sem.at[stage], device)
        copy.start()
        waits.append((None, copy))
        arrivals.append(copy)

    base = cube.dp_bits if full else 0

    def line(step, way):
        target = seq + way * (n - 1 - step)
        passes = (target >= 0) & (target < n)
        further = passes & ((seq > 0) if way > 0 else (seq < n - 1))
        slot = n if way < 0 and step == n - 2 else target
        block = own.at[settled + (target,)]
        index = base + 2 * step + (1 if way > 0 else 0)

        def copy():
            return remote(
                block, line_part.at[slot], send_sem.at[index], recv_sem.at[index], (dp, seq + way)
            )

        def arrival():
            at = line_part.at[target]
            return remote(at, at, send_sem.at[index - 2], recv_sem.at[index - 2], (dp, seq - way))

        return target, passes, further, copy, arrival

    def line_step(step):
        for way in (1, -1):
            target, passes, further, copy, arrival = line(step, way)
            if step > 0:

                @pl.when(further)
                def _():
                    arrival().wait_recv()
                    to, of = own.at[settled + (pl.ds(target, 1),)], line_part.at[pl.ds(target, 1)]
                    add_rows([(to, of)], 1, rows, cols)

            pl.when(passes)(lambda: copy().start())
            waits.append((passes, copy))

    def start():
        if factors is not None:
            _, _, ready, ring = factors
            ready()
            buffer = ring()
            for at, block in halves(1 - here.bits[0]):
                buffer[at] = block.astype(buffer.dtype)
            push(0, buffer, (here.flips[0], seq))
            ring(arrivals[0])
            waits.pop()
            return
        local.start()
        if full:
            push(0, source.at[lead + (1 - here.bits[0],)], (here.flips[0], seq))

    def after_dims(stage):
        if stage == 0 and factors is None:
            local.wait()
        arrivals[stage].wait_recv()
        if stage == 0 and factors is not None:
            for at, block in halves(here.bits[0]):
                own[at] = (block + own[at].astype(F32)).astype(own.dtype)
        closed = order[:stage]
        fixed = {bit: mine[bit] for bit in closed}
        open_bits = [bit for bit in reversed(range(1, cube.dp_bits)) if bit not in closed]

        pairs = []
        for values in itertools.product((0, 1), repeat=len(open_bits)):
            to = dims({**fixed, **dict(zip(open_bits, values))}, None)
            pairs.append((own.at[to], parts[stage].at[values]))
        if stage > 0 or factors is None:
            add_rows(pairs, n, rows, cols)
        if stage < len(order):
            bit = order[stage]
            at = dims({**fixed, bit: 1 - mine[bit]}, slice(None)) + (pl.ds(0, n),)
            push(stage + 1, own.at[at], (here.flips[bit], seq))
        else:
            line_step(0)

    def last():
        where = settled + (seq,)

        def sem(way):
            return recv_sem.at[base + 2 * (n - 2) + (1 if way > 0 else 0)]

        @pl.when(seq > 0)
        def _():
            at = line_part.at[seq]
            remote(at, at, send_sem.at[base], sem(1), (dp, seq - 1)).wait_recv()

        @pl.when(seq < n - 1)
        def _():
            at = line_part.at[n]
            remote(at, at, send_sem.at[base], sem(-1), (dp, seq + 1)).wait_recv()

        @pl.when(seq == 0)
        def _():
            out[...] = own[where].astype(F32) + line_part[n].astype(F32)

        @pl.when(seq == n - 1)
        def _():
            out[...] = own[where].astype(F32) + line_part[n - 1].astype(F32)

        @pl.when((seq > 0) & (seq < n - 1))
        def _():
            both = line_part[seq].astype(F32) + line_part[n].astype(F32)
            out[...] = own[where].astype(F32) + both

    stages = [start]
    if full:
        stages += [functools.partial(after_dims, stage) for stage in range(cube.dp_bits)]
    else:

        def begin():
            local.wait()
            line_step(0)

        stages.append(begin)
    stages += [functools.partial(line_step, step) for step in range(1, n - 1)]
    stages.append(last)

    def finish():
        for passes, copy in waits:
            if passes is None:
                copy.wait_send()
            else:
                pl.when(passes)(lambda: copy().wait_send())

    return stages, finish


class Product:
    def __init__(self, left, right, block):
        self.left, self.right, self.dtype = left, right, jnp.dtype(BF)
        self.shape = tuple(block)


class Ring:
    def __init__(self, buffers, depth):
        self.buffers, self.depth, self.copies = buffers, depth, []

    def __call__(self, copy=None):
        if copy is not None:
            self.copies.append(copy)
            return None
        turn = len(self.copies)
        if turn >= self.depth:
            self.copies[turn - self.depth].wait_send()
        return self.buffers.at[turn % self.depth]

    def finish(self):
        for copy in self.copies[-self.depth :]:
            copy.wait_send()


RING = 8


def scatter_kernel(cube, pieces, products, operands, *refs):
    count = 1 + max(piece[0] for piece in pieces)
    arrays = [index for index in range(count) if index not in products]
    ins = dict(zip(arrays, refs))
    refs = refs[len(arrays) :]
    sources, refs = refs[:operands], refs[operands:]
    outs, refs = refs[:count], refs[count:]
    send_sem, recv_sem, local_sem = refs[-3:]
    refs = refs[:-3]
    here = Place(cube)
    ring = None
    if operands:
        held, buffers, load_sem = refs[-2 - operands : -2], refs[-2], refs[-1]
        loads = [
            pltpu.make_async_copy(source, to, load_sem.at[turn])
            for turn, (source, to) in enumerate(zip(sources, held))
        ]
        for copy in loads:
            copy.start()
        ring = Ring(buffers, RING)
        waited = set()

        def ready(places):
            for place in places:
                if place not in waited:
                    loads[place].wait()
                    waited.add(place)

    plans = []
    for index, (array, full, variant, col, cols) in enumerate(pieces):
        cut = (slice(None), pl.ds(col, cols))
        if array in products:
            places = products[array]
            own, taken = refs[0], 1 + cube.dp_bits
            parts, source = refs[:taken], None
            left, right = held[places[0]], held[places[1]]
            factors = (left, ColumnsOf(right, col, cols), functools.partial(ready, places), ring)
        else:
            taken = 2 + (cube.dp_bits if full else 0)
            own, parts, factors = refs[0], refs[1:taken], None
            source = ins[array].at[(slice(None),) * (cube.dp_bits * full + 1) + cut]
        plans.append(
            scatter_stages(
                cube,
                here,
                full,
                variant,
                source,
                outs[array].at[cut],
                own,
                parts,
                send_sem.at[index],
                recv_sem.at[index],
                local_sem.at[index],
                factors,
            )
        )
        refs = refs[taken:]
    meet(cube, here)
    in_slots([stages for stages, _ in plans], 6)
    for _, finish in plans:
        finish()
    if ring is not None:
        ring.finish()


def scatter_shapes(cube, array, full, cols):
    block = (array.shape[-2], cols)
    shapes = []
    if full:
        for stage in range(0 if isinstance(array, Product) else -1, cube.dp_bits):
            lead = (2,) * (cube.dp_bits - 1 - max(stage, 0)) + (cube.n_seq,)
            shapes.append(lead + block)
    else:
        shapes.append((cube.n_seq,) + block)
    shapes.append((cube.n_seq + 1,) + block)
    return shapes


def scatter_group(cube, arrays, kinds, collective_id):
    pieces = cut_columns(kinds, arrays, 0.0, 0.7)
    outs = [jax.ShapeDtypeStruct(array.shape[-2:], F32) for array in arrays]
    scratch = []
    for array, full, _, _, cols in pieces:
        for shape in scatter_shapes(cube, arrays[array], full, cols):
            scratch.append(pltpu.VMEM(shape, arrays[array].dtype))
    given, operands, products = [], [], {}
    for index, array in enumerate(arrays):
        if not isinstance(array, Product):
            given.append(array)
            continue
        for factor in (array.left, array.right):
            if not any(factor is one for one in operands):
                operands.append(factor)
        places = [
            [factor is one for one in operands].index(True) for factor in (array.left, array.right)
        ]
        products[index] = tuple(places)
    if operands:
        scratch += [pltpu.VMEM(one.shape, one.dtype) for one in operands]
        halves = {
            scatter_shapes(cube, arrays[piece[0]], True, piece[4])[0]
            for piece in pieces
            if piece[0] in products
        }
        (half,) = halves
        scratch += [
            pltpu.VMEM((RING,) + half, BF),
            pltpu.SemaphoreType.DMA((len(operands),)),
        ]
    slots = 2 * cube.n_seq + cube.dp_bits
    scratch += [
        pltpu.SemaphoreType.DMA((len(pieces), slots)),
        pltpu.SemaphoreType.DMA((len(pieces), slots)),
        pltpu.SemaphoreType.DMA((len(pieces),)),
    ]
    return pl.pallas_call(
        functools.partial(scatter_kernel, cube, pieces, products, len(operands)),
        out_shape=outs,
        in_specs=[pl.BlockSpec(memory_space=pl.ANY)] * (len(given) + len(operands)),
        out_specs=[pl.BlockSpec(memory_space=pltpu.VMEM)] * len(arrays),
        scratch_shapes=scratch,
        compiler_params=pltpu.CompilerParams(
            collective_id=collective_id,
            has_side_effects=True,
            vmem_limit_bytes=60 * 1024 * 1024,
        ),
        name="scatter_grads",
    )(*given, *operands)


def scatter_all(cube, arrays, kinds, collective_id):
    groups, room = [[]], 0
    for index, (array, full) in enumerate(zip(arrays, kinds)):
        shapes = scatter_shapes(cube, array, full, array.shape[-1])
        need = sum(math.prod(shape) for shape in shapes) * array.dtype.itemsize
        need += 4 * math.prod(array.shape[-2:])
        if groups[-1] and room + need > 54 * 1024 * 1024:
            groups.append([])
            room = 0
        groups[-1].append(index)
        room += need
    sums = []
    for turn, group in enumerate(groups):
        sums += scatter_group(
            cube, [arrays[i] for i in group], [kinds[i] for i in group], collective_id + turn
        )
    return sums


class ColumnsOf:
    def __init__(self, ref, col, cols):
        self.ref, self.at = ref, (slice(None), pl.ds(col, cols))

    def read(self):
        return self.ref[self.at]


def hand_out_kernel(count, parts, *refs):
    sums, vec, part_sum, part_own, narrow = refs[:count], *refs[count : count + 4]
    refs = refs[count + 4 :]
    outs, vec_outs, refs = refs[:count], refs[count : count + len(parts)], refs[count + len(parts) :]
    part_out, wide = refs[:2]
    held, sem = refs[-1 - count : -1], refs[-1]
    ins = [
        pltpu.make_async_copy(one, mid, sem.at[0, turn])
        for turn, (one, mid) in enumerate(zip(sums, held))
    ]
    copies = [
        pltpu.make_async_copy(mid, out, sem.at[1, turn])
        for turn, (mid, out) in enumerate(zip(held, outs))
    ]
    for copy in ins:
        copy.start()
    for row, (size, out) in enumerate(zip(parts, vec_outs)):
        out[...] = vec[row, 0:size]
    part_out[...] = part_own[...] + part_sum[...]
    wide[...] = narrow[...].astype(F32)
    for before, copy in zip(ins, copies):
        before.wait()
        copy.start()
    for copy in copies:
        copy.wait()


def hand_out(sums, vec, parts, part_sum, part_own, narrow):
    anywhere = pl.BlockSpec(memory_space=pl.ANY)
    inside = pl.BlockSpec(memory_space=pltpu.VMEM)
    count = len(sums)
    return pl.pallas_call(
        functools.partial(hand_out_kernel, count, parts),
        out_shape=[jax.ShapeDtypeStruct(one.shape, F32) for one in sums]
        + [jax.ShapeDtypeStruct((size,), F32) for size in parts]
        + [jax.ShapeDtypeStruct(part_sum.shape, F32), jax.ShapeDtypeStruct(narrow.shape, F32)],
        in_specs=[anywhere] * count + [inside] * 4,
        out_specs=[anywhere] * count + [inside] * (len(parts) + 2),
        scratch_shapes=[pltpu.VMEM(one.shape, F32) for one in sums]
        + [pltpu.SemaphoreType.DMA((2, count))],
        compiler_params=pltpu.CompilerParams(vmem_limit_bytes=60 * 1024 * 1024),
        name="hand_out",
    )(*sums, vec, part_sum, part_own, narrow)


def write_bias(bias, key_ids, query_ids):
    same = key_ids[:, 0:1] == query_ids[0:1, :]
    early = key_ids[:, 1:2] <= query_ids[1:2, :]
    bias[...] = jnp.where(same & early, 0.0, NEG)


def one_head(array, head):
    lane = lax.broadcasted_iota(jnp.int32, array.shape, 1)
    keep = (lane < DH) if head == 0 else (lane >= DH)
    return jnp.where(keep, array, jnp.zeros_like(array))


def attend_kernel(masked, *refs):
    if masked:
        key_ids, query_ids, query_ref, key_ref, value_ref, out_ref, log_ref, bias = refs
        pl.when(pl.program_id(0) == 0)(lambda: write_bias(bias, key_ids[...], query_ids[...]))
    else:
        query_ref, key_ref, value_ref, out_ref, log_ref = refs
    query, key = query_ref[...], key_ref[...]
    value_t = value_ref[...].T
    outs, logs = [], []
    for head in range(2):
        scores = right_trans(key, one_head(query, head))
        if masked:
            scores = scores + bias[...]
        top = jnp.max(scores, axis=0, keepdims=True)
        expon = jnp.exp(scores - top)
        total = jnp.sum(expon, axis=0, keepdims=True)
        got = matmul(value_t[head * DH : (head + 1) * DH], expon.astype(BF))
        outs.append(got * (1.0 / total))
        logs.append(top + jnp.log(total))
    out_ref[...] = jnp.concatenate(outs, axis=0).T.astype(BF)
    log_ref[0] = jnp.concatenate(logs, axis=0)


def attend_back_kernel(masked, *refs):
    if masked:
        key_ids, query_ids, query_ref, key_ref, value_ref, grad_ref, got_ref, log_ref = refs[:8]
        dq_ref, dk_ref, dv_ref, probs, slopes, bias = refs[8:]
        pl.when(pl.program_id(0) == 0)(lambda: write_bias(bias, key_ids[...], query_ids[...]))
    else:
        query_ref, key_ref, value_ref, grad_ref, got_ref, log_ref = refs[:6]
        dq_ref, dk_ref, dv_ref, probs, slopes = refs[6:]
    query, grad = query_ref[...], grad_ref[...]
    keys = key_ref.shape[0]
    key_t = key_ref[...].T
    both = (grad.astype(F32) * got_ref[...].astype(F32)).T
    span = math.gcd(keys, 128)
    dq, dk, dv = [], None, None
    for head in range(2):
        query_head, grad_head = one_head(query, head), one_head(grad, head)
        delta = jnp.sum(both[head * DH : (head + 1) * DH], axis=0, keepdims=True)
        log = log_ref[0, head : head + 1, :]
        for first in range(0, keys, span):
            at = pl.ds(first, span)
            scores = right_trans(key_ref[at, :], query_head)
            if masked:
                scores = scores + bias[at, :]
            prob = jnp.exp(scores - log)
            grad_probs = right_trans(value_ref[at, :], grad_head)
            probs[at, :] = prob.astype(BF)
            slopes[at, :] = (prob * (grad_probs - delta)).astype(BF)
        dq.append(matmul(key_t[head * DH : (head + 1) * DH], slopes[...]))
        dk_head = matmul(slopes[...], query_head)
        dv_head = matmul(probs[...], grad_head)
        dk = dk_head if dk is None else dk + dk_head
        dv = dv_head if dv is None else dv + dv_head
    scale = DH ** (-0.5)
    dq_ref[...] = (jnp.concatenate(dq, axis=0).T.astype(BF).astype(F32) * scale).astype(BF)
    dk_ref[...] = dk.astype(BF)
    dv_ref[...] = dv.astype(BF)


def attend_call(back, ids, arrays):
    rows, width = arrays[0].shape
    keys = arrays[1].shape[0]
    pair = 2 * DH
    steps = width // pair
    masked = ids is not None
    by_query = pl.BlockSpec((rows, pair), lambda i: (0, i))
    by_key = pl.BlockSpec((keys, pair), lambda i: (0, i))
    logs = pl.BlockSpec((1, 2, rows), lambda i: (i, 0, 0))
    in_specs = [by_query, by_key, by_key]
    if masked:
        in_specs = [
            pl.BlockSpec((keys, 2), lambda i: (0, 0)),
            pl.BlockSpec((2, rows), lambda i: (0, 0)),
        ] + in_specs
        arrays = list(ids) + list(arrays)
    log_shape = jax.ShapeDtypeStruct((steps, 2, rows), F32)
    query_shape = jax.ShapeDtypeStruct((rows, width), BF)
    key_shape = jax.ShapeDtypeStruct((keys, width), BF)
    if back:
        in_specs += [by_query, by_query, logs]
        out_specs, out_shape = [by_query, by_key, by_key], [query_shape, key_shape, key_shape]
    else:
        out_specs, out_shape = [by_query, logs], [query_shape, log_shape]
    products = 7 if back else 2
    return pl.pallas_call(
        functools.partial(attend_back_kernel if back else attend_kernel, masked),
        grid=(steps,),
        in_specs=in_specs,
        out_specs=out_specs,
        out_shape=out_shape,
        scratch_shapes=[pltpu.VMEM((keys, rows), BF)] * (2 * back)
        + [pltpu.VMEM((keys, rows), F32)] * masked,
        cost_estimate=pl.CostEstimate(
            flops=2 * products * rows * keys * width,
            bytes_accessed=2 * width * (rows + keys) * products,
            transcendentals=rows * keys * width // DH,
        ),
        compiler_params=pltpu.CompilerParams(vmem_limit_bytes=48 * 1024 * 1024),
        name="attend_back" if back else "attend",
    )(*arrays)


def close_kernel(steps, act_ref, weight_ref, stream_ref, cot_ref, vec_ref, *refs):
    out_ref, grad_ref, rows_ref, sums_ref, weight_grad_ref, total = refs
    step = pl.program_id(0)
    span = act_ref.shape[1] // steps

    def columns(index):
        return act_ref[:, pl.ds(pl.multiple_of(index * span, span), span)]

    @pl.when(step == 0)
    def _():
        total[...] = stream_ref[...].astype(F32) + vec_ref[0:1, :]

    @pl.when(step < steps)
    def _():
        total[...] += matmul(columns(step), weight_ref[...])

    @pl.when(step == steps - 1)
    def _():
        normed, inv_std = layer_stats(total[...])
        gain = vec_ref[1:2, :]
        out_ref[...] = (normed * gain + vec_ref[2:3, :]).astype(BF)
        cot = cot_ref[...].astype(F32)
        grad = layer_back(cot * gain, normed, inv_std)
        grad_ref[...] = grad
        rows_ref[...] = grad.astype(BF)
        sums_ref[0:1, :] = jnp.sum(cot, axis=0, keepdims=True)
        sums_ref[1:2, :] = jnp.sum(cot * normed, axis=0, keepdims=True)
        sums_ref[2:3, :] = jnp.sum(grad, axis=0, keepdims=True)

    @pl.when(step >= steps)
    def _():
        weight_grad_ref[...] = left_outer(columns(step - steps), rows_ref[...]).astype(BF)


def close_layer(activated, weight, stream, cotangent, bias, gain, shift):
    rows, hidden = activated.shape
    width = stream.shape[1]
    steps = 4
    whole = lambda shape: pl.BlockSpec(shape, lambda i: (0, 0))
    vecs = jnp.stack([bias, gain, shift])
    return pl.pallas_call(
        functools.partial(close_kernel, steps),
        grid=(2 * steps,),
        in_specs=[
            whole((rows, hidden)),
            pl.BlockSpec((hidden // steps, width), lambda i: (jnp.minimum(i, steps - 1), 0)),
            whole((rows, width)),
            whole((rows, width)),
            whole((3, width)),
        ],
        out_specs=[
            whole((rows, width)),
            whole((rows, width)),
            whole((rows, width)),
            whole((3, width)),
            pl.BlockSpec((hidden // steps, width), lambda i: (jnp.maximum(i - steps, 0), 0)),
        ],
        out_shape=[
            jax.ShapeDtypeStruct((rows, width), BF),
            jax.ShapeDtypeStruct((rows, width), F32),
            jax.ShapeDtypeStruct((rows, width), BF),
            jax.ShapeDtypeStruct((3, width), F32),
            jax.ShapeDtypeStruct((hidden, width), BF),
        ],
        scratch_shapes=[pltpu.VMEM((rows, width), F32)],
        cost_estimate=pl.CostEstimate(
            flops=4 * rows * hidden * width,
            bytes_accessed=4 * hidden * width + 12 * rows * width,
            transcendentals=rows,
        ),
        compiler_params=pltpu.CompilerParams(vmem_limit_bytes=58 * 1024 * 1024),
        name="close_layer",
    )(activated, weight, stream, cotangent, vecs)


WIDE = 13


def local(
    cube,
    tokens,
    encoded,
    cotangent,
    doc_ids,
    block_ids,
    query_weight,
    key_weight,
    value_weight,
    out_weight,
    query_bias,
    value_bias,
    out_bias,
    first_gain,
    first_shift,
    probe_weight,
    lookup_weight,
    content_weight,
    merge_weight,
    probe_bias,
    content_bias,
    merge_bias,
    second_gain,
    second_shift,
    expand_weight,
    expand_bias,
    reduce_weight,
    reduce_bias,
    third_gain,
    third_shift,
):
    seq_count, local_rows, feat_width = tokens.shape
    assert seq_count == 1
    enc_local = encoded.shape[1]
    scale = DH ** (-0.5)
    flat = tokens.reshape(local_rows, feat_width)
    enc_flat = encoded.reshape(enc_local, feat_width)

    weights = [
        query_weight, key_weight, value_weight, out_weight, probe_weight,
        lookup_weight, content_weight, merge_weight, expand_weight, reduce_weight,
    ]
    vectors = [
        query_bias, value_bias, out_bias, first_gain, first_shift, probe_bias, content_bias,
        merge_bias, second_gain, second_shift, reduce_bias, third_gain, third_shift,
    ]
    part = vectors[0].shape[0]
    long_part = expand_bias.shape[0]
    held = WIDE * part + long_part
    padded = -(-held // 1024) * 1024
    vec_block = (8, padded // 8)
    packed = jnp.concatenate(vectors + [expand_bias, jnp.zeros((padded - held,), F32)])
    blocks = [w.reshape(block_shape(*w.shape)) for w in weights[:9]]
    kinds = [False, False] + [True] * (len(blocks) + 1)
    gathered = gather_all(
        cube,
        [flat, enc_flat] + blocks + [packed.reshape(vec_block)],
        kinds,
        tuple(range(2, 2 + len(blocks))),
        reduce_weight,
        0,
    )
    late, vec_all = lax.optimization_barrier((gathered[12], gathered[11]))
    reduce_mat = lax.all_gather(late, ("dp", "seq"), axis=0, tiled=True)
    n_dev = cube.n_dev
    tok_all = gathered[0].reshape(cube.n_seq * local_rows, feat_width)
    enc_all = gathered[1].reshape(cube.n_seq * enc_local, feat_width)
    (
        query_mat, key_mat, value_mat, out_mat, probe_mat,
        lookup_mat, content_mat, merge_mat, expand_mat,
    ) = [
        g.reshape(w.shape[0] * n_dev, w.shape[1]) for g, w in zip(gathered[2:11], weights)
    ]
    vec_all = vec_all.reshape(n_dev, padded)
    wide_all = (
        vec_all[:, : WIDE * part].reshape(n_dev, WIDE, part).transpose(1, 0, 2).reshape(WIDE, -1)
    )
    (
        query_vec, value_vec, out_vec, gain_first, shift_first, probe_vec, content_vec,
        merge_vec, gain_second, shift_second, reduce_vec, gain_third, shift_third,
    ) = [wide_all[i] for i in range(WIDE)]
    expand_vec = vec_all[:, WIDE * part : held].reshape(-1)

    offset = lax.axis_index("seq") * local_rows
    query_doc = lax.dynamic_slice_in_dim(doc_ids, offset, local_rows, 1)
    query_block = lax.dynamic_slice_in_dim(block_ids, offset, local_rows, 1)
    ids = (
        jnp.concatenate([doc_ids, block_ids], axis=0).T,
        jnp.concatenate([query_doc, query_block], axis=0),
    )
    token_float = flat.astype(F32)
    queries = ((matmul(flat, query_mat) + query_vec) * scale).astype(BF)
    all_keys = matmul(tok_all, key_mat).astype(BF)
    all_values = (matmul(tok_all, value_mat) + value_vec).astype(BF)
    self_outb, self_logs = attend_call(False, ids, [queries, all_keys, all_values])
    first_sum = token_float + matmul(self_outb, out_mat) + out_vec
    normed_one, inv_one = layer_stats(first_sum)
    stream_one = (normed_one * gain_first + shift_first).astype(BF)
    probe = ((matmul(stream_one, probe_mat) + probe_vec) * scale).astype(BF)
    enc_keys = matmul(enc_all, lookup_mat).astype(BF)
    enc_values = (matmul(enc_all, content_mat) + content_vec).astype(BF)
    cross_outb, cross_logs = attend_call(False, None, [probe, enc_keys, enc_values])
    second_sum = stream_one.astype(F32) + matmul(cross_outb, merge_mat) + merge_vec
    normed_two, inv_two = layer_stats(second_sum)
    stream_two = (normed_two * gain_second + shift_second).astype(BF)
    expanded = matmul(stream_two, expand_mat) + expand_vec
    below = 0.5 * (1.0 + jax.scipy.special.erf(expanded * INV_ROOT_TWO))
    activated = (expanded * below).astype(BF)
    slope = below + expanded * DENSITY_CONST * jnp.exp(-0.5 * expanded * expanded)
    slope, activated, reduce_mat = lax.optimization_barrier((slope, activated, reduce_mat))
    output, grad_three, reduce_rows, third_sums, g_reduce_mat = close_layer(
        activated,
        reduce_mat,
        stream_two,
        cotangent.reshape(local_rows, feat_width),
        reduce_vec,
        gain_third,
        shift_third,
    )
    g_shift_third, g_gain_third, g_reduce_vec = third_sums[0], third_sums[1], third_sums[2]
    reduce_part = g_reduce_mat.reshape((cube.n_dp, cube.n_seq) + reduce_weight.shape)
    reduce_part = lax.psum_scatter(reduce_part, "dp", scatter_dimension=0, tiled=True)
    grad_act = right_trans(reduce_rows, reduce_mat)
    grad_expanded = grad_act * slope
    g_expand_vec = jnp.sum(grad_expanded, axis=0)
    expand_rows = grad_expanded.astype(BF)

    def gradient(left, right, weight):
        block = block_shape(*weight.shape)
        if block == weight.shape and cube.n_seq * block[0] % 128 == 0:
            return Product(left, right, block)
        return left_outer(left, right).astype(BF).reshape(cube.lead(True) + block)

    g_expand_mat = gradient(stream_two, expand_rows, expand_weight)
    grad_two = grad_three + right_trans(expand_rows, expand_mat)
    g_shift_second = jnp.sum(grad_two, axis=0)
    g_gain_second = jnp.sum(grad_two * normed_two, axis=0)
    grad_second = layer_back(grad_two * gain_second, normed_two, inv_two)
    merge_rows = grad_second.astype(BF)
    g_merge_vec = jnp.sum(grad_second, axis=0)
    g_merge_mat = gradient(cross_outb, merge_rows, merge_weight)
    grad_cross = right_trans(merge_rows, merge_mat).astype(BF)
    probe_rows, enc_key_rows, enc_value_rows = attend_call(
        True, None, [probe, enc_keys, enc_values, grad_cross, cross_outb, cross_logs]
    )
    g_probe_vec = jnp.sum(probe_rows.astype(F32), axis=0)
    g_probe_mat = gradient(stream_one, probe_rows, probe_weight)
    g_lookup_mat = gradient(enc_all, enc_key_rows, lookup_weight)
    g_content_mat = gradient(enc_all, enc_value_rows, content_weight)
    g_content_vec = jnp.sum(enc_value_rows.astype(F32), axis=0)
    enc_part = right_trans(enc_key_rows, lookup_mat) + right_trans(enc_value_rows, content_mat)
    grad_one = grad_second + right_trans(probe_rows, probe_mat)
    g_shift_first = jnp.sum(grad_one, axis=0)
    g_gain_first = jnp.sum(grad_one * normed_one, axis=0)
    grad_first = layer_back(grad_one * gain_first, normed_one, inv_one)
    out_rows = grad_first.astype(BF)
    g_out_vec = jnp.sum(grad_first, axis=0)
    g_out_mat = gradient(self_outb, out_rows, out_weight)
    grad_self = right_trans(out_rows, out_mat).astype(BF)
    query_rows, key_rows, value_rows = attend_call(
        True, ids, [queries, all_keys, all_values, grad_self, self_outb, self_logs]
    )
    g_query_vec = jnp.sum(query_rows.astype(F32), axis=0)
    g_value_vec = jnp.sum(value_rows.astype(F32), axis=0)
    g_query_mat = gradient(flat, query_rows, query_weight)
    g_key_mat = gradient(tok_all, key_rows, key_weight)
    g_value_mat = gradient(tok_all, value_rows, value_weight)
    tok_part = right_trans(key_rows, key_mat) + right_trans(value_rows, value_mat)
    tok_own = grad_first + right_trans(query_rows, query_mat)
    tok_part = tok_part.astype(BF)
    enc_part = enc_part.astype(BF)

    wide_grads = jnp.stack(
        [
            g_query_vec, g_value_vec, g_out_vec, g_gain_first, g_shift_first, g_probe_vec, g_content_vec,
            g_merge_vec, g_gain_second, g_shift_second, g_reduce_vec, g_gain_third, g_shift_third,
        ]
    )
    lanes = 128
    vec_grads = jnp.pad(
        wide_grads.reshape(WIDE, n_dev, part).transpose(1, 0, 2), ((0, 0), (0, 0), (0, lanes - part))
    )
    long_row = jnp.pad(g_expand_vec.reshape(n_dev, 1, long_part), ((0, 0), (0, 0), (0, lanes - long_part)))
    vec_grads = jnp.concatenate([vec_grads, long_row, jnp.zeros((n_dev, 2, lanes), F32)], axis=1)
    vec_grads = vec_grads.reshape(cube.lead(True) + (WIDE + 3, lanes))
    mats = [
        g_expand_mat, g_merge_mat, g_probe_mat, g_lookup_mat, g_content_mat, g_out_mat,
        g_query_mat, g_key_mat, g_value_mat,
    ]
    shards = [
        expand_weight, merge_weight, probe_weight, lookup_weight, content_weight, out_weight,
        query_weight, key_weight, value_weight,
    ]
    tok_part, enc_part, tok_own, vec_grads, reduce_part = lax.optimization_barrier(
        (tok_part, enc_part, tok_own, vec_grads, reduce_part)
    )
    reduce_part = lax.psum_scatter(reduce_part, "seq", scatter_dimension=1, tiled=True)
    sums = scatter_all(
        cube,
        [
            enc_part.reshape(cube.n_seq, enc_local, feat_width),
            tok_part.reshape(cube.n_seq, local_rows, feat_width),
        ]
        + mats
        + [vec_grads],
        [False, False] + [True] * (len(mats) + 1),
        1,
    )
    done = hand_out(
        [sums[0]] + list(sums[2:11]),
        sums[11],
        (part,) * WIDE + (long_part,),
        sums[1],
        tok_own,
        reduce_part.reshape(reduce_weight.shape),
    )
    encoded_grad = done[0]
    (
        expand_sum, merge_sum, probe_sum, lookup_sum, content_sum, out_sum, query_sum, key_sum, value_sum,
    ) = [one.reshape(w.shape) for one, w in zip(done[1:10], shards)]
    (
        query_vs, value_vs, out_vs, gain1_vs, shift1_vs, probe_vs, content_vs,
        merge_vs, gain2_vs, shift2_vs, reduce_vs, gain3_vs, shift3_vs, expand_vs,
    ) = done[10:24]
    tokens_grad, reduce_sum = done[24:26]
    return (
        output[None],
        tokens_grad[None],
        encoded_grad[None],
        query_sum,
        key_sum,
        value_sum,
        out_sum,
        query_vs,
        value_vs,
        out_vs,
        gain1_vs,
        shift1_vs,
        probe_sum,
        lookup_sum,
        content_sum,
        merge_sum,
        probe_vs,
        content_vs,
        merge_vs,
        gain2_vs,
        shift2_vs,
        expand_sum,
        expand_vs,
        reduce_sum,
        reduce_vs,
        gain3_vs,
        shift3_vs,
    )


def solution(mesh):
    rows = P("dp", "seq", None)
    ids = P("dp", None)
    mat = P(("dp", "seq"), None)
    vec = P(("dp", "seq"))
    return jax.shard_map(
        functools.partial(local, Cube(mesh)),
        mesh=mesh,
        in_specs=(
            (rows, rows, rows, ids, ids)
            + (mat, mat, mat, mat, vec, vec, vec, vec, vec)
            + (mat, mat, mat, mat, vec, vec, vec, vec, vec)
            + (mat, vec, mat, vec, vec, vec)
        ),
        out_specs=(
            (rows, rows, rows)
            + (mat, mat, mat, mat, vec, vec, vec, vec, vec)
            + (mat, mat, mat, mat, vec, vec, vec, vec, vec)
            + (mat, vec, mat, vec, vec, vec)
        ),
        check_vma=False,
    )
```
